128 devices in a mesh: req: 4 (over x), seq: 32 (over z, y, core).
Axes of the slice: x: 4, y: 4, z: 4, core: 2. Of those that a mesh axis runs over, the one named last changes fastest.
Arguments:
- new_tokens: bfloat16 [32, 4, 2048], P('req'), may hold values from -6 to 6
- norm_gain: float32 [2048], replicated, may hold values from 0.5 to 1.5
- w_query: bfloat16 [2048, 2048], P(None, 'req'), may hold values from -0.25 to 0.25
- w_key: bfloat16 [2048, 1024], P(None, 'req'), may hold values from -0.125 to 0.125
- w_value: bfloat16 [2048, 1024], P(None, 'req'), may hold values from -0.125 to 0.125
- w_out: bfloat16 [2048, 2048], P('req'), may hold values from -0.125 to 0.125
- pool_keys: bfloat16 [16384, 16, 1024], P(('req', 'seq')), may hold values from -1000 to 1000
- pool_values: bfloat16 [16384, 16, 1024], P(('req', 'seq')), may hold values from -6 to 6
- cache_lengths: int32 [32], replicated, may hold values from 2 to 8188, as said below
- owner: int32 [32], replicated, may hold values from 0 to 31, as said below
- page_table: int32 [32, 512], replicated, may hold values from 0 to 16383, as said below
Outputs:
- out_hidden: bfloat16 [32, 4, 2048], P('req')
- keys_out: bfloat16 [32, 8192, 1024], P('req', 'seq')
- values_out: bfloat16 [32, 8192, 1024], P('req', 'seq')
The draws below stay inside these ranges and needn't reach their ends.
Inputs may be any that keep to these rules, and one draw needn't show every extreme that they name: A permutation: request r goes to owner slot owner[r], held by request group owner[r] // 8. page_table[r, j] is the pool page holding positions j * 16 to (j + 1) * 16 - 1 of request r; every pool page is named exactly once. Pool pages d * 128 to (d + 1) * 128 - 1 lie on device d of req+seq. The home of page j of request r is the device with req index owner[r] // 8 and seq index j // 16; every device's pool pages include exactly 1 pages of every home. `cache_lengths`: 8188 is reached in every draw.
All inputs are finite; a program needn't handle non-finite values.
Results may differ from the reference program's by a relative error of at most 0.015.
Values may be sent and summed in bfloat16 or wider, within the bound.
No kernel may reach another device: no remote copies, remote signals or barrier semaphores. Data moves between devices by JAX's collectives and lax.ppermute only.
A program may use at most 128 MiB of HBM per device.

```python
import math
import jax
import jax.numpy as jnp
from jax import lax

D = 2048
H = 16
KVH = 8
HD = 128
NEW = 4
PAGE = 16
R_DEV = 8
REQS = 32
L_MAX = 8192
PPD = 16
PPR = 512
PAGES_DEV = 128
PER_PEER = 1
POOL = 16384
QW = 2048
KVW = 1024


def route_tables(key):
    devices = POOL // PAGES_DEV
    seq_count = PPR // PPD
    first_key = jax.random.fold_in(key, 101)
    spread_key = jax.random.fold_in(key, 102)
    shuffle_key = jax.random.fold_in(key, 103)
    owners = jax.random.permutation(first_key, REQS).astype(jnp.int32)
    spread = jax.vmap(lambda single: jax.random.permutation(single, PAGES_DEV))(jax.random.split(spread_key, devices)).astype(jnp.int32)
    shuffle = jax.vmap(lambda single: jax.random.permutation(single, PAGES_DEV))(jax.random.split(shuffle_key, devices)).astype(jnp.int32)
    home_dev = jnp.arange(devices, dtype=jnp.int32)[:, None]
    source = (home_dev + spread) % devices
    position = home_dev * PER_PEER + spread // devices
    local_slot = shuffle[source, position]
    slot_table = source * PAGES_DEV + local_slot
    owner_col = owners[:, None]
    logical = jnp.arange(PPR, dtype=jnp.int32)[None, :]
    home_row = owner_col // R_DEV * seq_count + logical // PPD
    home_col = owner_col % R_DEV * PPD + logical % PPD
    return (owners, slot_table[home_row, home_col].astype(jnp.int32))


def draw_owner(key, part):
    return route_tables(key)[0]


def draw_page_table(key, part):
    return route_tables(key)[1]


def draw_cache_lengths(key, part):
    longest = L_MAX - NEW
    drawn_lengths = jax.random.randint(jax.random.fold_in(key, 201), (REQS,), 2, longest + 1)
    chosen = jax.random.randint(jax.random.fold_in(key, 202), (), 0, REQS)
    return jnp.where(jnp.arange(REQS) == chosen, longest, drawn_lengths).astype(jnp.int32)


def draw_pool_keys(key, part):
    shape_all = (POOL, PAGE, KVW)
    values = 1.5 * jnp.clip(jax.random.normal(jax.random.fold_in(key, 304), shape_all, jnp.float32), -6.0, 6.0)
    return values.astype(jnp.bfloat16)


def shard_levels(own_key, dims, shards, smallest, largest):
    factor_of = 1.0
    for dim, parts in shards:
        draws = jax.random.uniform(jax.random.fold_in(jax.random.fold_in(own_key, 6), dim), (parts,), jnp.float32, smallest / len(shards), largest / len(shards))
        factor_of = factor_of * jnp.repeat(jnp.exp(draws), dims[dim] // parts).reshape((-1,) + (1,) * (len(dims) - 1 - dim))
    return factor_of


def centred(stream_key, shape, scale, most, shards=(), held_as=jnp.bfloat16):
    entries = jax.random.normal(stream_key, shape, jnp.float32) * scale
    if len(shards) > 0:
        entries = shard_levels(stream_key, shape, shards, -0.22, 0.18) * entries
    return jnp.clip(entries, min=-most, max=most).astype(held_as)


def setup_inputs(seed: int = 0) -> dict:
    keys = jax.random.split(jax.random.key(seed), 12)
    return {
        "new_tokens": centred(keys[0], (REQS, NEW, D), 1.0, 6.0, ((0, 4),)),
        "norm_gain": jnp.clip(1.0 + 0.1 * jax.random.normal(keys[1], (D,), jnp.float32), 0.5, 1.5),
        "w_query": centred(keys[2], (D, QW), (D // 4) ** -0.5, 0.25, ((1, 4),)),
        "w_key": centred(keys[3], (D, KVW), D ** -0.5, 0.125, ((1, 4),)),
        "w_value": centred(keys[4], (D, KVW), D ** -0.5, 0.125, ((1, 4),)),
        "w_out": centred(keys[5], (QW, D), QW ** -0.5, 0.125, ((0, 4),)),
        "pool_keys": draw_pool_keys(jax.random.fold_in(keys[11], 71), 0),
        "pool_values": centred(keys[7], (POOL, PAGE, KVW), 1.0, 6.0, ((0, 128),)),
        "cache_lengths": draw_cache_lengths(jax.random.fold_in(keys[11], 71), 0),
        "owner": draw_owner(jax.random.fold_in(keys[11], 71), 0),
        "page_table": draw_page_table(jax.random.fold_in(keys[11], 71), 0),
    }


NORM_EPS = 1e-05
ROPE_BASE = 1000000.0
MASKED = -1e+30

def rotate(values, places):
    half_dim = values.shape[-1] // 2
    steps_up = jnp.arange(half_dim, dtype=jnp.float32) * (2.0 / values.shape[-1])
    inverse = ROPE_BASE ** (-steps_up)
    angles = places.astype(jnp.float32)[..., None] * inverse
    cosine = jnp.cos(angles)[..., None, :]
    sine_part = jnp.sin(angles)[..., None, :]
    first_half = values[..., :half_dim]
    second_half = values[..., half_dim:]
    return jnp.concatenate([first_half * cosine - second_half * sine_part, second_half * cosine + first_half * sine_part], axis=-1)

def reference(new_tokens, norm_gain, w_query, w_key, w_value, w_out, pool_keys, pool_values, cache_lengths, owner, page_table):
    groups = H // KVH
    slot_request = jnp.zeros((REQS,), jnp.int32).at[owner].set(jnp.arange(REQS, dtype=jnp.int32))
    slot_lengths = cache_lengths[slot_request]
    slot_pages = page_table[slot_request]
    tokens_wide = new_tokens.astype(jnp.float32)
    square_mean = lax.optimization_barrier(jnp.mean(tokens_wide * tokens_wide, axis=-1, keepdims=True))
    normed = (tokens_wide * lax.rsqrt(square_mean + NORM_EPS) * norm_gain.astype(jnp.float32)).astype(jnp.bfloat16)
    flat_rows = normed.reshape(REQS * NEW, D)
    places = slot_lengths[:, None] + jnp.arange(NEW, dtype=jnp.int32)[None, :]
    queries = jnp.dot(flat_rows, w_query, preferred_element_type=jnp.float32).reshape(REQS, NEW, H, HD)
    fresh_keys = jnp.dot(flat_rows, w_key, preferred_element_type=jnp.float32).reshape(REQS, NEW, KVH, HD)
    fresh_values = jnp.dot(flat_rows, w_value, preferred_element_type=jnp.float32).reshape(REQS, NEW, KVH, HD)
    queries = rotate(queries, places).astype(jnp.bfloat16)
    fresh_keys = rotate(fresh_keys, places).astype(jnp.bfloat16)
    fresh_values = fresh_values.astype(jnp.bfloat16)
    score_scale = 1.0 / math.sqrt(HD)
    key_pos = jnp.arange(L_MAX + NEW, dtype=jnp.int32)
    new_index = jnp.arange(NEW, dtype=jnp.int32)

    def attend(packed):
        page_rows, length, query_one, keys_one, values_one = packed
        cached_keys = pool_keys[page_rows].reshape(L_MAX, KVW)
        cached_values = pool_values[page_rows].reshape(L_MAX, KVW)
        all_keys = jnp.concatenate([cached_keys, keys_one.reshape(NEW, KVW)], axis=0).reshape(L_MAX + NEW, KVH, HD).astype(jnp.float32)
        all_values = jnp.concatenate([cached_values, values_one.reshape(NEW, KVW)], axis=0).reshape(L_MAX + NEW, KVH, HD).astype(jnp.float32)
        grouped = query_one.reshape(NEW, KVH, groups, HD).astype(jnp.float32)
        scores = jnp.einsum('tkgd,pkd->kgtp', grouped, all_keys) * score_scale
        visible = jnp.where(key_pos[None, :] < L_MAX, key_pos[None, :] < length, key_pos[None, :] - L_MAX <= new_index[:, None])
        scores = jnp.where(visible, scores, MASKED)
        row_peak = lax.optimization_barrier(jnp.max(scores, axis=-1, keepdims=True))
        weights = jnp.where(visible, jnp.exp(scores - row_peak), 0.0)
        denominator = lax.optimization_barrier(jnp.sum(weights, axis=-1))
        rounded = lax.optimization_barrier(weights.astype(jnp.bfloat16)).astype(jnp.float32)
        weighted = jnp.einsum('kgtp,pkd->tkgd', rounded, all_values)
        attended = (weighted / jnp.transpose(denominator, (2, 0, 1))[..., None]).reshape(NEW, QW).astype(jnp.bfloat16)
        keys_done = lax.dynamic_update_slice(cached_keys, keys_one.reshape(NEW, KVW), (length, jnp.int32(0)))
        values_done = lax.dynamic_update_slice(cached_values, values_one.reshape(NEW, KVW), (length, jnp.int32(0)))
        return (attended, keys_done, values_done)
    attention, keys_out, values_out = lax.map(attend, (slot_pages, slot_lengths, queries, fresh_keys, fresh_values))
    mixed_out = jnp.dot(attention.reshape(REQS * NEW, QW), w_out, preferred_element_type=jnp.float32).reshape(REQS, NEW, D)
    out_hidden = (tokens_wide + mixed_out).astype(jnp.bfloat16)
    return (out_hidden, keys_out, values_out)
```

```python
import math

import jax
import jax.numpy as jnp
from jax import lax
from jax.sharding import PartitionSpec as P

H = 16
KVH = 8
HD = 128


NORM_EPS = 1e-05
ROPE_BASE = 1000000.0
MASKED = -1e30


def rotate(values, places):
    half_dim = values.shape[-1] // 2
    steps_up = jnp.arange(half_dim, dtype=jnp.float32) * (2.0 / values.shape[-1])
    inverse = ROPE_BASE ** (-steps_up)
    angles = places.astype(jnp.float32)[..., None] * inverse
    cosine = jnp.cos(angles)[..., None, :]
    sine_part = jnp.sin(angles)[..., None, :]
    first_half = values[..., :half_dim]
    second_half = values[..., half_dim:]
    return jnp.concatenate(
        [
            first_half * cosine - second_half * sine_part,
            second_half * cosine + first_half * sine_part,
        ],
        axis=-1,
    )


def shards(
    new_tokens,
    norm_gain,
    w_query,
    w_key,
    w_value,
    w_out,
    pool_keys,
    pool_values,
    cache_lengths,
    owner,
    page_table,
):
    req_count = lax.axis_size("req")
    seq_count = lax.axis_size("seq")
    devices = req_count * seq_count
    req_index = lax.axis_index("req")
    seq_index = lax.axis_index("seq")
    device_index = req_index * seq_count + seq_index
    local_reqs, new_count, model_width = new_tokens.shape
    request_total = owner.shape[0]
    pages_dev, page_len, kv_width = pool_keys.shape
    pages_req = page_table.shape[1]
    pages_home = pages_req // seq_count
    positions = pages_home * page_len
    per_peer = pages_dev // devices
    groups = H // KVH
    query_cols = w_query.shape[1]
    key_cols = w_key.shape[1]
    all_requests = jnp.arange(request_total, dtype=jnp.int32)
    hits = owner[None, :] == all_requests[:, None]
    slot_request = jnp.sum(jnp.where(hits, all_requests[None, :], 0), axis=1)
    slot_lengths = jnp.sum(jnp.where(hits, cache_lengths[None, :], 0), axis=1)
    my_lengths = lax.dynamic_slice_in_dim(slot_lengths, req_index * local_reqs, local_reqs)
    slot_pages = page_table[slot_request]
    home_table = jnp.transpose(
        slot_pages.reshape(req_count, local_reqs, seq_count, pages_home), (0, 2, 1, 3)
    ).reshape(devices, local_reqs * pages_home)
    my_home = lax.dynamic_slice_in_dim(home_table, device_index, 1, axis=0).reshape(-1)
    arrival_src = my_home // pages_dev
    held_here = (home_table // pages_dev) == device_index
    send_pick = jnp.sum(jnp.where(held_here, home_table % pages_dev, 0), axis=1)
    outgoing_k = pool_keys[send_pick].reshape(devices, per_peer, page_len, kv_width)
    outgoing_v = pool_values[send_pick].reshape(devices, per_peer, page_len, kv_width)
    incoming_k = lax.all_to_all(outgoing_k, ("req", "seq"), split_axis=0, concat_axis=0, tiled=True)
    incoming_v = lax.all_to_all(outgoing_v, ("req", "seq"), split_axis=0, concat_axis=0, tiled=True)
    cache_keys = incoming_k.reshape(pages_dev, page_len, kv_width)[arrival_src].reshape(
        local_reqs, positions, kv_width
    )
    cache_values = incoming_v.reshape(pages_dev, page_len, kv_width)[arrival_src].reshape(
        local_reqs, positions, kv_width
    )
    tokens_wide = new_tokens.astype(jnp.float32)
    square_mean = jnp.mean(tokens_wide * tokens_wide, axis=-1, keepdims=True)
    normed = (tokens_wide * lax.rsqrt(square_mean + NORM_EPS) * norm_gain).astype(jnp.bfloat16)
    new_index = jnp.arange(new_count, dtype=jnp.int32)
    row_block = lax.all_gather(normed, "req", axis=0, tiled=True)
    row_count = row_block.shape[0]
    flat_rows = row_block.reshape(row_count * new_count, model_width)
    places = slot_lengths[:, None] + new_index[None, :]
    queries_now = jnp.dot(flat_rows, w_query, preferred_element_type=jnp.float32).reshape(
        row_count, new_count, query_cols // HD, HD
    )
    keys_now = jnp.dot(flat_rows, w_key, preferred_element_type=jnp.float32).reshape(
        row_count, new_count, key_cols // HD, HD
    )
    values_now = jnp.dot(flat_rows, w_value, preferred_element_type=jnp.float32).reshape(
        row_count, new_count, key_cols
    )
    queries_now = rotate(queries_now, places).reshape(row_count, new_count, query_cols)
    keys_now = rotate(keys_now, places).reshape(row_count, new_count, key_cols)
    projected = jnp.concatenate([queries_now, keys_now, values_now], axis=-1).astype(jnp.bfloat16)
    owned_rows = lax.all_to_all(projected, "req", split_axis=0, concat_axis=2, tiled=True)
    owned_rows = owned_rows.reshape(local_reqs, new_count, req_count, query_cols + 2 * key_cols)
    queries = owned_rows[..., :query_cols].reshape(local_reqs, new_count, KVH, groups, HD)
    fresh_keys = owned_rows[..., query_cols : query_cols + key_cols].reshape(
        local_reqs, new_count, KVH, HD
    )
    fresh_values = owned_rows[..., query_cols + key_cols :].reshape(local_reqs, new_count, KVH, HD)
    score_scale = 1.0 / math.sqrt(HD)
    grid_keys = cache_keys.reshape(local_reqs, positions, KVH, HD)
    grid_values = cache_values.reshape(local_reqs, positions, KVH, HD)
    scores = (
        jnp.einsum("rtkgd,rpkd->rkgtp", queries, grid_keys, preferred_element_type=jnp.float32)
        * score_scale
    )
    key_spots = seq_index * positions + jnp.arange(positions, dtype=jnp.int32)
    live_mask = (key_spots[None, :] < my_lengths[:, None])[:, None, None, None, :]
    scores = jnp.where(live_mask, scores, MASKED)
    row_peak = jnp.max(scores, axis=-1)
    weights = jnp.where(live_mask, jnp.exp(scores - row_peak[..., None]), 0.0)
    row_mass = jnp.sum(weights, axis=-1)
    gathered_sum = jnp.einsum(
        "rkgtp,rpkd->rkgtd",
        weights.astype(jnp.bfloat16),
        grid_values,
        preferred_element_type=jnp.float32,
    )
    step = 1
    while step < seq_count:
        pairs = [(i, i ^ step) for i in range(seq_count)]
        peer_peak, peer_mass, peer_sum = lax.ppermute((row_peak, row_mass, gathered_sum), "seq", pairs)
        upper = (seq_index & step) != 0
        peak_lo = jnp.where(upper, peer_peak, row_peak)
        peak_hi = jnp.where(upper, row_peak, peer_peak)
        mass_lo = jnp.where(upper, peer_mass, row_mass)
        mass_hi = jnp.where(upper, row_mass, peer_mass)
        sum_lo = jnp.where(upper, peer_sum, gathered_sum)
        sum_hi = jnp.where(upper, gathered_sum, peer_sum)
        merged_peak = jnp.maximum(peak_lo, peak_hi)
        scale_lo = jnp.exp(peak_lo - merged_peak)
        scale_hi = jnp.exp(peak_hi - merged_peak)
        row_mass = mass_lo * scale_lo + mass_hi * scale_hi
        gathered_sum = sum_lo * scale_lo[..., None] + sum_hi * scale_hi[..., None]
        row_peak = merged_peak
        step *= 2
    own_scores = (
        jnp.einsum("rtkgd,rskd->rkgts", queries, fresh_keys, preferred_element_type=jnp.float32)
        * score_scale
    )
    causal = new_index[None, :] <= new_index[:, None]
    own_scores = jnp.where(causal, own_scores, MASKED)
    final_peak = jnp.maximum(row_peak, jnp.max(own_scores, axis=-1))
    carried = jnp.exp(row_peak - final_peak)
    own_weights = jnp.where(causal, jnp.exp(own_scores - final_peak[..., None]), 0.0)
    row_mass = row_mass * carried + jnp.sum(own_weights, axis=-1)
    gathered_sum = gathered_sum * carried[..., None] + jnp.einsum(
        "rkgts,rskd->rkgtd",
        own_weights.astype(jnp.bfloat16),
        fresh_values,
        preferred_element_type=jnp.float32,
    )
    attended = (
        jnp.transpose(gathered_sum / row_mass[..., None], (0, 3, 1, 2, 4))
        .reshape(local_reqs, new_count, KVH * groups * HD)
        .astype(jnp.bfloat16)
    )
    headed = lax.all_to_all(attended, "req", split_axis=2, concat_axis=0, tiled=True)
    row_count = lax.axis_size("req") * local_reqs
    projected_out = lax.psum_scatter(
        jnp.dot(
            headed.reshape(row_count * new_count, -1), w_out, preferred_element_type=jnp.float32
        )
        .reshape(row_count, new_count, model_width)
        .astype(jnp.bfloat16),
        "req",
        scatter_dimension=0,
        tiled=True,
    ).astype(jnp.float32)
    out_hidden = (tokens_wide + projected_out).astype(jnp.bfloat16)
    new_hits = key_spots[None, :, None] == my_lengths[:, None, None] + new_index[None, None, :]
    filler = new_hits.astype(jnp.bfloat16)
    placed_keys = jnp.einsum(
        "rpt,rtc->rpc",
        filler,
        fresh_keys.reshape(local_reqs, new_count, kv_width),
        preferred_element_type=jnp.float32,
    ).astype(jnp.bfloat16)
    placed_values = jnp.einsum(
        "rpt,rtc->rpc",
        filler,
        fresh_values.reshape(local_reqs, new_count, kv_width),
        preferred_element_type=jnp.float32,
    ).astype(jnp.bfloat16)
    touched = jnp.any(new_hits, axis=-1)[..., None]
    keys_out = jnp.where(touched, placed_keys, cache_keys)
    values_out = jnp.where(touched, placed_values, cache_values)
    return (out_hidden, keys_out, values_out)


def solution(mesh):
    return jax.shard_map(
        shards,
        mesh=mesh,
        in_specs=(
            P("req", None, None),
            P(),
            P(None, "req"),
            P(None, "req"),
            P(None, "req"),
            P("req", None),
            P(("req", "seq"), None, None),
            P(("req", "seq"), None, None),
            P(),
            P(),
            P(),
        ),
        out_specs=(P("req", None, None), P("req", "seq", None), P("req", "seq", None)),
        check_vma=False,
    )
```

```python
import math

import jax
import jax.numpy as jnp
from jax import lax
from jax.sharding import PartitionSpec as P

H = 16
KVH = 8
HD = 128


NORM_EPS = 1e-05
ROPE_BASE = 1000000.0
MASKED = -1e30


def rotate(values, places):
    half_dim = values.shape[-1] // 2
    steps_up = jnp.arange(half_dim, dtype=jnp.float32) * (2.0 / values.shape[-1])
    inverse = ROPE_BASE ** (-steps_up)
    angles = places.astype(jnp.float32)[..., None] * inverse
    cosine = jnp.cos(angles)[..., None, :]
    sine_part = jnp.sin(angles)[..., None, :]
    first_half = values[..., :half_dim]
    second_half = values[..., half_dim:]
    return jnp.concatenate(
        [
            first_half * cosine - second_half * sine_part,
            second_half * cosine + first_half * sine_part,
        ],
        axis=-1,
    )


def shards(
    new_tokens,
    norm_gain,
    w_query,
    w_key,
    w_value,
    w_out,
    pool_keys,
    pool_values,
    cache_lengths,
    owner,
    page_table,
):
    req_count = lax.axis_size("req")
    seq_count = lax.axis_size("seq")
    devices = req_count * seq_count
    req_index = lax.axis_index("req")
    seq_index = lax.axis_index("seq")
    device_index = req_index * seq_count + seq_index
    local_reqs, new_count, model_width = new_tokens.shape
    request_total = owner.shape[0]
    pages_dev, page_len, kv_width = pool_keys.shape
    pages_req = page_table.shape[1]
    pages_home = pages_req // seq_count
    positions = pages_home * page_len
    per_peer = pages_dev // devices
    groups = H // KVH
    query_cols = w_query.shape[1]
    key_cols = w_key.shape[1]
    all_requests = jnp.arange(request_total, dtype=jnp.int32)
    hits = owner[None, :] == all_requests[:, None]
    slot_request = jnp.sum(jnp.where(hits, all_requests[None, :], 0), axis=1)
    slot_lengths = jnp.sum(jnp.where(hits, cache_lengths[None, :], 0), axis=1)
    my_lengths = lax.dynamic_slice_in_dim(slot_lengths, req_index * local_reqs, local_reqs)
    slot_pages = page_table[slot_request]
    home_table = jnp.transpose(
        slot_pages.reshape(req_count, local_reqs, seq_count, pages_home), (0, 2, 1, 3)
    ).reshape(devices, local_reqs * pages_home)
    my_home = lax.dynamic_slice_in_dim(home_table, device_index, 1, axis=0).reshape(-1)
    arrival_src = my_home // pages_dev
    held_here = (home_table // pages_dev) == device_index
    send_pick = jnp.sum(jnp.where(held_here, home_table % pages_dev, 0), axis=1)
    outgoing = jnp.stack([pool_keys[send_pick], pool_values[send_pick]], axis=1)
    outgoing = outgoing.reshape(devices, per_peer, 2, page_len, kv_width)
    incoming = lax.all_to_all(outgoing, ("req", "seq"), split_axis=0, concat_axis=0, tiled=True)
    arrived = incoming.reshape(pages_dev, 2, page_len, kv_width)[arrival_src]
    arrived = arrived.reshape(local_reqs, pages_home, 2, page_len, kv_width)
    cache_keys = arrived[:, :, 0].reshape(local_reqs, positions, kv_width)
    cache_values = arrived[:, :, 1].reshape(local_reqs, positions, kv_width)
    tokens_wide = new_tokens.astype(jnp.float32)
    square_mean = jnp.mean(tokens_wide * tokens_wide, axis=-1, keepdims=True)
    normed = (tokens_wide * lax.rsqrt(square_mean + NORM_EPS) * norm_gain).astype(jnp.bfloat16)
    new_index = jnp.arange(new_count, dtype=jnp.int32)
    def shift(value, places):
        if places % req_count == 0:
            return value
        pairs = [(i, (i + places) % req_count) for i in range(req_count)]
        return lax.ppermute(value, "req", pairs)

    row_block = jnp.concatenate([shift(normed, k) for k in range(req_count)], axis=0)
    row_count = row_block.shape[0]
    flat_rows = row_block.reshape(row_count * new_count, model_width)
    row_group = (req_index - jnp.arange(req_count, dtype=jnp.int32)) % req_count
    row_lengths = jnp.take(slot_lengths.reshape(req_count, local_reqs), row_group, axis=0).reshape(-1)
    places = row_lengths[:, None] + new_index[None, :]
    queries_now = jnp.dot(flat_rows, w_query, preferred_element_type=jnp.float32).reshape(
        row_count, new_count, query_cols // HD, HD
    )
    keys_now = jnp.dot(flat_rows, w_key, preferred_element_type=jnp.float32).reshape(
        row_count, new_count, key_cols // HD, HD
    )
    values_now = jnp.dot(flat_rows, w_value, preferred_element_type=jnp.float32).reshape(
        row_count, new_count, key_cols
    )
    queries_now = rotate(queries_now, places).reshape(row_count, new_count, query_cols)
    keys_now = rotate(keys_now, places).reshape(row_count, new_count, key_cols)
    projected = jnp.concatenate([queries_now, keys_now, values_now], axis=-1).astype(jnp.bfloat16)
    projected = projected.reshape(req_count, local_reqs, new_count, query_cols + 2 * key_cols)
    by_shift = jnp.stack([shift(projected[k], -k) for k in range(req_count)], axis=0)
    source_block = (jnp.arange(req_count, dtype=jnp.int32) - req_index) % req_count
    owned_rows = jnp.take(by_shift, source_block, axis=0)
    owned_rows = jnp.transpose(owned_rows, (1, 2, 0, 3))
    queries = owned_rows[..., :query_cols].reshape(local_reqs, new_count, KVH, groups, HD)
    fresh_keys = owned_rows[..., query_cols : query_cols + key_cols].reshape(
        local_reqs, new_count, KVH, HD
    )
    fresh_values = owned_rows[..., query_cols + key_cols :].reshape(local_reqs, new_count, KVH, HD)
    score_scale = 1.0 / math.sqrt(HD)
    grid_keys = cache_keys.reshape(local_reqs, positions, KVH, HD)
    grid_values = cache_values.reshape(local_reqs, positions, KVH, HD)
    scores = (
        jnp.einsum("rtkgd,rpkd->rkgtp", queries, grid_keys, preferred_element_type=jnp.float32)
        * score_scale
    )
    key_spots = seq_index * positions + jnp.arange(positions, dtype=jnp.int32)
    live_mask = (key_spots[None, :] < my_lengths[:, None])[:, None, None, None, :]
    scores = jnp.where(live_mask, scores, MASKED)
    row_peak = jnp.max(scores, axis=-1)
    weights = jnp.where(live_mask, jnp.exp(scores - row_peak[..., None]), 0.0)
    row_mass = jnp.sum(weights, axis=-1)
    gathered_sum = jnp.einsum(
        "rkgtp,rpkd->rkgtd",
        weights.astype(jnp.bfloat16),
        grid_values,
        preferred_element_type=jnp.float32,
    )
    stat_rows = row_peak.size // HD
    step = 1
    while step < seq_count:
        pairs = [(i, i ^ step) for i in range(seq_count)]
        packed = jnp.concatenate(
            [
                gathered_sum.reshape(-1, HD),
                row_peak.reshape(stat_rows, HD),
                row_mass.reshape(stat_rows, HD),
            ],
            axis=0,
        )
        other = lax.ppermute(packed, "seq", pairs)
        peer_sum = other[: gathered_sum.size // HD].reshape(gathered_sum.shape)
        peer_peak = other[gathered_sum.size // HD : -stat_rows].reshape(row_peak.shape)
        peer_mass = other[-stat_rows:].reshape(row_mass.shape)
        upper = (seq_index & step) != 0
        peak_lo = jnp.where(upper, peer_peak, row_peak)
        peak_hi = jnp.where(upper, row_peak, peer_peak)
        mass_lo = jnp.where(upper, peer_mass, row_mass)
        mass_hi = jnp.where(upper, row_mass, peer_mass)
        sum_lo = jnp.where(upper, peer_sum, gathered_sum)
        sum_hi = jnp.where(upper, gathered_sum, peer_sum)
        merged_peak = jnp.maximum(peak_lo, peak_hi)
        scale_lo = jnp.exp(peak_lo - merged_peak)
        scale_hi = jnp.exp(peak_hi - merged_peak)
        row_mass = mass_lo * scale_lo + mass_hi * scale_hi
        gathered_sum = sum_lo * scale_lo[..., None] + sum_hi * scale_hi[..., None]
        row_peak = merged_peak
        step *= 2
    own_scores = (
        jnp.einsum("rtkgd,rskd->rkgts", queries, fresh_keys, preferred_element_type=jnp.float32)
        * score_scale
    )
    causal = new_index[None, :] <= new_index[:, None]
    own_scores = jnp.where(causal, own_scores, MASKED)
    final_peak = jnp.maximum(row_peak, jnp.max(own_scores, axis=-1))
    carried = jnp.exp(row_peak - final_peak)
    own_weights = jnp.where(causal, jnp.exp(own_scores - final_peak[..., None]), 0.0)
    row_mass = row_mass * carried + jnp.sum(own_weights, axis=-1)
    gathered_sum = gathered_sum * carried[..., None] + jnp.einsum(
        "rkgts,rskd->rkgtd",
        own_weights.astype(jnp.bfloat16),
        fresh_values,
        preferred_element_type=jnp.float32,
    )
    attended = (
        jnp.transpose(gathered_sum / row_mass[..., None], (0, 3, 1, 2, 4))
        .reshape(local_reqs, new_count, KVH * groups * HD)
        .astype(jnp.bfloat16)
    )
    head_cols = attended.shape[-1] // req_count
    headed = jnp.concatenate(
        [
            shift(
                lax.dynamic_slice_in_dim(
                    attended, ((req_index + k) % req_count) * head_cols, head_cols, axis=2
                ),
                k,
            )
            for k in range(req_count)
        ],
        axis=0,
    )
    partial_out = (
        jnp.dot(headed.reshape(row_count * new_count, -1), w_out, preferred_element_type=jnp.float32)
        .reshape(req_count, local_reqs, new_count, model_width)
        .astype(jnp.bfloat16)
    )
    projected_out = shift(partial_out[0], 0).astype(jnp.float32)
    for k in range(1, req_count):
        projected_out = projected_out + shift(partial_out[k], -k).astype(jnp.float32)
    out_hidden = (tokens_wide + projected_out).astype(jnp.bfloat16)
    new_hits = key_spots[None, :, None] == my_lengths[:, None, None] + new_index[None, None, :]
    filler = new_hits.astype(jnp.bfloat16)
    placed_keys = jnp.einsum(
        "rpt,rtc->rpc",
        filler,
        fresh_keys.reshape(local_reqs, new_count, kv_width),
        preferred_element_type=jnp.float32,
    ).astype(jnp.bfloat16)
    placed_values = jnp.einsum(
        "rpt,rtc->rpc",
        filler,
        fresh_values.reshape(local_reqs, new_count, kv_width),
        preferred_element_type=jnp.float32,
    ).astype(jnp.bfloat16)
    touched = jnp.any(new_hits, axis=-1)[..., None]
    keys_out = jnp.where(touched, placed_keys, cache_keys)
    values_out = jnp.where(touched, placed_values, cache_values)
    return (out_hidden, keys_out, values_out)


def solution(mesh):
    return jax.shard_map(
        shards,
        mesh=mesh,
        in_specs=(
            P("req", None, None),
            P(),
            P(None, "req"),
            P(None, "req"),
            P(None, "req"),
            P("req", None),
            P(("req", "seq"), None, None),
            P(("req", "seq"), None, None),
            P(),
            P(),
            P(),
        ),
        out_specs=(P("req", None, None), P("req", "seq", None), P("req", "seq", None)),
        check_vma=False,
    )
```

```python
import math

import jax
import jax.numpy as jnp
from jax import lax
from jax.sharding import PartitionSpec as P

H = 16
KVH = 8
HD = 128


NORM_EPS = 1e-05
ROPE_BASE = 1000000.0
MASKED = -1e30


def rotate(values, places):
    half_dim = values.shape[-1] // 2
    steps_up = jnp.arange(half_dim, dtype=jnp.float32) * (2.0 / values.shape[-1])
    inverse = ROPE_BASE ** (-steps_up)
    angles = places.astype(jnp.float32)[..., None] * inverse
    cosine = jnp.cos(angles)[..., None, :]
    sine_part = jnp.sin(angles)[..., None, :]
    first_half = values[..., :half_dim]
    second_half = values[..., half_dim:]
    return jnp.concatenate(
        [
            first_half * cosine - second_half * sine_part,
            second_half * cosine + first_half * sine_part,
        ],
        axis=-1,
    )


def shards(
    new_tokens,
    norm_gain,
    w_query,
    w_key,
    w_value,
    w_out,
    pool_keys,
    pool_values,
    cache_lengths,
    owner,
    page_table,
):
    req_count = lax.axis_size("req")
    seq_count = lax.axis_size("seq")
    devices = req_count * seq_count
    req_index = lax.axis_index("req")
    seq_index = lax.axis_index("seq")
    device_index = req_index * seq_count + seq_index
    local_reqs, new_count, model_width = new_tokens.shape
    request_total = owner.shape[0]
    pages_dev, page_len, kv_width = pool_keys.shape
    pages_req = page_table.shape[1]
    pages_home = pages_req // seq_count
    positions = pages_home * page_len
    per_peer = pages_dev // devices
    groups = H // KVH
    query_cols = w_query.shape[1]
    key_cols = w_key.shape[1]
    all_requests = jnp.arange(request_total, dtype=jnp.int32)
    hits = owner[None, :] == all_requests[:, None]
    slot_request = jnp.sum(jnp.where(hits, all_requests[None, :], 0), axis=1)
    slot_lengths = jnp.sum(jnp.where(hits, cache_lengths[None, :], 0), axis=1)
    my_lengths = lax.dynamic_slice_in_dim(slot_lengths, req_index * local_reqs, local_reqs)
    slot_pages = page_table[slot_request]
    home_table = jnp.transpose(
        slot_pages.reshape(req_count, local_reqs, seq_count, pages_home), (0, 2, 1, 3)
    ).reshape(devices, local_reqs * pages_home)
    my_home = lax.dynamic_slice_in_dim(home_table, device_index, 1, axis=0).reshape(-1)
    arrival_src = my_home // pages_dev
    held_here = (home_table // pages_dev) == device_index
    send_pick = jnp.sum(jnp.where(held_here, home_table % pages_dev, 0), axis=1)
    tokens_wide = new_tokens.astype(jnp.float32)
    square_mean = jnp.mean(tokens_wide * tokens_wide, axis=-1, keepdims=True)
    normed = (tokens_wide * lax.rsqrt(square_mean + NORM_EPS) * norm_gain).astype(jnp.bfloat16)
    new_index = jnp.arange(new_count, dtype=jnp.int32)
    def shift(value, places):
        if places % req_count == 0:
            return value
        pairs = [(i, (i + places) % req_count) for i in range(req_count)]
        return lax.ppermute(value, "req", pairs)

    row_block = jnp.concatenate([shift(normed, k) for k in range(req_count)], axis=0)
    row_count = row_block.shape[0]
    flat_rows = row_block.reshape(row_count * new_count, model_width)
    row_group = (req_index - jnp.arange(req_count, dtype=jnp.int32)) % req_count
    row_lengths = jnp.take(slot_lengths.reshape(req_count, local_reqs), row_group, axis=0).reshape(-1)
    places = row_lengths[:, None] + new_index[None, :]
    queries_now = jnp.dot(flat_rows, w_query, preferred_element_type=jnp.float32).reshape(
        row_count, new_count, query_cols // HD, HD
    )
    keys_now = jnp.dot(flat_rows, w_key, preferred_element_type=jnp.float32).reshape(
        row_count, new_count, key_cols // HD, HD
    )
    values_now = jnp.dot(flat_rows, w_value, preferred_element_type=jnp.float32).reshape(
        row_count, new_count, key_cols
    )
    queries_now = rotate(queries_now, places).reshape(row_count, new_count, query_cols)
    keys_now = rotate(keys_now, places).reshape(row_count, new_count, key_cols)
    projected = jnp.concatenate([queries_now, keys_now, values_now], axis=-1).astype(jnp.bfloat16)
    projected = projected.reshape(req_count, local_reqs, new_count, query_cols + 2 * key_cols)
    by_shift = jnp.stack([shift(projected[k], -k) for k in range(req_count)], axis=0)
    outgoing = jnp.stack([pool_keys[send_pick], pool_values[send_pick]], axis=1)
    outgoing = outgoing.reshape(devices, per_peer, 2, page_len, kv_width)
    outgoing, by_shift = lax.optimization_barrier((outgoing, by_shift))
    incoming = lax.all_to_all(outgoing, ("req", "seq"), split_axis=0, concat_axis=0, tiled=True)
    arrived = incoming.reshape(pages_dev, 2, page_len, kv_width)[arrival_src]
    arrived = arrived.reshape(local_reqs, pages_home, 2, page_len, kv_width)
    cache_keys = arrived[:, :, 0].reshape(local_reqs, positions, kv_width)
    cache_values = arrived[:, :, 1].reshape(local_reqs, positions, kv_width)
    source_block = (jnp.arange(req_count, dtype=jnp.int32) - req_index) % req_count
    owned_rows = jnp.take(by_shift, source_block, axis=0)
    owned_rows = jnp.transpose(owned_rows, (1, 2, 0, 3))
    queries = owned_rows[..., :query_cols].reshape(local_reqs, new_count, KVH, groups, HD)
    fresh_keys = owned_rows[..., query_cols : query_cols + key_cols].reshape(
        local_reqs, new_count, KVH, HD
    )
    fresh_values = owned_rows[..., query_cols + key_cols :].reshape(local_reqs, new_count, KVH, HD)
    score_scale = 1.0 / math.sqrt(HD)
    grid_keys = cache_keys.reshape(local_reqs, positions, KVH, HD)
    grid_values = cache_values.reshape(local_reqs, positions, KVH, HD)
    scores = (
        jnp.einsum("rtkgd,rpkd->rkgtp", queries, grid_keys, preferred_element_type=jnp.float32)
        * score_scale
    )
    key_spots = seq_index * positions + jnp.arange(positions, dtype=jnp.int32)
    live_mask = (key_spots[None, :] < my_lengths[:, None])[:, None, None, None, :]
    scores = jnp.where(live_mask, scores, MASKED)
    row_peak = jnp.max(scores, axis=-1)
    weights = jnp.where(live_mask, jnp.exp(scores - row_peak[..., None]), 0.0)
    row_mass = jnp.sum(weights, axis=-1)
    gathered_sum = jnp.einsum(
        "rkgtp,rpkd->rkgtd",
        weights.astype(jnp.bfloat16),
        grid_values,
        preferred_element_type=jnp.float32,
    )
    stat_rows = row_peak.size // HD
    step = 1
    while step < seq_count:
        pairs = [(i, i ^ step) for i in range(seq_count)]
        packed = jnp.concatenate(
            [
                gathered_sum.reshape(-1, HD),
                row_peak.reshape(stat_rows, HD),
                row_mass.reshape(stat_rows, HD),
            ],
            axis=0,
        )
        other = lax.ppermute(packed, "seq", pairs)
        peer_sum = other[: gathered_sum.size // HD].reshape(gathered_sum.shape)
        peer_peak = other[gathered_sum.size // HD : -stat_rows].reshape(row_peak.shape)
        peer_mass = other[-stat_rows:].reshape(row_mass.shape)
        upper = (seq_index & step) != 0
        peak_lo = jnp.where(upper, peer_peak, row_peak)
        peak_hi = jnp.where(upper, row_peak, peer_peak)
        mass_lo = jnp.where(upper, peer_mass, row_mass)
        mass_hi = jnp.where(upper, row_mass, peer_mass)
        sum_lo = jnp.where(upper, peer_sum, gathered_sum)
        sum_hi = jnp.where(upper, gathered_sum, peer_sum)
        merged_peak = jnp.maximum(peak_lo, peak_hi)
        scale_lo = jnp.exp(peak_lo - merged_peak)
        scale_hi = jnp.exp(peak_hi - merged_peak)
        row_mass = mass_lo * scale_lo + mass_hi * scale_hi
        gathered_sum = sum_lo * scale_lo[..., None] + sum_hi * scale_hi[..., None]
        row_peak = merged_peak
        step *= 2
    own_scores = (
        jnp.einsum("rtkgd,rskd->rkgts", queries, fresh_keys, preferred_element_type=jnp.float32)
        * score_scale
    )
    causal = new_index[None, :] <= new_index[:, None]
    own_scores = jnp.where(causal, own_scores, MASKED)
    final_peak = jnp.maximum(row_peak, jnp.max(own_scores, axis=-1))
    carried = jnp.exp(row_peak - final_peak)
    own_weights = jnp.where(causal, jnp.exp(own_scores - final_peak[..., None]), 0.0)
    row_mass = row_mass * carried + jnp.sum(own_weights, axis=-1)
    gathered_sum = gathered_sum * carried[..., None] + jnp.einsum(
        "rkgts,rskd->rkgtd",
        own_weights.astype(jnp.bfloat16),
        fresh_values,
        preferred_element_type=jnp.float32,
    )
    attended = (
        jnp.transpose(gathered_sum / row_mass[..., None], (0, 3, 1, 2, 4))
        .reshape(local_reqs, new_count, KVH * groups * HD)
        .astype(jnp.bfloat16)
    )
    head_cols = attended.shape[-1] // req_count
    headed = jnp.concatenate(
        [
            shift(
                lax.dynamic_slice_in_dim(
                    attended, ((req_index + k) % req_count) * head_cols, head_cols, axis=2
                ),
                k,
            )
            for k in range(req_count)
        ],
        axis=0,
    )
    partial_out = (
        jnp.dot(headed.reshape(row_count * new_count, -1), w_out, preferred_element_type=jnp.float32)
        .reshape(req_count, local_reqs, new_count, model_width)
        .astype(jnp.bfloat16)
    )
    projected_out = shift(partial_out[0], 0).astype(jnp.float32)
    for k in range(1, req_count):
        projected_out = projected_out + shift(partial_out[k], -k).astype(jnp.float32)
    out_hidden = (tokens_wide + projected_out).astype(jnp.bfloat16)
    new_hits = key_spots[None, :, None] == my_lengths[:, None, None] + new_index[None, None, :]
    filler = new_hits.astype(jnp.bfloat16)
    placed_keys = jnp.einsum(
        "rpt,rtc->rpc",
        filler,
        fresh_keys.reshape(local_reqs, new_count, kv_width),
        preferred_element_type=jnp.float32,
    ).astype(jnp.bfloat16)
    placed_values = jnp.einsum(
        "rpt,rtc->rpc",
        filler,
        fresh_values.reshape(local_reqs, new_count, kv_width),
        preferred_element_type=jnp.float32,
    ).astype(jnp.bfloat16)
    touched = jnp.any(new_hits, axis=-1)[..., None]
    keys_out = jnp.where(touched, placed_keys, cache_keys)
    values_out = jnp.where(touched, placed_values, cache_values)
    return (out_hidden, keys_out, values_out)


def solution(mesh):
    return jax.shard_map(
        shards,
        mesh=mesh,
        in_specs=(
            P("req", None, None),
            P(),
            P(None, "req"),
            P(None, "req"),
            P(None, "req"),
            P("req", None),
            P(("req", "seq"), None, None),
            P(("req", "seq"), None, None),
            P(),
            P(),
            P(),
        ),
        out_specs=(P("req", None, None), P("req", "seq", None), P("req", "seq", None)),
        check_vma=False,
    )
```

```python
import functools
import math

import jax
import jax.numpy as jnp
from jax import lax
from jax.experimental import pallas as pl
from jax.experimental.pallas import tpu as pltpu
from jax.sharding import PartitionSpec as P

H = 16
KVH = 8
HD = 128


NORM_EPS = 1e-05
ROPE_BASE = 1000000.0
MASKED = -1e30


def rotate(values, places):
    half_dim = values.shape[-1] // 2
    steps_up = jnp.arange(half_dim, dtype=jnp.float32) * (2.0 / values.shape[-1])
    inverse = ROPE_BASE ** (-steps_up)
    angles = places.astype(jnp.float32)[..., None] * inverse
    cosine = jnp.cos(angles)[..., None, :]
    sine_part = jnp.sin(angles)[..., None, :]
    first_half = values[..., :half_dim]
    second_half = values[..., half_dim:]
    return jnp.concatenate(
        [
            first_half * cosine - second_half * sine_part,
            second_half * cosine + first_half * sine_part,
        ],
        axis=-1,
    )


def _arrive_kernel(
    arrival_ref, lengths_ref, base_ref, incoming_ref, q_ref, fk_ref, fv_ref,
    keys_out_ref, values_out_ref, acc_ref, peak_ref, mass_ref, in_sem, *, scale
):
    r = pl.program_id(0)
    positions = keys_out_ref.shape[1]
    page_len = incoming_ref.shape[2]
    pages = positions // page_len
    heads = q_ref.shape[1]
    head_dim = q_ref.shape[3]
    new_count = fk_ref.shape[1]
    copies = []
    for pp in range(pages):
        src = arrival_ref[r * pages + pp]
        rows = pl.ds(pp * page_len, page_len)
        for half, dst in ((0, keys_out_ref), (1, values_out_ref)):
            copy = pltpu.make_async_copy(
                incoming_ref.at[src, half], dst.at[0, rows], in_sem.at[half, pp]
            )
            copy.start()
            copies.append(copy)
    for copy in copies:
        copy.wait()
    length = lengths_ref[r]
    base = base_ref[0]
    spots = base + lax.broadcasted_iota(jnp.int32, (1, positions), 1)
    live = spots < length
    for kh in range(heads):
        cols = pl.ds(kh * head_dim, head_dim)
        keys_h = keys_out_ref[0, :, cols]
        query_h = q_ref[0, kh]
        scores = lax.dot_general(
            query_h, keys_h, (((1,), (1,)), ((), ())), preferred_element_type=jnp.float32
        ) * scale
        scores = jnp.where(live, scores, MASKED)
        peak = jnp.max(scores, axis=1, keepdims=True)
        weights = jnp.where(live, jnp.exp(scores - peak), 0.0)
        peak_ref[0, kh] = peak
        mass_ref[0, kh] = jnp.sum(weights, axis=1, keepdims=True)
        acc_ref[0, kh] = jnp.dot(
            weights.astype(jnp.bfloat16), values_out_ref[0, :, cols],
            preferred_element_type=jnp.float32,
        )
    first = length - base
    tile0 = (first // page_len) * page_len
    row_ids = lax.broadcasted_iota(jnp.int32, (page_len, 1), 0)
    fresh_k = fk_ref[0]
    fresh_v = fv_ref[0]
    for tile in (tile0, tile0 + page_len):
        @pl.when(jnp.logical_and(tile >= 0, tile < positions))
        def _():
            start = pl.multiple_of(tile, page_len)
            rows = pl.ds(start, page_len)
            block_k = keys_out_ref[0, rows, :]
            block_v = values_out_ref[0, rows, :]
            for t in range(new_count):
                hit = row_ids == first + t - tile
                block_k = jnp.where(hit, fresh_k[t : t + 1, :], block_k)
                block_v = jnp.where(hit, fresh_v[t : t + 1, :], block_v)
            keys_out_ref[0, rows, :] = block_k
            values_out_ref[0, rows, :] = block_v


def arrive_and_attend(arrival_src, lengths, base, incoming, queries, fresh_k, fresh_v, scale):
    local_reqs, new_count, kv_width = fresh_k.shape
    _, heads, rows, head_dim = queries.shape
    positions = arrival_src.shape[0] // local_reqs * incoming.shape[2]
    pages = positions // incoming.shape[2]
    grid_spec = pltpu.PrefetchScalarGridSpec(
        num_scalar_prefetch=3,
        grid=(local_reqs,),
        in_specs=[
            pl.BlockSpec(memory_space=pl.ANY),
            pl.BlockSpec((1, heads, rows, head_dim), lambda r, *_: (r, 0, 0, 0)),
            pl.BlockSpec((1, new_count, kv_width), lambda r, *_: (r, 0, 0)),
            pl.BlockSpec((1, new_count, kv_width), lambda r, *_: (r, 0, 0)),
        ],
        out_specs=[
            pl.BlockSpec((1, positions, kv_width), lambda r, *_: (r, 0, 0)),
            pl.BlockSpec((1, positions, kv_width), lambda r, *_: (r, 0, 0)),
            pl.BlockSpec((1, heads, rows, head_dim), lambda r, *_: (r, 0, 0, 0)),
            pl.BlockSpec((1, heads, rows, 1), lambda r, *_: (r, 0, 0, 0)),
            pl.BlockSpec((1, heads, rows, 1), lambda r, *_: (r, 0, 0, 0)),
        ],
        scratch_shapes=[pltpu.SemaphoreType.DMA((2, pages))],
    )
    cache_bytes = 2 * local_reqs * positions * kv_width * 2
    return pl.pallas_call(
        functools.partial(_arrive_kernel, scale=scale),
        out_shape=[
            jax.ShapeDtypeStruct((local_reqs, positions, kv_width), jnp.bfloat16),
            jax.ShapeDtypeStruct((local_reqs, positions, kv_width), jnp.bfloat16),
            jax.ShapeDtypeStruct((local_reqs, heads, rows, head_dim), jnp.float32),
            jax.ShapeDtypeStruct((local_reqs, heads, rows, 1), jnp.float32),
            jax.ShapeDtypeStruct((local_reqs, heads, rows, 1), jnp.float32),
        ],
        grid_spec=grid_spec,
        compiler_params=pltpu.CompilerParams(dimension_semantics=("arbitrary",)),
        cost_estimate=pl.CostEstimate(
            flops=4 * local_reqs * heads * rows * positions * head_dim,
            transcendentals=local_reqs * heads * rows * positions,
            bytes_accessed=2 * cache_bytes,
        ),
        name="arrive_and_attend",
    )(arrival_src, lengths, base, incoming, queries, fresh_k, fresh_v)


def shards(
    new_tokens,
    norm_gain,
    w_query,
    w_key,
    w_value,
    w_out,
    pool_keys,
    pool_values,
    cache_lengths,
    owner,
    page_table,
):
    req_count = lax.axis_size("req")
    seq_count = lax.axis_size("seq")
    devices = req_count * seq_count
    req_index = lax.axis_index("req")
    seq_index = lax.axis_index("seq")
    device_index = req_index * seq_count + seq_index
    local_reqs, new_count, model_width = new_tokens.shape
    request_total = owner.shape[0]
    pages_dev, page_len, kv_width = pool_keys.shape
    pages_req = page_table.shape[1]
    pages_home = pages_req // seq_count
    positions = pages_home * page_len
    per_peer = pages_dev // devices
    groups = H // KVH
    query_cols = w_query.shape[1]
    key_cols = w_key.shape[1]
    all_requests = jnp.arange(request_total, dtype=jnp.int32)
    hits = owner[None, :] == all_requests[:, None]
    slot_request = jnp.sum(jnp.where(hits, all_requests[None, :], 0), axis=1)
    slot_lengths = jnp.sum(jnp.where(hits, cache_lengths[None, :], 0), axis=1)
    my_lengths = lax.dynamic_slice_in_dim(slot_lengths, req_index * local_reqs, local_reqs)
    slot_pages = page_table[slot_request]
    home_table = jnp.transpose(
        slot_pages.reshape(req_count, local_reqs, seq_count, pages_home), (0, 2, 1, 3)
    ).reshape(devices, local_reqs * pages_home)
    my_home = lax.dynamic_slice_in_dim(home_table, device_index, 1, axis=0).reshape(-1)
    arrival_src = my_home // pages_dev
    held_here = (home_table // pages_dev) == device_index
    send_pick = jnp.sum(jnp.where(held_here, home_table % pages_dev, 0), axis=1)
    tokens_wide = new_tokens.astype(jnp.float32)
    square_mean = jnp.mean(tokens_wide * tokens_wide, axis=-1, keepdims=True)
    normed = (tokens_wide * lax.rsqrt(square_mean + NORM_EPS) * norm_gain).astype(jnp.bfloat16)
    new_index = jnp.arange(new_count, dtype=jnp.int32)
    def shift(value, places):
        if places % req_count == 0:
            return value
        pairs = [(i, (i + places) % req_count) for i in range(req_count)]
        return lax.ppermute(value, "req", pairs)

    row_block = jnp.concatenate([shift(normed, k) for k in range(req_count)], axis=0)
    row_count = row_block.shape[0]
    flat_rows = row_block.reshape(row_count * new_count, model_width)
    row_group = (req_index - jnp.arange(req_count, dtype=jnp.int32)) % req_count
    row_lengths = jnp.take(slot_lengths.reshape(req_count, local_reqs), row_group, axis=0).reshape(-1)
    places = row_lengths[:, None] + new_index[None, :]
    queries_now = jnp.dot(flat_rows, w_query, preferred_element_type=jnp.float32).reshape(
        row_count, new_count, query_cols // HD, HD
    )
    keys_now = jnp.dot(flat_rows, w_key, preferred_element_type=jnp.float32).reshape(
        row_count, new_count, key_cols // HD, HD
    )
    values_now = jnp.dot(flat_rows, w_value, preferred_element_type=jnp.float32).reshape(
        row_count, new_count, key_cols
    )
    queries_now = rotate(queries_now, places).reshape(row_count, new_count, query_cols)
    keys_now = rotate(keys_now, places).reshape(row_count, new_count, key_cols)
    projected = jnp.concatenate([queries_now, keys_now, values_now], axis=-1).astype(jnp.bfloat16)
    projected = projected.reshape(req_count, local_reqs, new_count, query_cols + 2 * key_cols)
    by_shift = jnp.stack([shift(projected[k], -k) for k in range(req_count)], axis=0)
    outgoing = jnp.stack([pool_keys[send_pick], pool_values[send_pick]], axis=1)
    outgoing = outgoing.reshape(devices, per_peer, 2, page_len, kv_width)
    outgoing, by_shift = lax.optimization_barrier((outgoing, by_shift))
    incoming = lax.all_to_all(outgoing, ("req", "seq"), split_axis=0, concat_axis=0, tiled=True)
    source_block = (jnp.arange(req_count, dtype=jnp.int32) - req_index) % req_count
    owned_rows = jnp.take(by_shift, source_block, axis=0)
    owned_rows = jnp.transpose(owned_rows, (1, 2, 0, 3))
    queries = owned_rows[..., :query_cols].reshape(local_reqs, new_count, KVH, groups, HD)
    fresh_keys = owned_rows[..., query_cols : query_cols + key_cols].reshape(
        local_reqs, new_count, KVH, HD
    )
    fresh_values = owned_rows[..., query_cols + key_cols :].reshape(local_reqs, new_count, KVH, HD)
    score_scale = 1.0 / math.sqrt(HD)
    kernel_queries = jnp.transpose(queries, (0, 2, 3, 1, 4)).reshape(
        local_reqs, KVH, groups * new_count, HD
    )
    keys_out, values_out, gathered_sum, row_peak, row_mass = arrive_and_attend(
        arrival_src,
        my_lengths,
        (seq_index * positions).reshape(1).astype(jnp.int32),
        incoming.reshape(pages_dev, 2, page_len, kv_width),
        kernel_queries,
        fresh_keys.reshape(local_reqs, new_count, kv_width),
        fresh_values.reshape(local_reqs, new_count, kv_width),
        score_scale,
    )
    gathered_sum = gathered_sum.reshape(local_reqs, KVH, groups, new_count, HD)
    row_peak = row_peak.reshape(local_reqs, KVH, groups, new_count)
    row_mass = row_mass.reshape(local_reqs, KVH, groups, new_count)
    stat_rows = row_peak.size // HD
    step = 1
    while step < seq_count:
        pairs = [(i, i ^ step) for i in range(seq_count)]
        packed = jnp.concatenate(
            [
                gathered_sum.reshape(-1, HD),
                row_peak.reshape(stat_rows, HD),
                row_mass.reshape(stat_rows, HD),
            ],
            axis=0,
        )
        other = lax.ppermute(packed, "seq", pairs)
        peer_sum = other[: gathered_sum.size // HD].reshape(gathered_sum.shape)
        peer_peak = other[gathered_sum.size // HD : -stat_rows].reshape(row_peak.shape)
        peer_mass = other[-stat_rows:].reshape(row_mass.shape)
        upper = (seq_index & step) != 0
        peak_lo = jnp.where(upper, peer_peak, row_peak)
        peak_hi = jnp.where(upper, row_peak, peer_peak)
        mass_lo = jnp.where(upper, peer_mass, row_mass)
        mass_hi = jnp.where(upper, row_mass, peer_mass)
        sum_lo = jnp.where(upper, peer_sum, gathered_sum)
        sum_hi = jnp.where(upper, gathered_sum, peer_sum)
        merged_peak = jnp.maximum(peak_lo, peak_hi)
        scale_lo = jnp.exp(peak_lo - merged_peak)
        scale_hi = jnp.exp(peak_hi - merged_peak)
        row_mass = mass_lo * scale_lo + mass_hi * scale_hi
        gathered_sum = sum_lo * scale_lo[..., None] + sum_hi * scale_hi[..., None]
        row_peak = merged_peak
        step *= 2
    own_scores = (
        jnp.einsum("rtkgd,rskd->rkgts", queries, fresh_keys, preferred_element_type=jnp.float32)
        * score_scale
    )
    causal = new_index[None, :] <= new_index[:, None]
    own_scores = jnp.where(causal, own_scores, MASKED)
    final_peak = jnp.maximum(row_peak, jnp.max(own_scores, axis=-1))
    carried = jnp.exp(row_peak - final_peak)
    own_weights = jnp.where(causal, jnp.exp(own_scores - final_peak[..., None]), 0.0)
    row_mass = row_mass * carried + jnp.sum(own_weights, axis=-1)
    gathered_sum = gathered_sum * carried[..., None] + jnp.einsum(
        "rkgts,rskd->rkgtd",
        own_weights.astype(jnp.bfloat16),
        fresh_values,
        preferred_element_type=jnp.float32,
    )
    attended = (
        jnp.transpose(gathered_sum / row_mass[..., None], (0, 3, 1, 2, 4))
        .reshape(local_reqs, new_count, KVH * groups * HD)
        .astype(jnp.bfloat16)
    )
    head_cols = attended.shape[-1] // req_count
    headed = jnp.concatenate(
        [
            shift(
                lax.dynamic_slice_in_dim(
                    attended, ((req_index + k) % req_count) * head_cols, head_cols, axis=2
                ),
                k,
            )
            for k in range(req_count)
        ],
        axis=0,
    )
    partial_out = (
        jnp.dot(headed.reshape(row_count * new_count, -1), w_out, preferred_element_type=jnp.float32)
        .reshape(req_count, local_reqs, new_count, model_width)
        .astype(jnp.bfloat16)
    )
    projected_out = shift(partial_out[0], 0).astype(jnp.float32)
    for k in range(1, req_count):
        projected_out = projected_out + shift(partial_out[k], -k).astype(jnp.float32)
    out_hidden = (tokens_wide + projected_out).astype(jnp.bfloat16)
    return (out_hidden, keys_out, values_out)


def solution(mesh):
    return jax.shard_map(
        shards,
        mesh=mesh,
        in_specs=(
            P("req", None, None),
            P(),
            P(None, "req"),
            P(None, "req"),
            P(None, "req"),
            P("req", None),
            P(("req", "seq"), None, None),
            P(("req", "seq"), None, None),
            P(),
            P(),
            P(),
        ),
        out_specs=(P("req", None, None), P("req", "seq", None), P("req", "seq", None)),
        check_vma=False,
    )
```

```python
import functools
import math

import jax
import jax.numpy as jnp
from jax import lax
from jax.experimental import pallas as pl
from jax.experimental.pallas import tpu as pltpu
from jax.sharding import PartitionSpec as P

H = 16
KVH = 8
HD = 128


NORM_EPS = 1e-05
ROPE_BASE = 1000000.0
MASKED = -1e30


def rotate(values, places):
    half_dim = values.shape[-1] // 2
    steps_up = jnp.arange(half_dim, dtype=jnp.float32) * (2.0 / values.shape[-1])
    inverse = ROPE_BASE ** (-steps_up)
    angles = places.astype(jnp.float32)[..., None] * inverse
    cosine = jnp.cos(angles)[..., None, :]
    sine_part = jnp.sin(angles)[..., None, :]
    first_half = values[..., :half_dim]
    second_half = values[..., half_dim:]
    return jnp.concatenate(
        [
            first_half * cosine - second_half * sine_part,
            second_half * cosine + first_half * sine_part,
        ],
        axis=-1,
    )


def _arrive_kernel(
    arrival_ref, lengths_ref, base_ref, incoming_ref, q_ref, fk_ref, fv_ref,
    keys_out_ref, values_out_ref, acc_ref, peak_ref, mass_ref,
    kbuf, vbuf, in_sem, out_sem, *, scale
):
    r = pl.program_id(0)
    n = pl.num_programs(0)
    slot = r % 2
    positions = kbuf.shape[1]
    page_len = incoming_ref.shape[2]
    pages = positions // page_len
    heads = q_ref.shape[1]
    head_dim = q_ref.shape[3]
    new_count = fk_ref.shape[1]
    bufs = (kbuf, vbuf)
    outs = (keys_out_ref, values_out_ref)

    def page_copy(req, s, half, pp, src):
        return pltpu.make_async_copy(
            incoming_ref.at[src, half],
            bufs[half].at[s, pl.ds(pp * page_len, page_len)],
            in_sem.at[half, s, pp],
        )

    def fetch(req, s):
        for pp in range(pages):
            src = arrival_ref[req * pages + pp]
            for half in range(2):
                page_copy(req, s, half, pp, src).start()

    def wait_fetch(s):
        for pp in range(pages):
            for half in range(2):
                page_copy(0, s, half, pp, 0).wait()

    def out_copy(req, s, half):
        return pltpu.make_async_copy(bufs[half].at[s], outs[half].at[req], out_sem.at[half, s])

    @pl.when(r == 0)
    def _():
        fetch(0, 0)

    wait_fetch(slot)

    @pl.when(r + 1 < n)
    def _():
        @pl.when(r >= 1)
        def _():
            for half in range(2):
                out_copy(r - 1, 1 - slot, half).wait()

        fetch(r + 1, 1 - slot)

    length = lengths_ref[r]
    base = base_ref[0]
    spots = base + lax.broadcasted_iota(jnp.int32, (1, positions), 1)
    live = spots < length
    for kh in range(heads):
        cols = pl.ds(kh * head_dim, head_dim)
        keys_h = kbuf[slot, :, cols]
        query_h = q_ref[0, kh]
        scores = lax.dot_general(
            query_h, keys_h, (((1,), (1,)), ((), ())), preferred_element_type=jnp.float32
        ) * scale
        scores = jnp.where(live, scores, MASKED)
        peak = jnp.max(scores, axis=1, keepdims=True)
        weights = jnp.where(live, jnp.exp(scores - peak), 0.0)
        peak_ref[0, kh] = peak
        mass_ref[0, kh] = jnp.sum(weights, axis=1, keepdims=True)
        acc_ref[0, kh] = jnp.dot(
            weights.astype(jnp.bfloat16), vbuf[slot, :, cols],
            preferred_element_type=jnp.float32,
        )
    first = length - base
    tile0 = (first // page_len) * page_len
    row_ids = lax.broadcasted_iota(jnp.int32, (page_len, 1), 0)
    fresh_k = fk_ref[0]
    fresh_v = fv_ref[0]
    for tile in (tile0, tile0 + page_len):
        @pl.when(jnp.logical_and(tile >= 0, tile < positions))
        def _():
            start = pl.multiple_of(tile, page_len)
            rows = pl.ds(start, page_len)
            block_k = kbuf[slot, rows, :]
            block_v = vbuf[slot, rows, :]
            for t in range(new_count):
                hit = row_ids == first + t - tile
                block_k = jnp.where(hit, fresh_k[t : t + 1, :], block_k)
                block_v = jnp.where(hit, fresh_v[t : t + 1, :], block_v)
            kbuf[slot, rows, :] = block_k
            vbuf[slot, rows, :] = block_v

    for half in range(2):
        out_copy(r, slot, half).start()

    @pl.when(r == n - 1)
    def _():
        @pl.when(r >= 1)
        def _():
            for half in range(2):
                out_copy(r - 1, 1 - slot, half).wait()

        for half in range(2):
            out_copy(r, slot, half).wait()


def arrive_and_attend(arrival_src, lengths, base, incoming, queries, fresh_k, fresh_v, scale):
    local_reqs, new_count, kv_width = fresh_k.shape
    _, heads, rows, head_dim = queries.shape
    positions = arrival_src.shape[0] // local_reqs * incoming.shape[2]
    pages = positions // incoming.shape[2]
    grid_spec = pltpu.PrefetchScalarGridSpec(
        num_scalar_prefetch=3,
        grid=(local_reqs,),
        in_specs=[
            pl.BlockSpec(memory_space=pl.ANY),
            pl.BlockSpec((1, heads, rows, head_dim), lambda r, *_: (r, 0, 0, 0)),
            pl.BlockSpec((1, new_count, kv_width), lambda r, *_: (r, 0, 0)),
            pl.BlockSpec((1, new_count, kv_width), lambda r, *_: (r, 0, 0)),
        ],
        out_specs=[
            pl.BlockSpec(memory_space=pl.ANY),
            pl.BlockSpec(memory_space=pl.ANY),
            pl.BlockSpec((1, heads, rows, head_dim), lambda r, *_: (r, 0, 0, 0)),
            pl.BlockSpec((1, heads, rows, 1), lambda r, *_: (r, 0, 0, 0)),
            pl.BlockSpec((1, heads, rows, 1), lambda r, *_: (r, 0, 0, 0)),
        ],
        scratch_shapes=[
            pltpu.VMEM((2, positions, kv_width), jnp.bfloat16),
            pltpu.VMEM((2, positions, kv_width), jnp.bfloat16),
            pltpu.SemaphoreType.DMA((2, 2, pages)),
            pltpu.SemaphoreType.DMA((2, 2)),
        ],
    )
    cache_bytes = 2 * local_reqs * positions * kv_width * 2
    return pl.pallas_call(
        functools.partial(_arrive_kernel, scale=scale),
        out_shape=[
            jax.ShapeDtypeStruct((local_reqs, positions, kv_width), jnp.bfloat16),
            jax.ShapeDtypeStruct((local_reqs, positions, kv_width), jnp.bfloat16),
            jax.ShapeDtypeStruct((local_reqs, heads, rows, head_dim), jnp.float32),
            jax.ShapeDtypeStruct((local_reqs, heads, rows, 1), jnp.float32),
            jax.ShapeDtypeStruct((local_reqs, heads, rows, 1), jnp.float32),
        ],
        grid_spec=grid_spec,
        compiler_params=pltpu.CompilerParams(dimension_semantics=("arbitrary",)),
        cost_estimate=pl.CostEstimate(
            flops=4 * local_reqs * heads * rows * positions * head_dim,
            transcendentals=local_reqs * heads * rows * positions,
            bytes_accessed=2 * cache_bytes,
        ),
        name="arrive_and_attend",
    )(arrival_src, lengths, base, incoming, queries, fresh_k, fresh_v)


def shards(
    new_tokens,
    norm_gain,
    w_query,
    w_key,
    w_value,
    w_out,
    pool_keys,
    pool_values,
    cache_lengths,
    owner,
    page_table,
):
    req_count = lax.axis_size("req")
    seq_count = lax.axis_size("seq")
    devices = req_count * seq_count
    req_index = lax.axis_index("req")
    seq_index = lax.axis_index("seq")
    device_index = req_index * seq_count + seq_index
    local_reqs, new_count, model_width = new_tokens.shape
    request_total = owner.shape[0]
    pages_dev, page_len, kv_width = pool_keys.shape
    pages_req = page_table.shape[1]
    pages_home = pages_req // seq_count
    positions = pages_home * page_len
    per_peer = pages_dev // devices
    groups = H // KVH
    query_cols = w_query.shape[1]
    key_cols = w_key.shape[1]
    all_requests = jnp.arange(request_total, dtype=jnp.int32)
    hits = owner[None, :] == all_requests[:, None]
    slot_request = jnp.sum(jnp.where(hits, all_requests[None, :], 0), axis=1)
    slot_lengths = jnp.sum(jnp.where(hits, cache_lengths[None, :], 0), axis=1)
    my_lengths = lax.dynamic_slice_in_dim(slot_lengths, req_index * local_reqs, local_reqs)
    slot_pages = page_table[slot_request]
    home_table = jnp.transpose(
        slot_pages.reshape(req_count, local_reqs, seq_count, pages_home), (0, 2, 1, 3)
    ).reshape(devices, local_reqs * pages_home)
    my_home = lax.dynamic_slice_in_dim(home_table, device_index, 1, axis=0).reshape(-1)
    arrival_src = my_home // pages_dev
    held_here = (home_table // pages_dev) == device_index
    send_pick = jnp.sum(jnp.where(held_here, home_table % pages_dev, 0), axis=1)
    tokens_wide = new_tokens.astype(jnp.float32)
    square_mean = jnp.mean(tokens_wide * tokens_wide, axis=-1, keepdims=True)
    normed = (tokens_wide * lax.rsqrt(square_mean + NORM_EPS) * norm_gain).astype(jnp.bfloat16)
    new_index = jnp.arange(new_count, dtype=jnp.int32)
    def shift(value, places):
        if places % req_count == 0:
            return value
        pairs = [(i, (i + places) % req_count) for i in range(req_count)]
        return lax.ppermute(value, "req", pairs)

    row_block = jnp.concatenate([shift(normed, k) for k in range(req_count)], axis=0)
    row_count = row_block.shape[0]
    flat_rows = row_block.reshape(row_count * new_count, model_width)
    row_group = (req_index - jnp.arange(req_count, dtype=jnp.int32)) % req_count
    row_lengths = jnp.take(slot_lengths.reshape(req_count, local_reqs), row_group, axis=0).reshape(-1)
    places = row_lengths[:, None] + new_index[None, :]
    queries_now = jnp.dot(flat_rows, w_query, preferred_element_type=jnp.float32).reshape(
        row_count, new_count, query_cols // HD, HD
    )
    keys_now = jnp.dot(flat_rows, w_key, preferred_element_type=jnp.float32).reshape(
        row_count, new_count, key_cols // HD, HD
    )
    values_now = jnp.dot(flat_rows, w_value, preferred_element_type=jnp.float32).reshape(
        row_count, new_count, key_cols
    )
    queries_now = rotate(queries_now, places).reshape(row_count, new_count, query_cols)
    keys_now = rotate(keys_now, places).reshape(row_count, new_count, key_cols)
    projected = jnp.concatenate([queries_now, keys_now, values_now], axis=-1).astype(jnp.bfloat16)
    projected = projected.reshape(req_count, local_reqs, new_count, query_cols + 2 * key_cols)
    by_shift = jnp.stack([shift(projected[k], -k) for k in range(req_count)], axis=0)
    outgoing = jnp.stack([pool_keys[send_pick], pool_values[send_pick]], axis=1)
    outgoing = outgoing.reshape(devices, per_peer, 2, page_len, kv_width)
    outgoing, by_shift = lax.optimization_barrier((outgoing, by_shift))
    incoming = lax.all_to_all(outgoing, ("req", "seq"), split_axis=0, concat_axis=0, tiled=True)
    source_block = (jnp.arange(req_count, dtype=jnp.int32) - req_index) % req_count
    owned_rows = jnp.take(by_shift, source_block, axis=0)
    owned_rows = jnp.transpose(owned_rows, (1, 2, 0, 3))
    queries = owned_rows[..., :query_cols].reshape(local_reqs, new_count, KVH, groups, HD)
    fresh_keys = owned_rows[..., query_cols : query_cols + key_cols].reshape(
        local_reqs, new_count, KVH, HD
    )
    fresh_values = owned_rows[..., query_cols + key_cols :].reshape(local_reqs, new_count, KVH, HD)
    score_scale = 1.0 / math.sqrt(HD)
    kernel_queries = jnp.transpose(queries, (0, 2, 3, 1, 4)).reshape(
        local_reqs, KVH, groups * new_count, HD
    )
    keys_out, values_out, gathered_sum, row_peak, row_mass = arrive_and_attend(
        arrival_src,
        my_lengths,
        (seq_index * positions).reshape(1).astype(jnp.int32),
        incoming.reshape(pages_dev, 2, page_len, kv_width),
        kernel_queries,
        fresh_keys.reshape(local_reqs, new_count, kv_width),
        fresh_values.reshape(local_reqs, new_count, kv_width),
        score_scale,
    )
    gathered_sum = gathered_sum.reshape(local_reqs, KVH, groups, new_count, HD)
    row_peak = row_peak.reshape(local_reqs, KVH, groups, new_count)
    row_mass = row_mass.reshape(local_reqs, KVH, groups, new_count)
    stat_rows = row_peak.size // HD
    step = 1
    while step < seq_count:
        pairs = [(i, i ^ step) for i in range(seq_count)]
        packed = jnp.concatenate(
            [
                gathered_sum.reshape(-1, HD),
                row_peak.reshape(stat_rows, HD),
                row_mass.reshape(stat_rows, HD),
            ],
            axis=0,
        )
        other = lax.ppermute(packed, "seq", pairs)
        peer_sum = other[: gathered_sum.size // HD].reshape(gathered_sum.shape)
        peer_peak = other[gathered_sum.size // HD : -stat_rows].reshape(row_peak.shape)
        peer_mass = other[-stat_rows:].reshape(row_mass.shape)
        upper = (seq_index & step) != 0
        peak_lo = jnp.where(upper, peer_peak, row_peak)
        peak_hi = jnp.where(upper, row_peak, peer_peak)
        mass_lo = jnp.where(upper, peer_mass, row_mass)
        mass_hi = jnp.where(upper, row_mass, peer_mass)
        sum_lo = jnp.where(upper, peer_sum, gathered_sum)
        sum_hi = jnp.where(upper, gathered_sum, peer_sum)
        merged_peak = jnp.maximum(peak_lo, peak_hi)
        scale_lo = jnp.exp(peak_lo - merged_peak)
        scale_hi = jnp.exp(peak_hi - merged_peak)
        row_mass = mass_lo * scale_lo + mass_hi * scale_hi
        gathered_sum = sum_lo * scale_lo[..., None] + sum_hi * scale_hi[..., None]
        row_peak = merged_peak
        step *= 2
    own_scores = (
        jnp.einsum("rtkgd,rskd->rkgts", queries, fresh_keys, preferred_element_type=jnp.float32)
        * score_scale
    )
    causal = new_index[None, :] <= new_index[:, None]
    own_scores = jnp.where(causal, own_scores, MASKED)
    final_peak = jnp.maximum(row_peak, jnp.max(own_scores, axis=-1))
    carried = jnp.exp(row_peak - final_peak)
    own_weights = jnp.where(causal, jnp.exp(own_scores - final_peak[..., None]), 0.0)
    row_mass = row_mass * carried + jnp.sum(own_weights, axis=-1)
    gathered_sum = gathered_sum * carried[..., None] + jnp.einsum(
        "rkgts,rskd->rkgtd",
        own_weights.astype(jnp.bfloat16),
        fresh_values,
        preferred_element_type=jnp.float32,
    )
    attended = (
        jnp.transpose(gathered_sum / row_mass[..., None], (0, 3, 1, 2, 4))
        .reshape(local_reqs, new_count, KVH * groups * HD)
        .astype(jnp.bfloat16)
    )
    head_cols = attended.shape[-1] // req_count
    headed = jnp.concatenate(
        [
            shift(
                lax.dynamic_slice_in_dim(
                    attended, ((req_index + k) % req_count) * head_cols, head_cols, axis=2
                ),
                k,
            )
            for k in range(req_count)
        ],
        axis=0,
    )
    partial_out = (
        jnp.dot(headed.reshape(row_count * new_count, -1), w_out, preferred_element_type=jnp.float32)
        .reshape(req_count, local_reqs, new_count, model_width)
        .astype(jnp.bfloat16)
    )
    projected_out = shift(partial_out[0], 0).astype(jnp.float32)
    for k in range(1, req_count):
        projected_out = projected_out + shift(partial_out[k], -k).astype(jnp.float32)
    out_hidden = (tokens_wide + projected_out).astype(jnp.bfloat16)
    return (out_hidden, keys_out, values_out)


def solution(mesh):
    return jax.shard_map(
        shards,
        mesh=mesh,
        in_specs=(
            P("req", None, None),
            P(),
            P(None, "req"),
            P(None, "req"),
            P(None, "req"),
            P("req", None),
            P(("req", "seq"), None, None),
            P(("req", "seq"), None, None),
            P(),
            P(),
            P(),
        ),
        out_specs=(P("req", None, None), P("req", "seq", None), P("req", "seq", None)),
        check_vma=False,
    )
```

```python
import functools
import math

import jax
import jax.numpy as jnp
from jax import lax
from jax.experimental import pallas as pl
from jax.experimental.pallas import tpu as pltpu
from jax.sharding import PartitionSpec as P

H = 16
KVH = 8
HD = 128


NORM_EPS = 1e-05
ROPE_BASE = 1000000.0
MASKED = -1e30


def rotate(values, places):
    half_dim = values.shape[-1] // 2
    steps_up = jnp.arange(half_dim, dtype=jnp.float32) * (2.0 / values.shape[-1])
    inverse = ROPE_BASE ** (-steps_up)
    angles = places.astype(jnp.float32)[..., None] * inverse
    cosine = jnp.cos(angles)[..., None, :]
    sine_part = jnp.sin(angles)[..., None, :]
    first_half = values[..., :half_dim]
    second_half = values[..., half_dim:]
    return jnp.concatenate(
        [
            first_half * cosine - second_half * sine_part,
            second_half * cosine + first_half * sine_part,
        ],
        axis=-1,
    )


def _arrive_kernel(
    arrival_ref, lengths_ref, base_ref, incoming_ref, q_ref, fk_ref, fv_ref,
    keys_out_ref, values_out_ref, acc_ref, peak_ref, mass_ref,
    kbuf, vbuf, in_sem, out_sem, *, scale
):
    r = pl.program_id(0)
    n = pl.num_programs(0)
    slot = r % 2
    positions = kbuf.shape[1]
    page_len = incoming_ref.shape[2]
    pages = positions // page_len
    heads = q_ref.shape[1]
    head_dim = q_ref.shape[3]
    new_count = fk_ref.shape[1]
    bufs = (kbuf, vbuf)
    outs = (keys_out_ref, values_out_ref)

    def page_copy(req, s, half, pp, src):
        return pltpu.make_async_copy(
            incoming_ref.at[src, half],
            bufs[half].at[s, pl.ds(pp * page_len, page_len)],
            in_sem.at[half, s, pp],
        )

    def fetch(req, s):
        for pp in range(pages):
            src = arrival_ref[req * pages + pp]
            for half in range(2):
                page_copy(req, s, half, pp, src).start()

    def wait_fetch(s):
        for pp in range(pages):
            for half in range(2):
                page_copy(0, s, half, pp, 0).wait()

    def out_copy(req, s, half):
        return pltpu.make_async_copy(bufs[half].at[s], outs[half].at[req], out_sem.at[half, s])

    @pl.when(r == 0)
    def _():
        fetch(0, 0)

    wait_fetch(slot)

    @pl.when(r + 1 < n)
    def _():
        @pl.when(r >= 1)
        def _():
            for half in range(2):
                out_copy(r - 1, 1 - slot, half).wait()

        fetch(r + 1, 1 - slot)

    length = lengths_ref[r]
    base = base_ref[0]
    spots = base + lax.broadcasted_iota(jnp.int32, (1, positions), 1)
    live = spots < length
    for kh in range(heads):
        cols = pl.ds(kh * head_dim, head_dim)
        keys_h = kbuf[slot, :, cols]
        query_h = q_ref[0, kh]
        scores = lax.dot_general(
            query_h, keys_h, (((1,), (1,)), ((), ())), preferred_element_type=jnp.float32
        ) * scale
        scores = jnp.where(live, scores, MASKED)
        peak = jnp.max(scores, axis=1, keepdims=True)
        weights = jnp.where(live, jnp.exp(scores - peak), 0.0)
        peak_ref[0, kh] = peak
        mass_ref[0, kh] = jnp.sum(weights, axis=1, keepdims=True)
        acc_ref[0, kh] = jnp.dot(
            weights.astype(jnp.bfloat16), vbuf[slot, :, cols],
            preferred_element_type=jnp.float32,
        )
    first = length - base
    tile0 = (first // page_len) * page_len
    row_ids = lax.broadcasted_iota(jnp.int32, (page_len, 1), 0)
    fresh_k = fk_ref[0]
    fresh_v = fv_ref[0]
    for tile in (tile0, tile0 + page_len):
        @pl.when(jnp.logical_and(tile >= 0, tile < positions))
        def _():
            start = pl.multiple_of(tile, page_len)
            rows = pl.ds(start, page_len)
            block_k = kbuf[slot, rows, :]
            block_v = vbuf[slot, rows, :]
            for t in range(new_count):
                hit = row_ids == first + t - tile
                block_k = jnp.where(hit, fresh_k[t : t + 1, :], block_k)
                block_v = jnp.where(hit, fresh_v[t : t + 1, :], block_v)
            kbuf[slot, rows, :] = block_k
            vbuf[slot, rows, :] = block_v

    for half in range(2):
        out_copy(r, slot, half).start()

    @pl.when(r == n - 1)
    def _():
        @pl.when(r >= 1)
        def _():
            for half in range(2):
                out_copy(r - 1, 1 - slot, half).wait()

        for half in range(2):
            out_copy(r, slot, half).wait()


def arrive_and_attend(arrival_src, lengths, base, incoming, queries, fresh_k, fresh_v, scale):
    local_reqs, new_count, kv_width = fresh_k.shape
    _, heads, rows, head_dim = queries.shape
    positions = arrival_src.shape[0] // local_reqs * incoming.shape[2]
    pages = positions // incoming.shape[2]
    grid_spec = pltpu.PrefetchScalarGridSpec(
        num_scalar_prefetch=3,
        grid=(local_reqs,),
        in_specs=[
            pl.BlockSpec(memory_space=pl.ANY),
            pl.BlockSpec((1, heads, rows, head_dim), lambda r, *_: (r, 0, 0, 0)),
            pl.BlockSpec((1, new_count, kv_width), lambda r, *_: (r, 0, 0)),
            pl.BlockSpec((1, new_count, kv_width), lambda r, *_: (r, 0, 0)),
        ],
        out_specs=[
            pl.BlockSpec(memory_space=pl.ANY),
            pl.BlockSpec(memory_space=pl.ANY),
            pl.BlockSpec((1, heads, rows, head_dim), lambda r, *_: (r, 0, 0, 0)),
            pl.BlockSpec((1, heads, rows, 1), lambda r, *_: (r, 0, 0, 0)),
            pl.BlockSpec((1, heads, rows, 1), lambda r, *_: (r, 0, 0, 0)),
        ],
        scratch_shapes=[
            pltpu.VMEM((2, positions, kv_width), jnp.bfloat16),
            pltpu.VMEM((2, positions, kv_width), jnp.bfloat16),
            pltpu.SemaphoreType.DMA((2, 2, pages)),
            pltpu.SemaphoreType.DMA((2, 2)),
        ],
    )
    cache_bytes = 2 * local_reqs * positions * kv_width * 2
    return pl.pallas_call(
        functools.partial(_arrive_kernel, scale=scale),
        out_shape=[
            jax.ShapeDtypeStruct((local_reqs, positions, kv_width), jnp.bfloat16),
            jax.ShapeDtypeStruct((local_reqs, positions, kv_width), jnp.bfloat16),
            jax.ShapeDtypeStruct((local_reqs, heads, rows, head_dim), jnp.float32),
            jax.ShapeDtypeStruct((local_reqs, heads, rows, 1), jnp.float32),
            jax.ShapeDtypeStruct((local_reqs, heads, rows, 1), jnp.float32),
        ],
        grid_spec=grid_spec,
        compiler_params=pltpu.CompilerParams(dimension_semantics=("arbitrary",)),
        cost_estimate=pl.CostEstimate(
            flops=4 * local_reqs * heads * rows * positions * head_dim,
            transcendentals=local_reqs * heads * rows * positions,
            bytes_accessed=2 * cache_bytes,
        ),
        name="arrive_and_attend",
    )(arrival_src, lengths, base, incoming, queries, fresh_k, fresh_v)


def shards(
    new_tokens,
    norm_gain,
    w_query,
    w_key,
    w_value,
    w_out,
    pool_keys,
    pool_values,
    cache_lengths,
    owner,
    page_table,
):
    req_count = lax.axis_size("req")
    seq_count = lax.axis_size("seq")
    devices = req_count * seq_count
    req_index = lax.axis_index("req")
    seq_index = lax.axis_index("seq")
    device_index = req_index * seq_count + seq_index
    local_reqs, new_count, model_width = new_tokens.shape
    request_total = owner.shape[0]
    pages_dev, page_len, kv_width = pool_keys.shape
    pages_req = page_table.shape[1]
    pages_home = pages_req // seq_count
    positions = pages_home * page_len
    per_peer = pages_dev // devices
    groups = H // KVH
    query_cols = w_query.shape[1]
    key_cols = w_key.shape[1]
    all_requests = jnp.arange(request_total, dtype=jnp.int32)
    hits = owner[None, :] == all_requests[:, None]
    slot_request = jnp.sum(jnp.where(hits, all_requests[None, :], 0), axis=1)
    slot_lengths = jnp.sum(jnp.where(hits, cache_lengths[None, :], 0), axis=1)
    my_lengths = lax.dynamic_slice_in_dim(slot_lengths, req_index * local_reqs, local_reqs)
    slot_pages = page_table[slot_request]
    home_table = jnp.transpose(
        slot_pages.reshape(req_count, local_reqs, seq_count, pages_home), (0, 2, 1, 3)
    ).reshape(devices, local_reqs * pages_home)
    my_home = lax.dynamic_slice_in_dim(home_table, device_index, 1, axis=0).reshape(-1)
    arrival_src = my_home // pages_dev
    held_here = (home_table // pages_dev) == device_index
    send_pick = jnp.sum(jnp.where(held_here, home_table % pages_dev, 0), axis=1)
    tokens_wide = new_tokens.astype(jnp.float32)
    square_mean = jnp.mean(tokens_wide * tokens_wide, axis=-1, keepdims=True)
    normed = (tokens_wide * lax.rsqrt(square_mean + NORM_EPS) * norm_gain).astype(jnp.bfloat16)
    new_index = jnp.arange(new_count, dtype=jnp.int32)
    def shift(value, places):
        if places % req_count == 0:
            return value
        pairs = [(i, (i + places) % req_count) for i in range(req_count)]
        return lax.ppermute(value, "req", pairs)

    row_block = jnp.concatenate([shift(normed, k) for k in range(req_count)], axis=0)
    outgoing = jnp.stack([pool_keys[send_pick], pool_values[send_pick]], axis=1)
    outgoing = outgoing.reshape(devices, per_peer, 2, page_len, kv_width)
    outgoing, row_block = lax.optimization_barrier((outgoing, row_block))
    incoming = lax.all_to_all(outgoing, ("req", "seq"), split_axis=0, concat_axis=0, tiled=True)
    row_count = row_block.shape[0]
    flat_rows = row_block.reshape(row_count * new_count, model_width)
    row_group = (req_index - jnp.arange(req_count, dtype=jnp.int32)) % req_count
    row_lengths = jnp.take(slot_lengths.reshape(req_count, local_reqs), row_group, axis=0).reshape(-1)
    places = row_lengths[:, None] + new_index[None, :]
    queries_now = jnp.dot(flat_rows, w_query, preferred_element_type=jnp.float32).reshape(
        row_count, new_count, query_cols // HD, HD
    )
    keys_now = jnp.dot(flat_rows, w_key, preferred_element_type=jnp.float32).reshape(
        row_count, new_count, key_cols // HD, HD
    )
    values_now = jnp.dot(flat_rows, w_value, preferred_element_type=jnp.float32).reshape(
        row_count, new_count, key_cols
    )
    queries_now = rotate(queries_now, places).reshape(row_count, new_count, query_cols)
    keys_now = rotate(keys_now, places).reshape(row_count, new_count, key_cols)
    projected = jnp.concatenate([queries_now, keys_now, values_now], axis=-1).astype(jnp.bfloat16)
    projected = projected.reshape(req_count, local_reqs, new_count, query_cols + 2 * key_cols)
    by_shift = jnp.stack([shift(projected[k], -k) for k in range(req_count)], axis=0)
    source_block = (jnp.arange(req_count, dtype=jnp.int32) - req_index) % req_count
    owned_rows = jnp.take(by_shift, source_block, axis=0)
    owned_rows = jnp.transpose(owned_rows, (1, 2, 0, 3))
    queries = owned_rows[..., :query_cols].reshape(local_reqs, new_count, KVH, groups, HD)
    fresh_keys = owned_rows[..., query_cols : query_cols + key_cols].reshape(
        local_reqs, new_count, KVH, HD
    )
    fresh_values = owned_rows[..., query_cols + key_cols :].reshape(local_reqs, new_count, KVH, HD)
    score_scale = 1.0 / math.sqrt(HD)
    kernel_queries = jnp.transpose(queries, (0, 2, 3, 1, 4)).reshape(
        local_reqs, KVH, groups * new_count, HD
    )
    keys_out, values_out, gathered_sum, row_peak, row_mass = arrive_and_attend(
        arrival_src,
        my_lengths,
        (seq_index * positions).reshape(1).astype(jnp.int32),
        incoming.reshape(pages_dev, 2, page_len, kv_width),
        kernel_queries,
        fresh_keys.reshape(local_reqs, new_count, kv_width),
        fresh_values.reshape(local_reqs, new_count, kv_width),
        score_scale,
    )
    gathered_sum = gathered_sum.reshape(local_reqs, KVH, groups, new_count, HD)
    row_peak = row_peak.reshape(local_reqs, KVH, groups, new_count)
    row_mass = row_mass.reshape(local_reqs, KVH, groups, new_count)
    stat_rows = row_peak.size // HD
    step = 1
    while step < seq_count:
        pairs = [(i, i ^ step) for i in range(seq_count)]
        packed = jnp.concatenate(
            [
                gathered_sum.reshape(-1, HD),
                row_peak.reshape(stat_rows, HD),
                row_mass.reshape(stat_rows, HD),
            ],
            axis=0,
        )
        other = lax.ppermute(packed, "seq", pairs)
        peer_sum = other[: gathered_sum.size // HD].reshape(gathered_sum.shape)
        peer_peak = other[gathered_sum.size // HD : -stat_rows].reshape(row_peak.shape)
        peer_mass = other[-stat_rows:].reshape(row_mass.shape)
        upper = (seq_index & step) != 0
        peak_lo = jnp.where(upper, peer_peak, row_peak)
        peak_hi = jnp.where(upper, row_peak, peer_peak)
        mass_lo = jnp.where(upper, peer_mass, row_mass)
        mass_hi = jnp.where(upper, row_mass, peer_mass)
        sum_lo = jnp.where(upper, peer_sum, gathered_sum)
        sum_hi = jnp.where(upper, gathered_sum, peer_sum)
        merged_peak = jnp.maximum(peak_lo, peak_hi)
        scale_lo = jnp.exp(peak_lo - merged_peak)
        scale_hi = jnp.exp(peak_hi - merged_peak)
        row_mass = mass_lo * scale_lo + mass_hi * scale_hi
        gathered_sum = sum_lo * scale_lo[..., None] + sum_hi * scale_hi[..., None]
        row_peak = merged_peak
        step *= 2
    own_scores = (
        jnp.einsum("rtkgd,rskd->rkgts", queries, fresh_keys, preferred_element_type=jnp.float32)
        * score_scale
    )
    causal = new_index[None, :] <= new_index[:, None]
    own_scores = jnp.where(causal, own_scores, MASKED)
    final_peak = jnp.maximum(row_peak, jnp.max(own_scores, axis=-1))
    carried = jnp.exp(row_peak - final_peak)
    own_weights = jnp.where(causal, jnp.exp(own_scores - final_peak[..., None]), 0.0)
    row_mass = row_mass * carried + jnp.sum(own_weights, axis=-1)
    gathered_sum = gathered_sum * carried[..., None] + jnp.einsum(
        "rkgts,rskd->rkgtd",
        own_weights.astype(jnp.bfloat16),
        fresh_values,
        preferred_element_type=jnp.float32,
    )
    attended = (
        jnp.transpose(gathered_sum / row_mass[..., None], (0, 3, 1, 2, 4))
        .reshape(local_reqs, new_count, KVH * groups * HD)
        .astype(jnp.bfloat16)
    )
    head_cols = attended.shape[-1] // req_count
    headed = jnp.concatenate(
        [
            shift(
                lax.dynamic_slice_in_dim(
                    attended, ((req_index + k) % req_count) * head_cols, head_cols, axis=2
                ),
                k,
            )
            for k in range(req_count)
        ],
        axis=0,
    )
    partial_out = (
        jnp.dot(headed.reshape(row_count * new_count, -1), w_out, preferred_element_type=jnp.float32)
        .reshape(req_count, local_reqs, new_count, model_width)
        .astype(jnp.bfloat16)
    )
    projected_out = shift(partial_out[0], 0).astype(jnp.float32)
    for k in range(1, req_count):
        projected_out = projected_out + shift(partial_out[k], -k).astype(jnp.float32)
    out_hidden = (tokens_wide + projected_out).astype(jnp.bfloat16)
    return (out_hidden, keys_out, values_out)


def solution(mesh):
    return jax.shard_map(
        shards,
        mesh=mesh,
        in_specs=(
            P("req", None, None),
            P(),
            P(None, "req"),
            P(None, "req"),
            P(None, "req"),
            P("req", None),
            P(("req", "seq"), None, None),
            P(("req", "seq"), None, None),
            P(),
            P(),
            P(),
        ),
        out_specs=(P("req", None, None), P("req", "seq", None), P("req", "seq", None)),
        check_vma=False,
    )
```

```python
import functools
import math

import jax
import jax.numpy as jnp
from jax import lax
from jax.experimental import pallas as pl
from jax.experimental.pallas import tpu as pltpu
from jax.sharding import PartitionSpec as P

H = 16
KVH = 8
HD = 128


NORM_EPS = 1e-05
ROPE_BASE = 1000000.0
MASKED = -1e30


def rotate(values, places):
    half_dim = values.shape[-1] // 2
    steps_up = jnp.arange(half_dim, dtype=jnp.float32) * (2.0 / values.shape[-1])
    inverse = ROPE_BASE ** (-steps_up)
    angles = places.astype(jnp.float32)[..., None] * inverse
    cosine = jnp.cos(angles)[..., None, :]
    sine_part = jnp.sin(angles)[..., None, :]
    first_half = values[..., :half_dim]
    second_half = values[..., half_dim:]
    return jnp.concatenate(
        [
            first_half * cosine - second_half * sine_part,
            second_half * cosine + first_half * sine_part,
        ],
        axis=-1,
    )


def _arrive_kernel(
    arrival_ref, lengths_ref, base_ref, incoming_ref, q_ref, fk_ref, fv_ref,
    keys_out_ref, values_out_ref, acc_ref, peak_ref, mass_ref,
    kbuf, vbuf, in_sem, out_sem, *, scale
):
    r = pl.program_id(0)
    n = pl.num_programs(0)
    slot = r % 2
    positions = kbuf.shape[1]
    page_len = incoming_ref.shape[2]
    pages = positions // page_len
    heads = q_ref.shape[1]
    head_dim = q_ref.shape[3]
    new_count = fk_ref.shape[1]
    bufs = (kbuf, vbuf)
    outs = (keys_out_ref, values_out_ref)

    def page_copy(req, s, half, pp, src):
        return pltpu.make_async_copy(
            incoming_ref.at[src, half],
            bufs[half].at[s, pl.ds(pp * page_len, page_len)],
            in_sem.at[half, s, pp],
        )

    def fetch(req, s):
        for pp in range(pages):
            src = arrival_ref[req * pages + pp]
            for half in range(2):
                page_copy(req, s, half, pp, src).start()

    def wait_fetch(s):
        for pp in range(pages):
            for half in range(2):
                page_copy(0, s, half, pp, 0).wait()

    def out_copy(req, s, half):
        return pltpu.make_async_copy(bufs[half].at[s], outs[half].at[req], out_sem.at[half, s])

    @pl.when(r == 0)
    def _():
        fetch(0, 0)

    wait_fetch(slot)

    @pl.when(r + 1 < n)
    def _():
        @pl.when(r >= 1)
        def _():
            for half in range(2):
                out_copy(r - 1, 1 - slot, half).wait()

        fetch(r + 1, 1 - slot)

    length = lengths_ref[r]
    base = base_ref[0]
    spots = base + lax.broadcasted_iota(jnp.int32, (1, positions), 1)
    live = spots < length
    for kh in range(heads):
        cols = pl.ds(kh * head_dim, head_dim)
        keys_h = kbuf[slot, :, cols]
        query_h = q_ref[0, kh]
        scores = lax.dot_general(
            query_h, keys_h, (((1,), (1,)), ((), ())), preferred_element_type=jnp.float32
        ) * scale
        scores = jnp.where(live, scores, MASKED)
        peak = jnp.max(scores, axis=1, keepdims=True)
        weights = jnp.where(live, jnp.exp(scores - peak), 0.0)
        peak_ref[0, kh] = peak
        mass_ref[0, kh] = jnp.sum(weights, axis=1, keepdims=True)
        acc_ref[0, kh] = jnp.dot(
            weights.astype(jnp.bfloat16), vbuf[slot, :, cols],
            preferred_element_type=jnp.float32,
        )
    first = length - base
    tile0 = (first // page_len) * page_len
    row_ids = lax.broadcasted_iota(jnp.int32, (page_len, 1), 0)
    fresh_k = fk_ref[0]
    fresh_v = fv_ref[0]
    for tile in (tile0, tile0 + page_len):
        @pl.when(jnp.logical_and(tile >= 0, tile < positions))
        def _():
            start = pl.multiple_of(tile, page_len)
            rows = pl.ds(start, page_len)
            block_k = kbuf[slot, rows, :]
            block_v = vbuf[slot, rows, :]
            for t in range(new_count):
                hit = row_ids == first + t - tile
                block_k = jnp.where(hit, fresh_k[t : t + 1, :], block_k)
                block_v = jnp.where(hit, fresh_v[t : t + 1, :], block_v)
            kbuf[slot, rows, :] = block_k
            vbuf[slot, rows, :] = block_v

    for half in range(2):
        out_copy(r, slot, half).start()

    @pl.when(r == n - 1)
    def _():
        @pl.when(r >= 1)
        def _():
            for half in range(2):
                out_copy(r - 1, 1 - slot, half).wait()

        for half in range(2):
            out_copy(r, slot, half).wait()


def arrive_and_attend(arrival_src, lengths, base, incoming, queries, fresh_k, fresh_v, scale):
    local_reqs, new_count, kv_width = fresh_k.shape
    _, heads, rows, head_dim = queries.shape
    positions = arrival_src.shape[0] // local_reqs * incoming.shape[2]
    pages = positions // incoming.shape[2]
    grid_spec = pltpu.PrefetchScalarGridSpec(
        num_scalar_prefetch=3,
        grid=(local_reqs,),
        in_specs=[
            pl.BlockSpec(memory_space=pl.ANY),
            pl.BlockSpec((1, heads, rows, head_dim), lambda r, *_: (r, 0, 0, 0)),
            pl.BlockSpec((1, new_count, kv_width), lambda r, *_: (r, 0, 0)),
            pl.BlockSpec((1, new_count, kv_width), lambda r, *_: (r, 0, 0)),
        ],
        out_specs=[
            pl.BlockSpec(memory_space=pl.ANY),
            pl.BlockSpec(memory_space=pl.ANY),
            pl.BlockSpec((1, heads, rows, head_dim), lambda r, *_: (r, 0, 0, 0)),
            pl.BlockSpec((1, heads, rows, 1), lambda r, *_: (r, 0, 0, 0)),
            pl.BlockSpec((1, heads, rows, 1), lambda r, *_: (r, 0, 0, 0)),
        ],
        scratch_shapes=[
            pltpu.VMEM((2, positions, kv_width), jnp.bfloat16),
            pltpu.VMEM((2, positions, kv_width), jnp.bfloat16),
            pltpu.SemaphoreType.DMA((2, 2, pages)),
            pltpu.SemaphoreType.DMA((2, 2)),
        ],
    )
    cache_bytes = 2 * local_reqs * positions * kv_width * 2
    return pl.pallas_call(
        functools.partial(_arrive_kernel, scale=scale),
        out_shape=[
            jax.ShapeDtypeStruct((local_reqs, positions, kv_width), jnp.bfloat16),
            jax.ShapeDtypeStruct((local_reqs, positions, kv_width), jnp.bfloat16),
            jax.ShapeDtypeStruct((local_reqs, heads, rows, head_dim), jnp.float32),
            jax.ShapeDtypeStruct((local_reqs, heads, rows, 1), jnp.float32),
            jax.ShapeDtypeStruct((local_reqs, heads, rows, 1), jnp.float32),
        ],
        grid_spec=grid_spec,
        compiler_params=pltpu.CompilerParams(dimension_semantics=("arbitrary",)),
        cost_estimate=pl.CostEstimate(
            flops=4 * local_reqs * heads * rows * positions * head_dim,
            transcendentals=local_reqs * heads * rows * positions,
            bytes_accessed=2 * cache_bytes,
        ),
        name="arrive_and_attend",
    )(arrival_src, lengths, base, incoming, queries, fresh_k, fresh_v)


def shards(
    new_tokens,
    norm_gain,
    w_query,
    w_key,
    w_value,
    w_out,
    pool_keys,
    pool_values,
    cache_lengths,
    owner,
    page_table,
):
    req_count = lax.axis_size("req")
    seq_count = lax.axis_size("seq")
    devices = req_count * seq_count
    req_index = lax.axis_index("req")
    seq_index = lax.axis_index("seq")
    device_index = req_index * seq_count + seq_index
    local_reqs, new_count, model_width = new_tokens.shape
    request_total = owner.shape[0]
    pages_dev, page_len, kv_width = pool_keys.shape
    pages_req = page_table.shape[1]
    pages_home = pages_req // seq_count
    positions = pages_home * page_len
    per_peer = pages_dev // devices
    groups = H // KVH
    query_cols = w_query.shape[1]
    key_cols = w_key.shape[1]
    all_requests = jnp.arange(request_total, dtype=jnp.int32)
    hits = owner[None, :] == all_requests[:, None]
    slot_request = jnp.sum(jnp.where(hits, all_requests[None, :], 0), axis=1)
    slot_lengths = jnp.sum(jnp.where(hits, cache_lengths[None, :], 0), axis=1)
    my_lengths = lax.dynamic_slice_in_dim(slot_lengths, req_index * local_reqs, local_reqs)
    slot_pages = page_table[slot_request]
    home_table = jnp.transpose(
        slot_pages.reshape(req_count, local_reqs, seq_count, pages_home), (0, 2, 1, 3)
    ).reshape(devices, local_reqs * pages_home)
    my_home = lax.dynamic_slice_in_dim(home_table, device_index, 1, axis=0).reshape(-1)
    arrival_src = my_home // pages_dev
    held_here = (home_table // pages_dev) == device_index
    send_pick = jnp.sum(jnp.where(held_here, home_table % pages_dev, 0), axis=1)
    tokens_wide = new_tokens.astype(jnp.float32)
    square_mean = jnp.mean(tokens_wide * tokens_wide, axis=-1, keepdims=True)
    normed = (tokens_wide * lax.rsqrt(square_mean + NORM_EPS) * norm_gain).astype(jnp.bfloat16)
    new_index = jnp.arange(new_count, dtype=jnp.int32)
    def shift(value, places):
        if places % req_count == 0:
            return value
        pairs = [(i, (i + places) % req_count) for i in range(req_count)]
        return lax.ppermute(value, "req", pairs)

    row_block = jnp.concatenate([shift(normed, k) for k in range(req_count)], axis=0)
    outgoing = jnp.stack([pool_keys[send_pick], pool_values[send_pick]], axis=1)
    outgoing = outgoing.reshape(devices, per_peer, 2, page_len, kv_width)
    outgoing, row_block = lax.optimization_barrier((outgoing, row_block))
    incoming = lax.all_to_all(outgoing, ("req", "seq"), split_axis=0, concat_axis=0, tiled=True)
    row_count = row_block.shape[0]
    flat_rows = row_block.reshape(row_count * new_count, model_width)
    row_group = (req_index - jnp.arange(req_count, dtype=jnp.int32)) % req_count
    row_lengths = jnp.take(slot_lengths.reshape(req_count, local_reqs), row_group, axis=0).reshape(-1)
    places = row_lengths[:, None] + new_index[None, :]
    queries_now = jnp.dot(flat_rows, w_query, preferred_element_type=jnp.float32).reshape(
        row_count, new_count, query_cols // HD, HD
    )
    keys_now = jnp.dot(flat_rows, w_key, preferred_element_type=jnp.float32).reshape(
        row_count, new_count, key_cols // HD, HD
    )
    values_now = jnp.dot(flat_rows, w_value, preferred_element_type=jnp.float32).reshape(
        row_count, new_count, key_cols
    )
    queries_now = rotate(queries_now, places).reshape(row_count, new_count, query_cols)
    keys_now = rotate(keys_now, places).reshape(row_count, new_count, key_cols)
    projected = jnp.concatenate([queries_now, keys_now, values_now], axis=-1).astype(jnp.bfloat16)
    projected = projected.reshape(req_count, local_reqs, new_count, query_cols + 2 * key_cols)
    by_shift = jnp.stack([shift(projected[k], -k) for k in range(req_count)], axis=0)
    source_block = (jnp.arange(req_count, dtype=jnp.int32) - req_index) % req_count
    owned_rows = jnp.take(by_shift, source_block, axis=0)
    owned_rows = jnp.transpose(owned_rows, (1, 2, 0, 3))
    queries = owned_rows[..., :query_cols].reshape(local_reqs, new_count, KVH, groups, HD)
    fresh_keys = owned_rows[..., query_cols : query_cols + key_cols].reshape(
        local_reqs, new_count, KVH, HD
    )
    fresh_values = owned_rows[..., query_cols + key_cols :].reshape(local_reqs, new_count, KVH, HD)
    score_scale = 1.0 / math.sqrt(HD)
    kernel_queries = jnp.transpose(queries, (0, 2, 3, 1, 4)).reshape(
        local_reqs, KVH, groups * new_count, HD
    )
    keys_out, values_out, gathered_sum, row_peak, row_mass = arrive_and_attend(
        arrival_src,
        my_lengths,
        (seq_index * positions).reshape(1).astype(jnp.int32),
        incoming.reshape(pages_dev, 2, page_len, kv_width),
        kernel_queries,
        fresh_keys.reshape(local_reqs, new_count, kv_width),
        fresh_values.reshape(local_reqs, new_count, kv_width),
        score_scale,
    )
    gathered_sum = gathered_sum.reshape(local_reqs, KVH, groups, new_count, HD)
    row_peak = row_peak.reshape(local_reqs, KVH, groups, new_count)
    row_mass = row_mass.reshape(local_reqs, KVH, groups, new_count)
    def pack(total, peak, mass):
        stat_rows = peak.size // HD
        return jnp.concatenate(
            [total.reshape(-1, HD), peak.reshape(stat_rows, HD), mass.reshape(stat_rows, HD)], axis=0
        )

    def unpack(packed, total, peak, mass):
        stat_rows = peak.size // HD
        return (
            packed[: total.size // HD].reshape(total.shape),
            packed[total.size // HD : -stat_rows].reshape(peak.shape),
            packed[-stat_rows:].reshape(mass.shape),
        )

    def merge(step, total, peak, mass):
        pairs = [(i, i ^ step) for i in range(seq_count)]
        other = lax.ppermute(pack(total, peak, mass), "seq", pairs)
        peer_sum, peer_peak, peer_mass = unpack(other, total, peak, mass)
        upper = (seq_index & step) != 0
        peak_lo = jnp.where(upper, peer_peak, peak)
        peak_hi = jnp.where(upper, peak, peer_peak)
        mass_lo = jnp.where(upper, peer_mass, mass)
        mass_hi = jnp.where(upper, mass, peer_mass)
        sum_lo = jnp.where(upper, peer_sum, total)
        sum_hi = jnp.where(upper, total, peer_sum)
        merged_peak = jnp.maximum(peak_lo, peak_hi)
        scale_lo = jnp.exp(peak_lo - merged_peak)
        scale_hi = jnp.exp(peak_hi - merged_peak)
        return (
            sum_lo * scale_lo[..., None] + sum_hi * scale_hi[..., None],
            merged_peak,
            mass_lo * scale_lo + mass_hi * scale_hi,
        )

    gathered_sum, row_peak, row_mass = merge(1, gathered_sum, row_peak, row_mass)
    half = local_reqs // 2
    core = seq_index % 2
    mine = tuple(
        lax.dynamic_slice_in_dim(x, core * half, half, axis=0)
        for x in (gathered_sum, row_peak, row_mass)
    )
    step = 2
    while step < seq_count:
        mine = merge(step, *mine)
        step *= 2
    mine_packed = pack(*mine)
    other_packed = lax.ppermute(mine_packed, "seq", [(i, i ^ 1) for i in range(seq_count)])
    first_half = unpack(jnp.where(core == 0, mine_packed, other_packed), *mine)
    second_half = unpack(jnp.where(core == 0, other_packed, mine_packed), *mine)
    gathered_sum, row_peak, row_mass = (
        jnp.concatenate([p, q], axis=0) for p, q in zip(first_half, second_half)
    )
    own_scores = (
        jnp.einsum("rtkgd,rskd->rkgts", queries, fresh_keys, preferred_element_type=jnp.float32)
        * score_scale
    )
    causal = new_index[None, :] <= new_index[:, None]
    own_scores = jnp.where(causal, own_scores, MASKED)
    final_peak = jnp.maximum(row_peak, jnp.max(own_scores, axis=-1))
    carried = jnp.exp(row_peak - final_peak)
    own_weights = jnp.where(causal, jnp.exp(own_scores - final_peak[..., None]), 0.0)
    row_mass = row_mass * carried + jnp.sum(own_weights, axis=-1)
    gathered_sum = gathered_sum * carried[..., None] + jnp.einsum(
        "rkgts,rskd->rkgtd",
        own_weights.astype(jnp.bfloat16),
        fresh_values,
        preferred_element_type=jnp.float32,
    )
    attended = (
        jnp.transpose(gathered_sum / row_mass[..., None], (0, 3, 1, 2, 4))
        .reshape(local_reqs, new_count, KVH * groups * HD)
        .astype(jnp.bfloat16)
    )
    head_cols = attended.shape[-1] // req_count
    headed = jnp.concatenate(
        [
            shift(
                lax.dynamic_slice_in_dim(
                    attended, ((req_index + k) % req_count) * head_cols, head_cols, axis=2
                ),
                k,
            )
            for k in range(req_count)
        ],
        axis=0,
    )
    partial_out = (
        jnp.dot(headed.reshape(row_count * new_count, -1), w_out, preferred_element_type=jnp.float32)
        .reshape(req_count, local_reqs, new_count, model_width)
        .astype(jnp.bfloat16)
    )
    projected_out = shift(partial_out[0], 0).astype(jnp.float32)
    for k in range(1, req_count):
        projected_out = projected_out + shift(partial_out[k], -k).astype(jnp.float32)
    out_hidden = (tokens_wide + projected_out).astype(jnp.bfloat16)
    return (out_hidden, keys_out, values_out)


def solution(mesh):
    return jax.shard_map(
        shards,
        mesh=mesh,
        in_specs=(
            P("req", None, None),
            P(),
            P(None, "req"),
            P(None, "req"),
            P(None, "req"),
            P("req", None),
            P(("req", "seq"), None, None),
            P(("req", "seq"), None, None),
            P(),
            P(),
            P(),
        ),
        out_specs=(P("req", None, None), P("req", "seq", None), P("req", "seq", None)),
        check_vma=False,
    )
```

```python
import functools
import math

import jax
import jax.numpy as jnp
from jax import lax
from jax.experimental import pallas as pl
from jax.experimental.pallas import tpu as pltpu
from jax.sharding import PartitionSpec as P

H = 16
KVH = 8
HD = 128


NORM_EPS = 1e-05
ROPE_BASE = 1000000.0
MASKED = -1e30


def rotate(values, places):
    half_dim = values.shape[-1] // 2
    steps_up = jnp.arange(half_dim, dtype=jnp.float32) * (2.0 / values.shape[-1])
    inverse = ROPE_BASE ** (-steps_up)
    angles = places.astype(jnp.float32)[..., None] * inverse
    cosine = jnp.cos(angles)[..., None, :]
    sine_part = jnp.sin(angles)[..., None, :]
    first_half = values[..., :half_dim]
    second_half = values[..., half_dim:]
    return jnp.concatenate(
        [
            first_half * cosine - second_half * sine_part,
            second_half * cosine + first_half * sine_part,
        ],
        axis=-1,
    )


def _arrive_kernel(
    arrival_ref, lengths_ref, base_ref, incoming_ref, q_ref, fk_ref, fv_ref,
    keys_out_ref, values_out_ref, acc_ref, peak_ref, mass_ref,
    buf, in_sem, out_sem, *, scale
):
    r = pl.program_id(0)
    n = pl.num_programs(0)
    slot = r % 2
    pages = buf.shape[1]
    page_len = buf.shape[3]
    positions = pages * page_len
    heads = q_ref.shape[1]
    head_dim = q_ref.shape[3]
    new_count = fk_ref.shape[1]
    outs = (keys_out_ref, values_out_ref)

    def page_copy(s, pp, src):
        return pltpu.make_async_copy(incoming_ref.at[src], buf.at[s, pp], in_sem.at[s, pp])

    def fetch(req, s):
        for pp in range(pages):
            page_copy(s, pp, arrival_ref[req * pages + pp]).start()

    def wait_fetch(s):
        for pp in range(pages):
            page_copy(s, pp, 0).wait()

    def out_copy(req, s, half):
        return pltpu.make_async_copy(buf.at[s, :, half], outs[half].at[req], out_sem.at[half, s])

    @pl.when(r == 0)
    def _():
        fetch(0, 0)

    wait_fetch(slot)

    @pl.when(r + 1 < n)
    def _():
        @pl.when(r >= 1)
        def _():
            for half in range(2):
                out_copy(r - 1, 1 - slot, half).wait()

        fetch(r + 1, 1 - slot)

    length = lengths_ref[r]
    base = base_ref[0]
    spots = base + lax.broadcasted_iota(jnp.int32, (1, positions), 1)
    live = spots < length
    for kh in range(heads):
        cols = pl.ds(kh * head_dim, head_dim)
        keys_h = buf[slot, :, 0, :, cols].reshape(positions, head_dim)
        values_h = buf[slot, :, 1, :, cols].reshape(positions, head_dim)
        query_h = q_ref[0, kh]
        scores = lax.dot_general(
            query_h, keys_h, (((1,), (1,)), ((), ())), preferred_element_type=jnp.float32
        ) * scale
        scores = jnp.where(live, scores, MASKED)
        peak = jnp.max(scores, axis=1, keepdims=True)
        weights = jnp.where(live, jnp.exp(scores - peak), 0.0)
        peak_ref[0, kh] = peak
        mass_ref[0, kh] = jnp.sum(weights, axis=1, keepdims=True)
        acc_ref[0, kh] = jnp.dot(
            weights.astype(jnp.bfloat16), values_h, preferred_element_type=jnp.float32
        )
    first = length - base
    page0 = first // page_len
    row_ids = lax.broadcasted_iota(jnp.int32, (page_len, 1), 0)
    fresh = (fk_ref[0], fv_ref[0])
    for page in (page0, page0 + 1):
        @pl.when(jnp.logical_and(page >= 0, page < pages))
        def _():
            for half in range(2):
                block = buf[slot, page, half]
                for t in range(new_count):
                    hit = row_ids == first + t - page * page_len
                    block = jnp.where(hit, fresh[half][t : t + 1, :], block)
                buf[slot, page, half] = block

    for half in range(2):
        out_copy(r, slot, half).start()

    @pl.when(r == n - 1)
    def _():
        @pl.when(r >= 1)
        def _():
            for half in range(2):
                out_copy(r - 1, 1 - slot, half).wait()

        for half in range(2):
            out_copy(r, slot, half).wait()


def arrive_and_attend(arrival_src, lengths, base, incoming, queries, fresh_k, fresh_v, scale):
    local_reqs, new_count, kv_width = fresh_k.shape
    _, heads, rows, head_dim = queries.shape
    page_len = incoming.shape[2]
    pages = arrival_src.shape[0] // local_reqs
    positions = pages * page_len
    grid_spec = pltpu.PrefetchScalarGridSpec(
        num_scalar_prefetch=3,
        grid=(local_reqs,),
        in_specs=[
            pl.BlockSpec(memory_space=pl.ANY),
            pl.BlockSpec((1, heads, rows, head_dim), lambda r, *_: (r, 0, 0, 0)),
            pl.BlockSpec((1, new_count, kv_width), lambda r, *_: (r, 0, 0)),
            pl.BlockSpec((1, new_count, kv_width), lambda r, *_: (r, 0, 0)),
        ],
        out_specs=[
            pl.BlockSpec(memory_space=pl.ANY),
            pl.BlockSpec(memory_space=pl.ANY),
            pl.BlockSpec((1, heads, rows, head_dim), lambda r, *_: (r, 0, 0, 0)),
            pl.BlockSpec((1, heads, rows, 1), lambda r, *_: (r, 0, 0, 0)),
            pl.BlockSpec((1, heads, rows, 1), lambda r, *_: (r, 0, 0, 0)),
        ],
        scratch_shapes=[
            pltpu.VMEM((2, pages, 2, page_len, kv_width), jnp.bfloat16),
            pltpu.SemaphoreType.DMA((2, pages)),
            pltpu.SemaphoreType.DMA((2, 2)),
        ],
    )
    cache_bytes = 2 * local_reqs * positions * kv_width * 2
    keys_out, values_out, acc, peak, mass = pl.pallas_call(
        functools.partial(_arrive_kernel, scale=scale),
        out_shape=[
            jax.ShapeDtypeStruct((local_reqs, pages, page_len, kv_width), jnp.bfloat16),
            jax.ShapeDtypeStruct((local_reqs, pages, page_len, kv_width), jnp.bfloat16),
            jax.ShapeDtypeStruct((local_reqs, heads, rows, head_dim), jnp.float32),
            jax.ShapeDtypeStruct((local_reqs, heads, rows, 1), jnp.float32),
            jax.ShapeDtypeStruct((local_reqs, heads, rows, 1), jnp.float32),
        ],
        grid_spec=grid_spec,
        compiler_params=pltpu.CompilerParams(dimension_semantics=("arbitrary",)),
        cost_estimate=pl.CostEstimate(
            flops=4 * local_reqs * heads * rows * positions * head_dim,
            transcendentals=local_reqs * heads * rows * positions,
            bytes_accessed=2 * cache_bytes,
        ),
        name="arrive_and_attend",
    )(arrival_src, lengths, base, incoming, queries, fresh_k, fresh_v)
    keys_out = keys_out.reshape(local_reqs, positions, kv_width)
    values_out = values_out.reshape(local_reqs, positions, kv_width)
    return keys_out, values_out, acc, peak, mass


def shards(
    new_tokens,
    norm_gain,
    w_query,
    w_key,
    w_value,
    w_out,
    pool_keys,
    pool_values,
    cache_lengths,
    owner,
    page_table,
):
    req_count = lax.axis_size("req")
    seq_count = lax.axis_size("seq")
    devices = req_count * seq_count
    req_index = lax.axis_index("req")
    seq_index = lax.axis_index("seq")
    device_index = req_index * seq_count + seq_index
    local_reqs, new_count, model_width = new_tokens.shape
    request_total = owner.shape[0]
    pages_dev, page_len, kv_width = pool_keys.shape
    pages_req = page_table.shape[1]
    pages_home = pages_req // seq_count
    positions = pages_home * page_len
    per_peer = pages_dev // devices
    groups = H // KVH
    query_cols = w_query.shape[1]
    key_cols = w_key.shape[1]
    all_requests = jnp.arange(request_total, dtype=jnp.int32)
    hits = owner[None, :] == all_requests[:, None]
    slot_request = jnp.sum(jnp.where(hits, all_requests[None, :], 0), axis=1)
    slot_lengths = jnp.sum(jnp.where(hits, cache_lengths[None, :], 0), axis=1)
    my_lengths = lax.dynamic_slice_in_dim(slot_lengths, req_index * local_reqs, local_reqs)
    slot_pages = page_table[slot_request]
    home_table = jnp.transpose(
        slot_pages.reshape(req_count, local_reqs, seq_count, pages_home), (0, 2, 1, 3)
    ).reshape(devices, local_reqs * pages_home)
    my_home = lax.dynamic_slice_in_dim(home_table, device_index, 1, axis=0).reshape(-1)
    arrival_src = my_home // pages_dev
    held_here = (home_table // pages_dev) == device_index
    send_pick = jnp.sum(jnp.where(held_here, home_table % pages_dev, 0), axis=1)
    tokens_wide = new_tokens.astype(jnp.float32)
    square_mean = jnp.mean(tokens_wide * tokens_wide, axis=-1, keepdims=True)
    normed = (tokens_wide * lax.rsqrt(square_mean + NORM_EPS) * norm_gain).astype(jnp.bfloat16)
    new_index = jnp.arange(new_count, dtype=jnp.int32)
    def shift(value, places):
        if places % req_count == 0:
            return value
        pairs = [(i, (i + places) % req_count) for i in range(req_count)]
        return lax.ppermute(value, "req", pairs)

    row_block = jnp.concatenate([shift(normed, k) for k in range(req_count)], axis=0)
    outgoing = jnp.stack([pool_keys[send_pick], pool_values[send_pick]], axis=1)
    outgoing = outgoing.reshape(devices, per_peer, 2, page_len, kv_width)
    outgoing, row_block = lax.optimization_barrier((outgoing, row_block))
    incoming = lax.all_to_all(outgoing, ("req", "seq"), split_axis=0, concat_axis=0, tiled=True)
    row_count = row_block.shape[0]
    flat_rows = row_block.reshape(row_count * new_count, model_width)
    row_group = (req_index - jnp.arange(req_count, dtype=jnp.int32)) % req_count
    row_lengths = jnp.take(slot_lengths.reshape(req_count, local_reqs), row_group, axis=0).reshape(-1)
    places = row_lengths[:, None] + new_index[None, :]
    queries_now = jnp.dot(flat_rows, w_query, preferred_element_type=jnp.float32).reshape(
        row_count, new_count, query_cols // HD, HD
    )
    keys_now = jnp.dot(flat_rows, w_key, preferred_element_type=jnp.float32).reshape(
        row_count, new_count, key_cols // HD, HD
    )
    values_now = jnp.dot(flat_rows, w_value, preferred_element_type=jnp.float32).reshape(
        row_count, new_count, key_cols
    )
    queries_now = rotate(queries_now, places).reshape(row_count, new_count, query_cols)
    keys_now = rotate(keys_now, places).reshape(row_count, new_count, key_cols)
    projected = jnp.concatenate([queries_now, keys_now, values_now], axis=-1).astype(jnp.bfloat16)
    projected = projected.reshape(req_count, local_reqs, new_count, query_cols + 2 * key_cols)
    by_shift = jnp.stack([shift(projected[k], -k) for k in range(req_count)], axis=0)
    source_block = (jnp.arange(req_count, dtype=jnp.int32) - req_index) % req_count
    owned_rows = jnp.take(by_shift, source_block, axis=0)
    owned_rows = jnp.transpose(owned_rows, (1, 2, 0, 3))
    queries = owned_rows[..., :query_cols].reshape(local_reqs, new_count, KVH, groups, HD)
    fresh_keys = owned_rows[..., query_cols : query_cols + key_cols].reshape(
        local_reqs, new_count, KVH, HD
    )
    fresh_values = owned_rows[..., query_cols + key_cols :].reshape(local_reqs, new_count, KVH, HD)
    score_scale = 1.0 / math.sqrt(HD)
    kernel_queries = jnp.transpose(queries, (0, 2, 3, 1, 4)).reshape(
        local_reqs, KVH, groups * new_count, HD
    )
    keys_out, values_out, gathered_sum, row_peak, row_mass = arrive_and_attend(
        arrival_src,
        my_lengths,
        (seq_index * positions).reshape(1).astype(jnp.int32),
        incoming.reshape(pages_dev, 2, page_len, kv_width),
        kernel_queries,
        fresh_keys.reshape(local_reqs, new_count, kv_width),
        fresh_values.reshape(local_reqs, new_count, kv_width),
        score_scale,
    )
    gathered_sum = gathered_sum.reshape(local_reqs, KVH, groups, new_count, HD)
    row_peak = row_peak.reshape(local_reqs, KVH, groups, new_count)
    row_mass = row_mass.reshape(local_reqs, KVH, groups, new_count)
    def pack(total, peak, mass):
        stat_rows = peak.size // HD
        return jnp.concatenate(
            [total.reshape(-1, HD), peak.reshape(stat_rows, HD), mass.reshape(stat_rows, HD)], axis=0
        )

    def unpack(packed, total, peak, mass):
        stat_rows = peak.size // HD
        return (
            packed[: total.size // HD].reshape(total.shape),
            packed[total.size // HD : -stat_rows].reshape(peak.shape),
            packed[-stat_rows:].reshape(mass.shape),
        )

    def merge(step, total, peak, mass):
        pairs = [(i, i ^ step) for i in range(seq_count)]
        other = lax.ppermute(pack(total, peak, mass), "seq", pairs)
        peer_sum, peer_peak, peer_mass = unpack(other, total, peak, mass)
        upper = (seq_index & step) != 0
        peak_lo = jnp.where(upper, peer_peak, peak)
        peak_hi = jnp.where(upper, peak, peer_peak)
        mass_lo = jnp.where(upper, peer_mass, mass)
        mass_hi = jnp.where(upper, mass, peer_mass)
        sum_lo = jnp.where(upper, peer_sum, total)
        sum_hi = jnp.where(upper, total, peer_sum)
        merged_peak = jnp.maximum(peak_lo, peak_hi)
        scale_lo = jnp.exp(peak_lo - merged_peak)
        scale_hi = jnp.exp(peak_hi - merged_peak)
        return (
            sum_lo * scale_lo[..., None] + sum_hi * scale_hi[..., None],
            merged_peak,
            mass_lo * scale_lo + mass_hi * scale_hi,
        )

    gathered_sum, row_peak, row_mass = merge(1, gathered_sum, row_peak, row_mass)
    half = local_reqs // 2
    core = seq_index % 2
    mine = tuple(
        lax.dynamic_slice_in_dim(x, core * half, half, axis=0)
        for x in (gathered_sum, row_peak, row_mass)
    )
    step = 2
    while step < seq_count:
        mine = merge(step, *mine)
        step *= 2
    mine_packed = pack(*mine)
    other_packed = lax.ppermute(mine_packed, "seq", [(i, i ^ 1) for i in range(seq_count)])
    first_half = unpack(jnp.where(core == 0, mine_packed, other_packed), *mine)
    second_half = unpack(jnp.where(core == 0, other_packed, mine_packed), *mine)
    gathered_sum, row_peak, row_mass = (
        jnp.concatenate([p, q], axis=0) for p, q in zip(first_half, second_half)
    )
    own_scores = (
        jnp.einsum("rtkgd,rskd->rkgts", queries, fresh_keys, preferred_element_type=jnp.float32)
        * score_scale
    )
    causal = new_index[None, :] <= new_index[:, None]
    own_scores = jnp.where(causal, own_scores, MASKED)
    final_peak = jnp.maximum(row_peak, jnp.max(own_scores, axis=-1))
    carried = jnp.exp(row_peak - final_peak)
    own_weights = jnp.where(causal, jnp.exp(own_scores - final_peak[..., None]), 0.0)
    row_mass = row_mass * carried + jnp.sum(own_weights, axis=-1)
    gathered_sum = gathered_sum * carried[..., None] + jnp.einsum(
        "rkgts,rskd->rkgtd",
        own_weights.astype(jnp.bfloat16),
        fresh_values,
        preferred_element_type=jnp.float32,
    )
    attended = (
        jnp.transpose(gathered_sum / row_mass[..., None], (0, 3, 1, 2, 4))
        .reshape(local_reqs, new_count, KVH * groups * HD)
        .astype(jnp.bfloat16)
    )
    head_cols = attended.shape[-1] // req_count
    headed = jnp.concatenate(
        [
            shift(
                lax.dynamic_slice_in_dim(
                    attended, ((req_index + k) % req_count) * head_cols, head_cols, axis=2
                ),
                k,
            )
            for k in range(req_count)
        ],
        axis=0,
    )
    partial_out = (
        jnp.dot(headed.reshape(row_count * new_count, -1), w_out, preferred_element_type=jnp.float32)
        .reshape(req_count, local_reqs, new_count, model_width)
        .astype(jnp.bfloat16)
    )
    projected_out = shift(partial_out[0], 0).astype(jnp.float32)
    for k in range(1, req_count):
        projected_out = projected_out + shift(partial_out[k], -k).astype(jnp.float32)
    out_hidden = (tokens_wide + projected_out).astype(jnp.bfloat16)
    return (out_hidden, keys_out, values_out)


def solution(mesh):
    return jax.shard_map(
        shards,
        mesh=mesh,
        in_specs=(
            P("req", None, None),
            P(),
            P(None, "req"),
            P(None, "req"),
            P(None, "req"),
            P("req", None),
            P(("req", "seq"), None, None),
            P(("req", "seq"), None, None),
            P(),
            P(),
            P(),
        ),
        out_specs=(P("req", None, None), P("req", "seq", None), P("req", "seq", None)),
        check_vma=False,
    )
```

```python
import functools
import math

import jax
import jax.numpy as jnp
from jax import lax
from jax.experimental import pallas as pl
from jax.experimental.pallas import tpu as pltpu
from jax.sharding import PartitionSpec as P

H = 16
KVH = 8
HD = 128


NORM_EPS = 1e-05
ROPE_BASE = 1000000.0
MASKED = -1e30


def rotate(values, places):
    half_dim = values.shape[-1] // 2
    steps_up = jnp.arange(half_dim, dtype=jnp.float32) * (2.0 / values.shape[-1])
    inverse = ROPE_BASE ** (-steps_up)
    angles = places.astype(jnp.float32)[..., None] * inverse
    cosine = jnp.cos(angles)[..., None, :]
    sine_part = jnp.sin(angles)[..., None, :]
    first_half = values[..., :half_dim]
    second_half = values[..., half_dim:]
    return jnp.concatenate(
        [
            first_half * cosine - second_half * sine_part,
            second_half * cosine + first_half * sine_part,
        ],
        axis=-1,
    )


def _arrive_kernel(
    arrival_ref, lengths_ref, base_ref, incoming_ref, q_ref, fk_ref, fv_ref,
    keys_out_ref, values_out_ref, acc_ref, peak_ref, mass_ref,
    buf, in_sem, out_sem, *, scale
):
    r = pl.program_id(0)
    n = pl.num_programs(0)
    slot = r % 2
    pages = buf.shape[1]
    page_len = buf.shape[3]
    positions = pages * page_len
    heads = q_ref.shape[1]
    head_dim = q_ref.shape[2]
    new_count = fk_ref.shape[1]
    outs = (keys_out_ref, values_out_ref)

    def page_copy(s, pp, src):
        return pltpu.make_async_copy(incoming_ref.at[src], buf.at[s, pp], in_sem.at[s, pp])

    def fetch(req, s):
        for pp in range(pages):
            page_copy(s, pp, arrival_ref[req * pages + pp]).start()

    def wait_fetch(s):
        for pp in range(pages):
            page_copy(s, pp, 0).wait()

    def out_copy(req, s, half):
        return pltpu.make_async_copy(buf.at[s, :, half], outs[half].at[req], out_sem.at[half, s])

    @pl.when(r == 0)
    def _():
        fetch(0, 0)

    wait_fetch(slot)

    @pl.when(r + 1 < n)
    def _():
        @pl.when(r >= 1)
        def _():
            for half in range(2):
                out_copy(r - 1, 1 - slot, half).wait()

        fetch(r + 1, 1 - slot)

    length = lengths_ref[r]
    base = base_ref[0]
    spots = base + lax.broadcasted_iota(jnp.int32, (positions, 1), 0)
    live = spots < length
    for kh in range(heads):
        cols = pl.ds(kh * head_dim, head_dim)
        keys_h = buf[slot, :, 0, :, cols].reshape(positions, head_dim)
        values_h = buf[slot, :, 1, :, cols].reshape(positions, head_dim)
        query_t = q_ref[0, kh]
        scores = jnp.dot(keys_h, query_t, preferred_element_type=jnp.float32) * scale
        scores = jnp.where(live, scores, MASKED)
        peak = jnp.max(scores, axis=0, keepdims=True)
        weights = jnp.where(live, jnp.exp(scores - peak), 0.0)
        peak_ref[0, kh] = peak
        mass_ref[0, kh] = jnp.sum(weights, axis=0, keepdims=True)
        acc_ref[0, kh] = lax.dot_general(
            weights.astype(jnp.bfloat16), values_h, (((0,), (0,)), ((), ())),
            preferred_element_type=jnp.float32,
        )
    first = length - base
    page0 = first // page_len
    row_ids = lax.broadcasted_iota(jnp.int32, (page_len, 1), 0)
    fresh = (fk_ref[0], fv_ref[0])
    for page in (page0, page0 + 1):
        @pl.when(jnp.logical_and(page >= 0, page < pages))
        def _():
            for half in range(2):
                block = buf[slot, page, half]
                for t in range(new_count):
                    hit = row_ids == first + t - page * page_len
                    block = jnp.where(hit, fresh[half][t : t + 1, :], block)
                buf[slot, page, half] = block

    for half in range(2):
        out_copy(r, slot, half).start()

    @pl.when(r == n - 1)
    def _():
        @pl.when(r >= 1)
        def _():
            for half in range(2):
                out_copy(r - 1, 1 - slot, half).wait()

        for half in range(2):
            out_copy(r, slot, half).wait()


def arrive_and_attend(arrival_src, lengths, base, incoming, queries, fresh_k, fresh_v, scale):
    local_reqs, new_count, kv_width = fresh_k.shape
    _, heads, head_dim, rows = queries.shape
    page_len = incoming.shape[2]
    pages = arrival_src.shape[0] // local_reqs
    positions = pages * page_len
    grid_spec = pltpu.PrefetchScalarGridSpec(
        num_scalar_prefetch=3,
        grid=(local_reqs,),
        in_specs=[
            pl.BlockSpec(memory_space=pl.ANY),
            pl.BlockSpec((1, heads, head_dim, rows), lambda r, *_: (r, 0, 0, 0)),
            pl.BlockSpec((1, new_count, kv_width), lambda r, *_: (r, 0, 0)),
            pl.BlockSpec((1, new_count, kv_width), lambda r, *_: (r, 0, 0)),
        ],
        out_specs=[
            pl.BlockSpec(memory_space=pl.ANY),
            pl.BlockSpec(memory_space=pl.ANY),
            pl.BlockSpec((1, heads, rows, head_dim), lambda r, *_: (r, 0, 0, 0)),
            pl.BlockSpec((1, heads, 1, rows), lambda r, *_: (r, 0, 0, 0)),
            pl.BlockSpec((1, heads, 1, rows), lambda r, *_: (r, 0, 0, 0)),
        ],
        scratch_shapes=[
            pltpu.VMEM((2, pages, 2, page_len, kv_width), jnp.bfloat16),
            pltpu.SemaphoreType.DMA((2, pages)),
            pltpu.SemaphoreType.DMA((2, 2)),
        ],
    )
    cache_bytes = 2 * local_reqs * positions * kv_width * 2
    keys_out, values_out, acc, peak, mass = pl.pallas_call(
        functools.partial(_arrive_kernel, scale=scale),
        out_shape=[
            jax.ShapeDtypeStruct((local_reqs, pages, page_len, kv_width), jnp.bfloat16),
            jax.ShapeDtypeStruct((local_reqs, pages, page_len, kv_width), jnp.bfloat16),
            jax.ShapeDtypeStruct((local_reqs, heads, rows, head_dim), jnp.float32),
            jax.ShapeDtypeStruct((local_reqs, heads, 1, rows), jnp.float32),
            jax.ShapeDtypeStruct((local_reqs, heads, 1, rows), jnp.float32),
        ],
        grid_spec=grid_spec,
        compiler_params=pltpu.CompilerParams(dimension_semantics=("arbitrary",)),
        cost_estimate=pl.CostEstimate(
            flops=4 * local_reqs * heads * rows * positions * head_dim,
            transcendentals=local_reqs * heads * rows * positions,
            bytes_accessed=2 * cache_bytes,
        ),
        name="arrive_and_attend",
    )(arrival_src, lengths, base, incoming, queries, fresh_k, fresh_v)
    keys_out = keys_out.reshape(local_reqs, positions, kv_width)
    values_out = values_out.reshape(local_reqs, positions, kv_width)
    return keys_out, values_out, acc, peak, mass


def shards(
    new_tokens,
    norm_gain,
    w_query,
    w_key,
    w_value,
    w_out,
    pool_keys,
    pool_values,
    cache_lengths,
    owner,
    page_table,
):
    req_count = lax.axis_size("req")
    seq_count = lax.axis_size("seq")
    devices = req_count * seq_count
    req_index = lax.axis_index("req")
    seq_index = lax.axis_index("seq")
    device_index = req_index * seq_count + seq_index
    local_reqs, new_count, model_width = new_tokens.shape
    request_total = owner.shape[0]
    pages_dev, page_len, kv_width = pool_keys.shape
    pages_req = page_table.shape[1]
    pages_home = pages_req // seq_count
    positions = pages_home * page_len
    per_peer = pages_dev // devices
    groups = H // KVH
    query_cols = w_query.shape[1]
    key_cols = w_key.shape[1]
    all_requests = jnp.arange(request_total, dtype=jnp.int32)
    hits = owner[None, :] == all_requests[:, None]
    slot_request = jnp.sum(jnp.where(hits, all_requests[None, :], 0), axis=1)
    slot_lengths = jnp.sum(jnp.where(hits, cache_lengths[None, :], 0), axis=1)
    my_lengths = lax.dynamic_slice_in_dim(slot_lengths, req_index * local_reqs, local_reqs)
    slot_pages = page_table[slot_request]
    home_table = jnp.transpose(
        slot_pages.reshape(req_count, local_reqs, seq_count, pages_home), (0, 2, 1, 3)
    ).reshape(devices, local_reqs * pages_home)
    my_home = lax.dynamic_slice_in_dim(home_table, device_index, 1, axis=0).reshape(-1)
    arrival_src = my_home // pages_dev
    held_here = (home_table // pages_dev) == device_index
    send_pick = jnp.sum(jnp.where(held_here, home_table % pages_dev, 0), axis=1)
    tokens_wide = new_tokens.astype(jnp.float32)
    square_mean = jnp.mean(tokens_wide * tokens_wide, axis=-1, keepdims=True)
    normed = (tokens_wide * lax.rsqrt(square_mean + NORM_EPS) * norm_gain).astype(jnp.bfloat16)
    new_index = jnp.arange(new_count, dtype=jnp.int32)
    def shift(value, places):
        if places % req_count == 0:
            return value
        pairs = [(i, (i + places) % req_count) for i in range(req_count)]
        return lax.ppermute(value, "req", pairs)

    row_block = jnp.concatenate([shift(normed, k) for k in range(req_count)], axis=0)
    outgoing = jnp.stack([pool_keys[send_pick], pool_values[send_pick]], axis=1)
    outgoing = outgoing.reshape(devices, per_peer, 2, page_len, kv_width)
    outgoing, row_block = lax.optimization_barrier((outgoing, row_block))
    incoming = lax.all_to_all(outgoing, ("req", "seq"), split_axis=0, concat_axis=0, tiled=True)
    row_count = row_block.shape[0]
    flat_rows = row_block.reshape(row_count * new_count, model_width)
    row_group = (req_index - jnp.arange(req_count, dtype=jnp.int32)) % req_count
    row_lengths = jnp.take(slot_lengths.reshape(req_count, local_reqs), row_group, axis=0).reshape(-1)
    places = row_lengths[:, None] + new_index[None, :]
    queries_now = jnp.dot(flat_rows, w_query, preferred_element_type=jnp.float32).reshape(
        row_count, new_count, query_cols // HD, HD
    )
    keys_now = jnp.dot(flat_rows, w_key, preferred_element_type=jnp.float32).reshape(
        row_count, new_count, key_cols // HD, HD
    )
    values_now = jnp.dot(flat_rows, w_value, preferred_element_type=jnp.float32).reshape(
        row_count, new_count, key_cols
    )
    queries_now = rotate(queries_now, places).reshape(row_count, new_count, query_cols)
    keys_now = rotate(keys_now, places).reshape(row_count, new_count, key_cols)
    projected = jnp.concatenate([queries_now, keys_now, values_now], axis=-1).astype(jnp.bfloat16)
    projected = projected.reshape(req_count, local_reqs, new_count, query_cols + 2 * key_cols)
    by_shift = jnp.stack([shift(projected[k], -k) for k in range(req_count)], axis=0)
    source_block = (jnp.arange(req_count, dtype=jnp.int32) - req_index) % req_count
    owned_rows = jnp.take(by_shift, source_block, axis=0)
    owned_rows = jnp.transpose(owned_rows, (1, 2, 0, 3))
    queries = owned_rows[..., :query_cols].reshape(local_reqs, new_count, KVH, groups, HD)
    fresh_keys = owned_rows[..., query_cols : query_cols + key_cols].reshape(
        local_reqs, new_count, KVH, HD
    )
    fresh_values = owned_rows[..., query_cols + key_cols :].reshape(local_reqs, new_count, KVH, HD)
    score_scale = 1.0 / math.sqrt(HD)
    kernel_queries = jnp.transpose(queries, (0, 2, 4, 3, 1)).reshape(
        local_reqs, KVH, HD, groups * new_count
    )
    keys_out, values_out, gathered_sum, row_peak, row_mass = arrive_and_attend(
        arrival_src,
        my_lengths,
        (seq_index * positions).reshape(1).astype(jnp.int32),
        incoming.reshape(pages_dev, 2, page_len, kv_width),
        kernel_queries,
        fresh_keys.reshape(local_reqs, new_count, kv_width),
        fresh_values.reshape(local_reqs, new_count, kv_width),
        score_scale,
    )
    gathered_sum = gathered_sum.reshape(local_reqs, KVH, groups, new_count, HD)
    row_peak = row_peak.reshape(local_reqs, KVH, groups, new_count)
    row_mass = row_mass.reshape(local_reqs, KVH, groups, new_count)
    def pack(total, peak, mass):
        stat_rows = peak.size // HD
        return jnp.concatenate(
            [total.reshape(-1, HD), peak.reshape(stat_rows, HD), mass.reshape(stat_rows, HD)], axis=0
        )

    def unpack(packed, total, peak, mass):
        stat_rows = peak.size // HD
        return (
            packed[: total.size // HD].reshape(total.shape),
            packed[total.size // HD : -stat_rows].reshape(peak.shape),
            packed[-stat_rows:].reshape(mass.shape),
        )

    def merge(step, total, peak, mass):
        pairs = [(i, i ^ step) for i in range(seq_count)]
        other = lax.ppermute(pack(total, peak, mass), "seq", pairs)
        peer_sum, peer_peak, peer_mass = unpack(other, total, peak, mass)
        upper = (seq_index & step) != 0
        peak_lo = jnp.where(upper, peer_peak, peak)
        peak_hi = jnp.where(upper, peak, peer_peak)
        mass_lo = jnp.where(upper, peer_mass, mass)
        mass_hi = jnp.where(upper, mass, peer_mass)
        sum_lo = jnp.where(upper, peer_sum, total)
        sum_hi = jnp.where(upper, total, peer_sum)
        merged_peak = jnp.maximum(peak_lo, peak_hi)
        scale_lo = jnp.exp(peak_lo - merged_peak)
        scale_hi = jnp.exp(peak_hi - merged_peak)
        return (
            sum_lo * scale_lo[..., None] + sum_hi * scale_hi[..., None],
            merged_peak,
            mass_lo * scale_lo + mass_hi * scale_hi,
        )

    gathered_sum, row_peak, row_mass = merge(1, gathered_sum, row_peak, row_mass)
    half = local_reqs // 2
    core = seq_index % 2
    mine = tuple(
        lax.dynamic_slice_in_dim(x, core * half, half, axis=0)
        for x in (gathered_sum, row_peak, row_mass)
    )
    step = 2
    while step < seq_count:
        mine = merge(step, *mine)
        step *= 2
    mine_packed = pack(*mine)
    other_packed = lax.ppermute(mine_packed, "seq", [(i, i ^ 1) for i in range(seq_count)])
    first_half = unpack(jnp.where(core == 0, mine_packed, other_packed), *mine)
    second_half = unpack(jnp.where(core == 0, other_packed, mine_packed), *mine)
    gathered_sum, row_peak, row_mass = (
        jnp.concatenate([p, q], axis=0) for p, q in zip(first_half, second_half)
    )
    own_scores = (
        jnp.einsum("rtkgd,rskd->rkgts", queries, fresh_keys, preferred_element_type=jnp.float32)
        * score_scale
    )
    causal = new_index[None, :] <= new_index[:, None]
    own_scores = jnp.where(causal, own_scores, MASKED)
    final_peak = jnp.maximum(row_peak, jnp.max(own_scores, axis=-1))
    carried = jnp.exp(row_peak - final_peak)
    own_weights = jnp.where(causal, jnp.exp(own_scores - final_peak[..., None]), 0.0)
    row_mass = row_mass * carried + jnp.sum(own_weights, axis=-1)
    gathered_sum = gathered_sum * carried[..., None] + jnp.einsum(
        "rkgts,rskd->rkgtd",
        own_weights.astype(jnp.bfloat16),
        fresh_values,
        preferred_element_type=jnp.float32,
    )
    attended = (
        jnp.transpose(gathered_sum / row_mass[..., None], (0, 3, 1, 2, 4))
        .reshape(local_reqs, new_count, KVH * groups * HD)
        .astype(jnp.bfloat16)
    )
    head_cols = attended.shape[-1] // req_count
    headed = jnp.concatenate(
        [
            shift(
                lax.dynamic_slice_in_dim(
                    attended, ((req_index + k) % req_count) * head_cols, head_cols, axis=2
                ),
                k,
            )
            for k in range(req_count)
        ],
        axis=0,
    )
    partial_out = (
        jnp.dot(headed.reshape(row_count * new_count, -1), w_out, preferred_element_type=jnp.float32)
        .reshape(req_count, local_reqs, new_count, model_width)
        .astype(jnp.bfloat16)
    )
    projected_out = shift(partial_out[0], 0).astype(jnp.float32)
    for k in range(1, req_count):
        projected_out = projected_out + shift(partial_out[k], -k).astype(jnp.float32)
    out_hidden = (tokens_wide + projected_out).astype(jnp.bfloat16)
    return (out_hidden, keys_out, values_out)


def solution(mesh):
    return jax.shard_map(
        shards,
        mesh=mesh,
        in_specs=(
            P("req", None, None),
            P(),
            P(None, "req"),
            P(None, "req"),
            P(None, "req"),
            P("req", None),
            P(("req", "seq"), None, None),
            P(("req", "seq"), None, None),
            P(),
            P(),
            P(),
        ),
        out_specs=(P("req", None, None), P("req", "seq", None), P("req", "seq", None)),
        check_vma=False,
    )
```

```python
import functools
import math

import jax
import jax.numpy as jnp
from jax import lax
from jax.experimental import pallas as pl
from jax.experimental.pallas import tpu as pltpu
from jax.sharding import PartitionSpec as P

H = 16
KVH = 8
HD = 128


NORM_EPS = 1e-05
ROPE_BASE = 1000000.0
MASKED = -1e30


def rotate(values, places):
    half_dim = values.shape[-1] // 2
    steps_up = jnp.arange(half_dim, dtype=jnp.float32) * (2.0 / values.shape[-1])
    inverse = ROPE_BASE ** (-steps_up)
    angles = places.astype(jnp.float32)[..., None] * inverse
    cosine = jnp.cos(angles)[..., None, :]
    sine_part = jnp.sin(angles)[..., None, :]
    first_half = values[..., :half_dim]
    second_half = values[..., half_dim:]
    return jnp.concatenate(
        [
            first_half * cosine - second_half * sine_part,
            second_half * cosine + first_half * sine_part,
        ],
        axis=-1,
    )


def _arrive_kernel(
    lengths_ref, base_ref, arrived_ref, q_ref, fk_ref, fv_ref,
    keys_out_ref, values_out_ref, acc_ref, peak_ref, mass_ref, *, scale
):
    r = pl.program_id(0)
    pages = arrived_ref.shape[1]
    page_len = arrived_ref.shape[3]
    positions = pages * page_len
    heads = q_ref.shape[1]
    head_dim = q_ref.shape[3]
    new_count = fk_ref.shape[1]
    outs = (keys_out_ref, values_out_ref)
    keys_out_ref[0] = arrived_ref[0, :, 0]
    values_out_ref[0] = arrived_ref[0, :, 1]
    length = lengths_ref[r]
    base = base_ref[0]
    spots = base + lax.broadcasted_iota(jnp.int32, (1, positions), 1)
    live = spots < length
    for kh in range(heads):
        cols = pl.ds(kh * head_dim, head_dim)
        keys_h = arrived_ref[0, :, 0, :, cols].reshape(positions, head_dim)
        values_h = arrived_ref[0, :, 1, :, cols].reshape(positions, head_dim)
        query_h = q_ref[0, kh]
        scores = lax.dot_general(
            query_h, keys_h, (((1,), (1,)), ((), ())), preferred_element_type=jnp.float32
        ) * scale
        scores = jnp.where(live, scores, MASKED)
        peak = jnp.max(scores, axis=1, keepdims=True)
        weights = jnp.where(live, jnp.exp(scores - peak), 0.0)
        peak_ref[0, kh] = peak
        mass_ref[0, kh] = jnp.sum(weights, axis=1, keepdims=True)
        acc_ref[0, kh] = jnp.dot(
            weights.astype(jnp.bfloat16), values_h, preferred_element_type=jnp.float32
        )
    first = length - base
    page0 = first // page_len
    row_ids = lax.broadcasted_iota(jnp.int32, (page_len, 1), 0)
    fresh = (fk_ref[0], fv_ref[0])
    for page in (page0, page0 + 1):
        @pl.when(jnp.logical_and(page >= 0, page < pages))
        def _():
            for half in range(2):
                block = outs[half][0, page]
                for t in range(new_count):
                    hit = row_ids == first + t - page * page_len
                    block = jnp.where(hit, fresh[half][t : t + 1, :], block)
                outs[half][0, page] = block


def arrive_and_attend(arrival_src, lengths, base, incoming, queries, fresh_k, fresh_v, scale):
    local_reqs, new_count, kv_width = fresh_k.shape
    _, heads, rows, head_dim = queries.shape
    page_len = incoming.shape[2]
    pages = arrival_src.shape[0] // local_reqs
    positions = pages * page_len
    arrived = incoming[arrival_src].reshape(local_reqs, pages, 2, page_len, kv_width)
    grid_spec = pltpu.PrefetchScalarGridSpec(
        num_scalar_prefetch=2,
        grid=(local_reqs,),
        in_specs=[
            pl.BlockSpec((1, pages, 2, page_len, kv_width), lambda r, *_: (r, 0, 0, 0, 0)),
            pl.BlockSpec((1, heads, rows, head_dim), lambda r, *_: (r, 0, 0, 0)),
            pl.BlockSpec((1, new_count, kv_width), lambda r, *_: (r, 0, 0)),
            pl.BlockSpec((1, new_count, kv_width), lambda r, *_: (r, 0, 0)),
        ],
        out_specs=[
            pl.BlockSpec((1, pages, page_len, kv_width), lambda r, *_: (r, 0, 0, 0)),
            pl.BlockSpec((1, pages, page_len, kv_width), lambda r, *_: (r, 0, 0, 0)),
            pl.BlockSpec((1, heads, rows, head_dim), lambda r, *_: (r, 0, 0, 0)),
            pl.BlockSpec((1, heads, rows, 1), lambda r, *_: (r, 0, 0, 0)),
            pl.BlockSpec((1, heads, rows, 1), lambda r, *_: (r, 0, 0, 0)),
        ],
    )
    cache_bytes = 2 * local_reqs * positions * kv_width * 2
    keys_out, values_out, acc, peak, mass = pl.pallas_call(
        functools.partial(_arrive_kernel, scale=scale),
        out_shape=[
            jax.ShapeDtypeStruct((local_reqs, pages, page_len, kv_width), jnp.bfloat16),
            jax.ShapeDtypeStruct((local_reqs, pages, page_len, kv_width), jnp.bfloat16),
            jax.ShapeDtypeStruct((local_reqs, heads, rows, head_dim), jnp.float32),
            jax.ShapeDtypeStruct((local_reqs, heads, rows, 1), jnp.float32),
            jax.ShapeDtypeStruct((local_reqs, heads, rows, 1), jnp.float32),
        ],
        grid_spec=grid_spec,
        compiler_params=pltpu.CompilerParams(
            dimension_semantics=("arbitrary",), vmem_limit_bytes=48 * 1024 * 1024
        ),
        cost_estimate=pl.CostEstimate(
            flops=4 * local_reqs * heads * rows * positions * head_dim,
            transcendentals=local_reqs * heads * rows * positions,
            bytes_accessed=2 * cache_bytes,
        ),
        name="arrive_and_attend",
    )(lengths, base, arrived, queries, fresh_k, fresh_v)
    keys_out = keys_out.reshape(local_reqs, positions, kv_width)
    values_out = values_out.reshape(local_reqs, positions, kv_width)
    return keys_out, values_out, acc, peak, mass


def shards(
    new_tokens,
    norm_gain,
    w_query,
    w_key,
    w_value,
    w_out,
    pool_keys,
    pool_values,
    cache_lengths,
    owner,
    page_table,
):
    req_count = lax.axis_size("req")
    seq_count = lax.axis_size("seq")
    devices = req_count * seq_count
    req_index = lax.axis_index("req")
    seq_index = lax.axis_index("seq")
    device_index = req_index * seq_count + seq_index
    local_reqs, new_count, model_width = new_tokens.shape
    request_total = owner.shape[0]
    pages_dev, page_len, kv_width = pool_keys.shape
    pages_req = page_table.shape[1]
    pages_home = pages_req // seq_count
    positions = pages_home * page_len
    per_peer = pages_dev // devices
    groups = H // KVH
    query_cols = w_query.shape[1]
    key_cols = w_key.shape[1]
    all_requests = jnp.arange(request_total, dtype=jnp.int32)
    hits = owner[None, :] == all_requests[:, None]
    slot_request = jnp.sum(jnp.where(hits, all_requests[None, :], 0), axis=1)
    slot_lengths = jnp.sum(jnp.where(hits, cache_lengths[None, :], 0), axis=1)
    my_lengths = lax.dynamic_slice_in_dim(slot_lengths, req_index * local_reqs, local_reqs)
    slot_pages = page_table[slot_request]
    home_table = jnp.transpose(
        slot_pages.reshape(req_count, local_reqs, seq_count, pages_home), (0, 2, 1, 3)
    ).reshape(devices, local_reqs * pages_home)
    my_home = lax.dynamic_slice_in_dim(home_table, device_index, 1, axis=0).reshape(-1)
    arrival_src = my_home // pages_dev
    held_here = (home_table // pages_dev) == device_index
    send_pick = jnp.sum(jnp.where(held_here, home_table % pages_dev, 0), axis=1)
    tokens_wide = new_tokens.astype(jnp.float32)
    square_mean = jnp.mean(tokens_wide * tokens_wide, axis=-1, keepdims=True)
    normed = (tokens_wide * lax.rsqrt(square_mean + NORM_EPS) * norm_gain).astype(jnp.bfloat16)
    new_index = jnp.arange(new_count, dtype=jnp.int32)
    def shift(value, places):
        if places % req_count == 0:
            return value
        pairs = [(i, (i + places) % req_count) for i in range(req_count)]
        return lax.ppermute(value, "req", pairs)

    row_block = jnp.concatenate([shift(normed, k) for k in range(req_count)], axis=0)
    outgoing = jnp.stack([pool_keys[send_pick], pool_values[send_pick]], axis=1)
    outgoing = outgoing.reshape(devices, per_peer, 2, page_len, kv_width)
    outgoing, row_block = lax.optimization_barrier((outgoing, row_block))
    incoming = lax.all_to_all(outgoing, ("req", "seq"), split_axis=0, concat_axis=0, tiled=True)
    row_count = row_block.shape[0]
    flat_rows = row_block.reshape(row_count * new_count, model_width)
    row_group = (req_index - jnp.arange(req_count, dtype=jnp.int32)) % req_count
    row_lengths = jnp.take(slot_lengths.reshape(req_count, local_reqs), row_group, axis=0).reshape(-1)
    places = row_lengths[:, None] + new_index[None, :]
    queries_now = jnp.dot(flat_rows, w_query, preferred_element_type=jnp.float32).reshape(
        row_count, new_count, query_cols // HD, HD
    )
    keys_now = jnp.dot(flat_rows, w_key, preferred_element_type=jnp.float32).reshape(
        row_count, new_count, key_cols // HD, HD
    )
    values_now = jnp.dot(flat_rows, w_value, preferred_element_type=jnp.float32).reshape(
        row_count, new_count, key_cols
    )
    queries_now = rotate(queries_now, places).reshape(row_count, new_count, query_cols)
    keys_now = rotate(keys_now, places).reshape(row_count, new_count, key_cols)
    projected = jnp.concatenate([queries_now, keys_now, values_now], axis=-1).astype(jnp.bfloat16)
    projected = projected.reshape(req_count, local_reqs, new_count, query_cols + 2 * key_cols)
    by_shift = jnp.stack([shift(projected[k], -k) for k in range(req_count)], axis=0)
    source_block = (jnp.arange(req_count, dtype=jnp.int32) - req_index) % req_count
    owned_rows = jnp.take(by_shift, source_block, axis=0)
    owned_rows = jnp.transpose(owned_rows, (1, 2, 0, 3))
    queries = owned_rows[..., :query_cols].reshape(local_reqs, new_count, KVH, groups, HD)
    fresh_keys = owned_rows[..., query_cols : query_cols + key_cols].reshape(
        local_reqs, new_count, KVH, HD
    )
    fresh_values = owned_rows[..., query_cols + key_cols :].reshape(local_reqs, new_count, KVH, HD)
    score_scale = 1.0 / math.sqrt(HD)
    kernel_queries = jnp.transpose(queries, (0, 2, 3, 1, 4)).reshape(
        local_reqs, KVH, groups * new_count, HD
    )
    keys_out, values_out, gathered_sum, row_peak, row_mass = arrive_and_attend(
        arrival_src,
        my_lengths,
        (seq_index * positions).reshape(1).astype(jnp.int32),
        incoming.reshape(pages_dev, 2, page_len, kv_width),
        kernel_queries,
        fresh_keys.reshape(local_reqs, new_count, kv_width),
        fresh_values.reshape(local_reqs, new_count, kv_width),
        score_scale,
    )
    gathered_sum = gathered_sum.reshape(local_reqs, KVH, groups, new_count, HD)
    row_peak = row_peak.reshape(local_reqs, KVH, groups, new_count)
    row_mass = row_mass.reshape(local_reqs, KVH, groups, new_count)
    def pack(total, peak, mass):
        stat_rows = peak.size // HD
        return jnp.concatenate(
            [total.reshape(-1, HD), peak.reshape(stat_rows, HD), mass.reshape(stat_rows, HD)], axis=0
        )

    def unpack(packed, total, peak, mass):
        stat_rows = peak.size // HD
        return (
            packed[: total.size // HD].reshape(total.shape),
            packed[total.size // HD : -stat_rows].reshape(peak.shape),
            packed[-stat_rows:].reshape(mass.shape),
        )

    def merge(step, total, peak, mass):
        pairs = [(i, i ^ step) for i in range(seq_count)]
        other = lax.ppermute(pack(total, peak, mass), "seq", pairs)
        peer_sum, peer_peak, peer_mass = unpack(other, total, peak, mass)
        upper = (seq_index & step) != 0
        peak_lo = jnp.where(upper, peer_peak, peak)
        peak_hi = jnp.where(upper, peak, peer_peak)
        mass_lo = jnp.where(upper, peer_mass, mass)
        mass_hi = jnp.where(upper, mass, peer_mass)
        sum_lo = jnp.where(upper, peer_sum, total)
        sum_hi = jnp.where(upper, total, peer_sum)
        merged_peak = jnp.maximum(peak_lo, peak_hi)
        scale_lo = jnp.exp(peak_lo - merged_peak)
        scale_hi = jnp.exp(peak_hi - merged_peak)
        return (
            sum_lo * scale_lo[..., None] + sum_hi * scale_hi[..., None],
            merged_peak,
            mass_lo * scale_lo + mass_hi * scale_hi,
        )

    gathered_sum, row_peak, row_mass = merge(1, gathered_sum, row_peak, row_mass)
    half = local_reqs // 2
    core = seq_index % 2
    mine = tuple(
        lax.dynamic_slice_in_dim(x, core * half, half, axis=0)
        for x in (gathered_sum, row_peak, row_mass)
    )
    step = 2
    while step < seq_count:
        mine = merge(step, *mine)
        step *= 2
    mine_packed = pack(*mine)
    other_packed = lax.ppermute(mine_packed, "seq", [(i, i ^ 1) for i in range(seq_count)])
    first_half = unpack(jnp.where(core == 0, mine_packed, other_packed), *mine)
    second_half = unpack(jnp.where(core == 0, other_packed, mine_packed), *mine)
    gathered_sum, row_peak, row_mass = (
        jnp.concatenate([p, q], axis=0) for p, q in zip(first_half, second_half)
    )
    own_scores = (
        jnp.einsum("rtkgd,rskd->rkgts", queries, fresh_keys, preferred_element_type=jnp.float32)
        * score_scale
    )
    causal = new_index[None, :] <= new_index[:, None]
    own_scores = jnp.where(causal, own_scores, MASKED)
    final_peak = jnp.maximum(row_peak, jnp.max(own_scores, axis=-1))
    carried = jnp.exp(row_peak - final_peak)
    own_weights = jnp.where(causal, jnp.exp(own_scores - final_peak[..., None]), 0.0)
    row_mass = row_mass * carried + jnp.sum(own_weights, axis=-1)
    gathered_sum = gathered_sum * carried[..., None] + jnp.einsum(
        "rkgts,rskd->rkgtd",
        own_weights.astype(jnp.bfloat16),
        fresh_values,
        preferred_element_type=jnp.float32,
    )
    attended = (
        jnp.transpose(gathered_sum / row_mass[..., None], (0, 3, 1, 2, 4))
        .reshape(local_reqs, new_count, KVH * groups * HD)
        .astype(jnp.bfloat16)
    )
    head_cols = attended.shape[-1] // req_count
    headed = jnp.concatenate(
        [
            shift(
                lax.dynamic_slice_in_dim(
                    attended, ((req_index + k) % req_count) * head_cols, head_cols, axis=2
                ),
                k,
            )
            for k in range(req_count)
        ],
        axis=0,
    )
    partial_out = (
        jnp.dot(headed.reshape(row_count * new_count, -1), w_out, preferred_element_type=jnp.float32)
        .reshape(req_count, local_reqs, new_count, model_width)
        .astype(jnp.bfloat16)
    )
    projected_out = shift(partial_out[0], 0).astype(jnp.float32)
    for k in range(1, req_count):
        projected_out = projected_out + shift(partial_out[k], -k).astype(jnp.float32)
    out_hidden = (tokens_wide + projected_out).astype(jnp.bfloat16)
    return (out_hidden, keys_out, values_out)


def solution(mesh):
    return jax.shard_map(
        shards,
        mesh=mesh,
        in_specs=(
            P("req", None, None),
            P(),
            P(None, "req"),
            P(None, "req"),
            P(None, "req"),
            P("req", None),
            P(("req", "seq"), None, None),
            P(("req", "seq"), None, None),
            P(),
            P(),
            P(),
        ),
        out_specs=(P("req", None, None), P("req", "seq", None), P("req", "seq", None)),
        check_vma=False,
    )
```

```python
import functools
import math

import jax
import jax.numpy as jnp
from jax import lax
from jax.experimental import pallas as pl
from jax.experimental.pallas import tpu as pltpu
from jax.sharding import PartitionSpec as P

H = 16
KVH = 8
HD = 128


NORM_EPS = 1e-05
ROPE_BASE = 1000000.0
MASKED = -1e30


def rotate(values, places):
    half_dim = values.shape[-1] // 2
    steps_up = jnp.arange(half_dim, dtype=jnp.float32) * (2.0 / values.shape[-1])
    inverse = ROPE_BASE ** (-steps_up)
    angles = places.astype(jnp.float32)[..., None] * inverse
    cosine = jnp.cos(angles)[..., None, :]
    sine_part = jnp.sin(angles)[..., None, :]
    first_half = values[..., :half_dim]
    second_half = values[..., half_dim:]
    return jnp.concatenate(
        [
            first_half * cosine - second_half * sine_part,
            second_half * cosine + first_half * sine_part,
        ],
        axis=-1,
    )


def _arrive_kernel(
    lengths_ref, base_ref, q_ref, fk_ref, fv_ref, keys_in_ref, values_in_ref,
    keys_out_ref, values_out_ref, acc_ref, peak_ref, mass_ref,
    buf, tiles, in_sem, tile_sem, *, scale
):
    r = pl.program_id(0)
    n = pl.num_programs(0)
    slot = r % 2
    positions = buf.shape[2]
    page_len = tiles.shape[2]
    pages = positions // page_len
    heads = q_ref.shape[1]
    head_dim = q_ref.shape[3]
    new_count = fk_ref.shape[1]
    ins = (keys_in_ref, values_in_ref)
    outs = (keys_out_ref, values_out_ref)

    def block_copy(req, s, half):
        return pltpu.make_async_copy(ins[half].at[req], buf.at[s, half], in_sem.at[s, half])

    @pl.when(r == 0)
    def _():
        for half in range(2):
            block_copy(0, 0, half).start()

    for half in range(2):
        block_copy(r, slot, half).wait()

    @pl.when(r + 1 < n)
    def _():
        for half in range(2):
            block_copy(r + 1, 1 - slot, half).start()

    length = lengths_ref[r]
    base = base_ref[0]
    spots = base + lax.broadcasted_iota(jnp.int32, (1, positions), 1)
    live = spots < length
    for kh in range(heads):
        cols = pl.ds(kh * head_dim, head_dim)
        keys_h = buf[slot, 0, :, cols]
        values_h = buf[slot, 1, :, cols]
        query_h = q_ref[0, kh]
        scores = lax.dot_general(
            query_h, keys_h, (((1,), (1,)), ((), ())), preferred_element_type=jnp.float32
        ) * scale
        scores = jnp.where(live, scores, MASKED)
        peak = jnp.max(scores, axis=1, keepdims=True)
        weights = jnp.where(live, jnp.exp(scores - peak), 0.0)
        peak_ref[0, kh] = peak
        mass_ref[0, kh] = jnp.sum(weights, axis=1, keepdims=True)
        acc_ref[0, kh] = jnp.dot(
            weights.astype(jnp.bfloat16), values_h, preferred_element_type=jnp.float32
        )
    first = length - base
    page0 = first // page_len
    row_ids = lax.broadcasted_iota(jnp.int32, (page_len, 1), 0)
    fresh = (fk_ref[0], fv_ref[0])
    for j, page in enumerate((page0, page0 + 1)):
        @pl.when(jnp.logical_and(page >= 0, page < pages))
        def _():
            rows = pl.ds(pl.multiple_of(page * page_len, page_len), page_len)
            copies = []
            for half in range(2):
                block = buf[slot, half, rows, :]
                for t in range(new_count):
                    hit = row_ids == first + t - page * page_len
                    block = jnp.where(hit, fresh[half][t : t + 1, :], block)
                tiles[j, half] = block
                copy = pltpu.make_async_copy(
                    tiles.at[j, half], outs[half].at[r, rows], tile_sem.at[j, half]
                )
                copy.start()
                copies.append(copy)
            for copy in copies:
                copy.wait()


def arrive_and_attend(arrival_src, lengths, base, incoming, queries, fresh_k, fresh_v, scale):
    local_reqs, new_count, kv_width = fresh_k.shape
    _, heads, rows, head_dim = queries.shape
    page_len = incoming.shape[2]
    pages = arrival_src.shape[0] // local_reqs
    positions = pages * page_len
    cache_k = incoming[arrival_src, 0].reshape(local_reqs, positions, kv_width)
    cache_v = incoming[arrival_src, 1].reshape(local_reqs, positions, kv_width)
    grid_spec = pltpu.PrefetchScalarGridSpec(
        num_scalar_prefetch=2,
        grid=(local_reqs,),
        in_specs=[
            pl.BlockSpec((1, heads, rows, head_dim), lambda r, *_: (r, 0, 0, 0)),
            pl.BlockSpec((1, new_count, kv_width), lambda r, *_: (r, 0, 0)),
            pl.BlockSpec((1, new_count, kv_width), lambda r, *_: (r, 0, 0)),
            pl.BlockSpec(memory_space=pl.ANY),
            pl.BlockSpec(memory_space=pl.ANY),
        ],
        out_specs=[
            pl.BlockSpec(memory_space=pl.ANY),
            pl.BlockSpec(memory_space=pl.ANY),
            pl.BlockSpec((1, heads, rows, head_dim), lambda r, *_: (r, 0, 0, 0)),
            pl.BlockSpec((1, heads, rows, 1), lambda r, *_: (r, 0, 0, 0)),
            pl.BlockSpec((1, heads, rows, 1), lambda r, *_: (r, 0, 0, 0)),
        ],
        scratch_shapes=[
            pltpu.VMEM((2, 2, positions, kv_width), jnp.bfloat16),
            pltpu.VMEM((2, 2, page_len, kv_width), jnp.bfloat16),
            pltpu.SemaphoreType.DMA((2, 2)),
            pltpu.SemaphoreType.DMA((2, 2)),
        ],
    )
    cache_bytes = 2 * local_reqs * positions * kv_width * 2
    return pl.pallas_call(
        functools.partial(_arrive_kernel, scale=scale),
        out_shape=[
            jax.ShapeDtypeStruct((local_reqs, positions, kv_width), jnp.bfloat16),
            jax.ShapeDtypeStruct((local_reqs, positions, kv_width), jnp.bfloat16),
            jax.ShapeDtypeStruct((local_reqs, heads, rows, head_dim), jnp.float32),
            jax.ShapeDtypeStruct((local_reqs, heads, rows, 1), jnp.float32),
            jax.ShapeDtypeStruct((local_reqs, heads, rows, 1), jnp.float32),
        ],
        grid_spec=grid_spec,
        input_output_aliases={5: 0, 6: 1},
        compiler_params=pltpu.CompilerParams(dimension_semantics=("arbitrary",)),
        cost_estimate=pl.CostEstimate(
            flops=4 * local_reqs * heads * rows * positions * head_dim,
            transcendentals=local_reqs * heads * rows * positions,
            bytes_accessed=cache_bytes,
        ),
        name="arrive_and_attend",
    )(lengths, base, queries, fresh_k, fresh_v, cache_k, cache_v)


def shards(
    new_tokens,
    norm_gain,
    w_query,
    w_key,
    w_value,
    w_out,
    pool_keys,
    pool_values,
    cache_lengths,
    owner,
    page_table,
):
    req_count = lax.axis_size("req")
    seq_count = lax.axis_size("seq")
    devices = req_count * seq_count
    req_index = lax.axis_index("req")
    seq_index = lax.axis_index("seq")
    device_index = req_index * seq_count + seq_index
    local_reqs, new_count, model_width = new_tokens.shape
    request_total = owner.shape[0]
    pages_dev, page_len, kv_width = pool_keys.shape
    pages_req = page_table.shape[1]
    pages_home = pages_req // seq_count
    positions = pages_home * page_len
    per_peer = pages_dev // devices
    groups = H // KVH
    query_cols = w_query.shape[1]
    key_cols = w_key.shape[1]
    all_requests = jnp.arange(request_total, dtype=jnp.int32)
    hits = owner[None, :] == all_requests[:, None]
    slot_request = jnp.sum(jnp.where(hits, all_requests[None, :], 0), axis=1)
    slot_lengths = jnp.sum(jnp.where(hits, cache_lengths[None, :], 0), axis=1)
    my_lengths = lax.dynamic_slice_in_dim(slot_lengths, req_index * local_reqs, local_reqs)
    slot_pages = page_table[slot_request]
    home_table = jnp.transpose(
        slot_pages.reshape(req_count, local_reqs, seq_count, pages_home), (0, 2, 1, 3)
    ).reshape(devices, local_reqs * pages_home)
    my_home = lax.dynamic_slice_in_dim(home_table, device_index, 1, axis=0).reshape(-1)
    arrival_src = my_home // pages_dev
    held_here = (home_table // pages_dev) == device_index
    send_pick = jnp.sum(jnp.where(held_here, home_table % pages_dev, 0), axis=1)
    tokens_wide = new_tokens.astype(jnp.float32)
    square_mean = jnp.mean(tokens_wide * tokens_wide, axis=-1, keepdims=True)
    normed = (tokens_wide * lax.rsqrt(square_mean + NORM_EPS) * norm_gain).astype(jnp.bfloat16)
    new_index = jnp.arange(new_count, dtype=jnp.int32)
    def shift(value, places):
        if places % req_count == 0:
            return value
        pairs = [(i, (i + places) % req_count) for i in range(req_count)]
        return lax.ppermute(value, "req", pairs)

    row_block = jnp.concatenate([shift(normed, k) for k in range(req_count)], axis=0)
    outgoing = jnp.stack([pool_keys[send_pick], pool_values[send_pick]], axis=1)
    outgoing = outgoing.reshape(devices, per_peer, 2, page_len, kv_width)
    outgoing, row_block = lax.optimization_barrier((outgoing, row_block))
    incoming = lax.all_to_all(outgoing, ("req", "seq"), split_axis=0, concat_axis=0, tiled=True)
    row_count = row_block.shape[0]
    flat_rows = row_block.reshape(row_count * new_count, model_width)
    row_group = (req_index - jnp.arange(req_count, dtype=jnp.int32)) % req_count
    row_lengths = jnp.take(slot_lengths.reshape(req_count, local_reqs), row_group, axis=0).reshape(-1)
    places = row_lengths[:, None] + new_index[None, :]
    queries_now = jnp.dot(flat_rows, w_query, preferred_element_type=jnp.float32).reshape(
        row_count, new_count, query_cols // HD, HD
    )
    keys_now = jnp.dot(flat_rows, w_key, preferred_element_type=jnp.float32).reshape(
        row_count, new_count, key_cols // HD, HD
    )
    values_now = jnp.dot(flat_rows, w_value, preferred_element_type=jnp.float32).reshape(
        row_count, new_count, key_cols
    )
    queries_now = rotate(queries_now, places).reshape(row_count, new_count, query_cols)
    keys_now = rotate(keys_now, places).reshape(row_count, new_count, key_cols)
    projected = jnp.concatenate([queries_now, keys_now, values_now], axis=-1).astype(jnp.bfloat16)
    projected = projected.reshape(req_count, local_reqs, new_count, query_cols + 2 * key_cols)
    by_shift = jnp.stack([shift(projected[k], -k) for k in range(req_count)], axis=0)
    source_block = (jnp.arange(req_count, dtype=jnp.int32) - req_index) % req_count
    owned_rows = jnp.take(by_shift, source_block, axis=0)
    owned_rows = jnp.transpose(owned_rows, (1, 2, 0, 3))
    queries = owned_rows[..., :query_cols].reshape(local_reqs, new_count, KVH, groups, HD)
    fresh_keys = owned_rows[..., query_cols : query_cols + key_cols].reshape(
        local_reqs, new_count, KVH, HD
    )
    fresh_values = owned_rows[..., query_cols + key_cols :].reshape(local_reqs, new_count, KVH, HD)
    score_scale = 1.0 / math.sqrt(HD)
    kernel_queries = jnp.transpose(queries, (0, 2, 3, 1, 4)).reshape(
        local_reqs, KVH, groups * new_count, HD
    )
    keys_out, values_out, gathered_sum, row_peak, row_mass = arrive_and_attend(
        arrival_src,
        my_lengths,
        (seq_index * positions).reshape(1).astype(jnp.int32),
        incoming.reshape(pages_dev, 2, page_len, kv_width),
        kernel_queries,
        fresh_keys.reshape(local_reqs, new_count, kv_width),
        fresh_values.reshape(local_reqs, new_count, kv_width),
        score_scale,
    )
    gathered_sum = gathered_sum.reshape(local_reqs, KVH, groups, new_count, HD)
    row_peak = row_peak.reshape(local_reqs, KVH, groups, new_count)
    row_mass = row_mass.reshape(local_reqs, KVH, groups, new_count)
    def pack(total, peak, mass):
        stat_rows = peak.size // HD
        return jnp.concatenate(
            [total.reshape(-1, HD), peak.reshape(stat_rows, HD), mass.reshape(stat_rows, HD)], axis=0
        )

    def unpack(packed, total, peak, mass):
        stat_rows = peak.size // HD
        return (
            packed[: total.size // HD].reshape(total.shape),
            packed[total.size // HD : -stat_rows].reshape(peak.shape),
            packed[-stat_rows:].reshape(mass.shape),
        )

    def merge(step, total, peak, mass):
        pairs = [(i, i ^ step) for i in range(seq_count)]
        other = lax.ppermute(pack(total, peak, mass), "seq", pairs)
        peer_sum, peer_peak, peer_mass = unpack(other, total, peak, mass)
        upper = (seq_index & step) != 0
        peak_lo = jnp.where(upper, peer_peak, peak)
        peak_hi = jnp.where(upper, peak, peer_peak)
        mass_lo = jnp.where(upper, peer_mass, mass)
        mass_hi = jnp.where(upper, mass, peer_mass)
        sum_lo = jnp.where(upper, peer_sum, total)
        sum_hi = jnp.where(upper, total, peer_sum)
        merged_peak = jnp.maximum(peak_lo, peak_hi)
        scale_lo = jnp.exp(peak_lo - merged_peak)
        scale_hi = jnp.exp(peak_hi - merged_peak)
        return (
            sum_lo * scale_lo[..., None] + sum_hi * scale_hi[..., None],
            merged_peak,
            mass_lo * scale_lo + mass_hi * scale_hi,
        )

    gathered_sum, row_peak, row_mass = merge(1, gathered_sum, row_peak, row_mass)
    half = local_reqs // 2
    core = seq_index % 2
    mine = tuple(
        lax.dynamic_slice_in_dim(x, core * half, half, axis=0)
        for x in (gathered_sum, row_peak, row_mass)
    )
    step = 2
    while step < seq_count:
        mine = merge(step, *mine)
        step *= 2
    mine_packed = pack(*mine)
    other_packed = lax.ppermute(mine_packed, "seq", [(i, i ^ 1) for i in range(seq_count)])
    first_half = unpack(jnp.where(core == 0, mine_packed, other_packed), *mine)
    second_half = unpack(jnp.where(core == 0, other_packed, mine_packed), *mine)
    gathered_sum, row_peak, row_mass = (
        jnp.concatenate([p, q], axis=0) for p, q in zip(first_half, second_half)
    )
    own_scores = (
        jnp.einsum("rtkgd,rskd->rkgts", queries, fresh_keys, preferred_element_type=jnp.float32)
        * score_scale
    )
    causal = new_index[None, :] <= new_index[:, None]
    own_scores = jnp.where(causal, own_scores, MASKED)
    final_peak = jnp.maximum(row_peak, jnp.max(own_scores, axis=-1))
    carried = jnp.exp(row_peak - final_peak)
    own_weights = jnp.where(causal, jnp.exp(own_scores - final_peak[..., None]), 0.0)
    row_mass = row_mass * carried + jnp.sum(own_weights, axis=-1)
    gathered_sum = gathered_sum * carried[..., None] + jnp.einsum(
        "rkgts,rskd->rkgtd",
        own_weights.astype(jnp.bfloat16),
        fresh_values,
        preferred_element_type=jnp.float32,
    )
    attended = (
        jnp.transpose(gathered_sum / row_mass[..., None], (0, 3, 1, 2, 4))
        .reshape(local_reqs, new_count, KVH * groups * HD)
        .astype(jnp.bfloat16)
    )
    head_cols = attended.shape[-1] // req_count
    headed = jnp.concatenate(
        [
            shift(
                lax.dynamic_slice_in_dim(
                    attended, ((req_index + k) % req_count) * head_cols, head_cols, axis=2
                ),
                k,
            )
            for k in range(req_count)
        ],
        axis=0,
    )
    partial_out = (
        jnp.dot(headed.reshape(row_count * new_count, -1), w_out, preferred_element_type=jnp.float32)
        .reshape(req_count, local_reqs, new_count, model_width)
        .astype(jnp.bfloat16)
    )
    projected_out = shift(partial_out[0], 0).astype(jnp.float32)
    for k in range(1, req_count):
        projected_out = projected_out + shift(partial_out[k], -k).astype(jnp.float32)
    out_hidden = (tokens_wide + projected_out).astype(jnp.bfloat16)
    return (out_hidden, keys_out, values_out)


def solution(mesh):
    return jax.shard_map(
        shards,
        mesh=mesh,
        in_specs=(
            P("req", None, None),
            P(),
            P(None, "req"),
            P(None, "req"),
            P(None, "req"),
            P("req", None),
            P(("req", "seq"), None, None),
            P(("req", "seq"), None, None),
            P(),
            P(),
            P(),
        ),
        out_specs=(P("req", None, None), P("req", "seq", None), P("req", "seq", None)),
        check_vma=False,
    )
```

```python
import functools
import math

import jax
import jax.numpy as jnp
from jax import lax
from jax.experimental import pallas as pl
from jax.experimental.pallas import tpu as pltpu
from jax.sharding import PartitionSpec as P

H = 16
KVH = 8
HD = 128


NORM_EPS = 1e-05
ROPE_BASE = 1000000.0
MASKED = -1e30


def rotate(values, places):
    half_dim = values.shape[-1] // 2
    steps_up = jnp.arange(half_dim, dtype=jnp.float32) * (2.0 / values.shape[-1])
    inverse = ROPE_BASE ** (-steps_up)
    angles = places.astype(jnp.float32)[..., None] * inverse
    cosine = jnp.cos(angles)[..., None, :]
    sine_part = jnp.sin(angles)[..., None, :]
    first_half = values[..., :half_dim]
    second_half = values[..., half_dim:]
    return jnp.concatenate(
        [
            first_half * cosine - second_half * sine_part,
            second_half * cosine + first_half * sine_part,
        ],
        axis=-1,
    )


def _arrive_kernel(
    lengths_ref, base_ref, arrived_ref, q_ref, fk_ref, fv_ref,
    keys_out_ref, values_out_ref, acc_ref, peak_ref, mass_ref, *, scale
):
    r = pl.program_id(0)
    pages = arrived_ref.shape[1]
    page_len = arrived_ref.shape[3]
    positions = pages * page_len
    heads = q_ref.shape[1]
    head_dim = q_ref.shape[2]
    new_count = fk_ref.shape[1]
    outs = (keys_out_ref, values_out_ref)
    keys_out_ref[0] = arrived_ref[0, :, 0]
    values_out_ref[0] = arrived_ref[0, :, 1]
    length = lengths_ref[r]
    base = base_ref[0]
    spots = base + lax.broadcasted_iota(jnp.int32, (positions, 1), 0)
    live = spots < length
    for kh in range(heads):
        cols = pl.ds(kh * head_dim, head_dim)
        keys_h = arrived_ref[0, :, 0, :, cols].reshape(positions, head_dim)
        values_h = arrived_ref[0, :, 1, :, cols].reshape(positions, head_dim)
        query_t = q_ref[0, kh]
        scores = jnp.dot(keys_h, query_t, preferred_element_type=jnp.float32) * scale
        scores = jnp.where(live, scores, MASKED)
        peak = jnp.max(scores, axis=0, keepdims=True)
        weights = jnp.where(live, jnp.exp(scores - peak), 0.0)
        peak_ref[0, kh] = peak
        mass_ref[0, kh] = jnp.sum(weights, axis=0, keepdims=True)
        acc_ref[0, kh] = lax.dot_general(
            weights.astype(jnp.bfloat16), values_h, (((0,), (0,)), ((), ())),
            preferred_element_type=jnp.float32,
        )
    first = length - base
    page0 = first // page_len
    row_ids = lax.broadcasted_iota(jnp.int32, (page_len, 1), 0)
    fresh = (fk_ref[0], fv_ref[0])
    for page in (page0, page0 + 1):
        @pl.when(jnp.logical_and(page >= 0, page < pages))
        def _():
            for half in range(2):
                block = outs[half][0, page]
                for t in range(new_count):
                    hit = row_ids == first + t - page * page_len
                    block = jnp.where(hit, fresh[half][t : t + 1, :], block)
                outs[half][0, page] = block


def arrive_and_attend(arrival_src, lengths, base, incoming, queries, fresh_k, fresh_v, scale):
    local_reqs, new_count, kv_width = fresh_k.shape
    _, heads, head_dim, rows = queries.shape
    page_len = incoming.shape[2]
    pages = arrival_src.shape[0] // local_reqs
    positions = pages * page_len
    arrived = incoming[arrival_src].reshape(local_reqs, pages, 2, page_len, kv_width)
    grid_spec = pltpu.PrefetchScalarGridSpec(
        num_scalar_prefetch=2,
        grid=(local_reqs,),
        in_specs=[
            pl.BlockSpec((1, pages, 2, page_len, kv_width), lambda r, *_: (r, 0, 0, 0, 0)),
            pl.BlockSpec((1, heads, head_dim, rows), lambda r, *_: (r, 0, 0, 0)),
            pl.BlockSpec((1, new_count, kv_width), lambda r, *_: (r, 0, 0)),
            pl.BlockSpec((1, new_count, kv_width), lambda r, *_: (r, 0, 0)),
        ],
        out_specs=[
            pl.BlockSpec((1, pages, page_len, kv_width), lambda r, *_: (r, 0, 0, 0)),
            pl.BlockSpec((1, pages, page_len, kv_width), lambda r, *_: (r, 0, 0, 0)),
            pl.BlockSpec((1, heads, rows, head_dim), lambda r, *_: (r, 0, 0, 0)),
            pl.BlockSpec((1, heads, 1, rows), lambda r, *_: (r, 0, 0, 0)),
            pl.BlockSpec((1, heads, 1, rows), lambda r, *_: (r, 0, 0, 0)),
        ],
    )
    cache_bytes = 2 * local_reqs * positions * kv_width * 2
    keys_out, values_out, acc, peak, mass = pl.pallas_call(
        functools.partial(_arrive_kernel, scale=scale),
        out_shape=[
            jax.ShapeDtypeStruct((local_reqs, pages, page_len, kv_width), jnp.bfloat16),
            jax.ShapeDtypeStruct((local_reqs, pages, page_len, kv_width), jnp.bfloat16),
            jax.ShapeDtypeStruct((local_reqs, heads, rows, head_dim), jnp.float32),
            jax.ShapeDtypeStruct((local_reqs, heads, 1, rows), jnp.float32),
            jax.ShapeDtypeStruct((local_reqs, heads, 1, rows), jnp.float32),
        ],
        grid_spec=grid_spec,
        compiler_params=pltpu.CompilerParams(
            dimension_semantics=("arbitrary",), vmem_limit_bytes=48 * 1024 * 1024
        ),
        cost_estimate=pl.CostEstimate(
            flops=4 * local_reqs * heads * rows * positions * head_dim,
            transcendentals=local_reqs * heads * rows * positions,
            bytes_accessed=2 * cache_bytes,
        ),
        name="arrive_and_attend",
    )(lengths, base, arrived, queries, fresh_k, fresh_v)
    keys_out = keys_out.reshape(local_reqs, positions, kv_width)
    values_out = values_out.reshape(local_reqs, positions, kv_width)
    return keys_out, values_out, acc, peak, mass


def shards(
    new_tokens,
    norm_gain,
    w_query,
    w_key,
    w_value,
    w_out,
    pool_keys,
    pool_values,
    cache_lengths,
    owner,
    page_table,
):
    req_count = lax.axis_size("req")
    seq_count = lax.axis_size("seq")
    devices = req_count * seq_count
    req_index = lax.axis_index("req")
    seq_index = lax.axis_index("seq")
    device_index = req_index * seq_count + seq_index
    local_reqs, new_count, model_width = new_tokens.shape
    request_total = owner.shape[0]
    pages_dev, page_len, kv_width = pool_keys.shape
    pages_req = page_table.shape[1]
    pages_home = pages_req // seq_count
    positions = pages_home * page_len
    per_peer = pages_dev // devices
    groups = H // KVH
    query_cols = w_query.shape[1]
    key_cols = w_key.shape[1]
    all_requests = jnp.arange(request_total, dtype=jnp.int32)
    hits = owner[None, :] == all_requests[:, None]
    slot_request = jnp.sum(jnp.where(hits, all_requests[None, :], 0), axis=1)
    slot_lengths = jnp.sum(jnp.where(hits, cache_lengths[None, :], 0), axis=1)
    my_lengths = lax.dynamic_slice_in_dim(slot_lengths, req_index * local_reqs, local_reqs)
    slot_pages = page_table[slot_request]
    home_table = jnp.transpose(
        slot_pages.reshape(req_count, local_reqs, seq_count, pages_home), (0, 2, 1, 3)
    ).reshape(devices, local_reqs * pages_home)
    my_home = lax.dynamic_slice_in_dim(home_table, device_index, 1, axis=0).reshape(-1)
    arrival_src = my_home // pages_dev
    held_here = (home_table // pages_dev) == device_index
    send_pick = jnp.sum(jnp.where(held_here, home_table % pages_dev, 0), axis=1)
    tokens_wide = new_tokens.astype(jnp.float32)
    square_mean = jnp.mean(tokens_wide * tokens_wide, axis=-1, keepdims=True)
    normed = (tokens_wide * lax.rsqrt(square_mean + NORM_EPS) * norm_gain).astype(jnp.bfloat16)
    new_index = jnp.arange(new_count, dtype=jnp.int32)
    def shift(value, places):
        if places % req_count == 0:
            return value
        pairs = [(i, (i + places) % req_count) for i in range(req_count)]
        return lax.ppermute(value, "req", pairs)

    row_block = jnp.concatenate([shift(normed, k) for k in range(req_count)], axis=0)
    outgoing = jnp.stack([pool_keys[send_pick], pool_values[send_pick]], axis=1)
    outgoing = outgoing.reshape(devices, per_peer, 2, page_len, kv_width)
    outgoing, row_block = lax.optimization_barrier((outgoing, row_block))
    incoming = lax.all_to_all(outgoing, ("req", "seq"), split_axis=0, concat_axis=0, tiled=True)
    row_count = row_block.shape[0]
    flat_rows = row_block.reshape(row_count * new_count, model_width)
    row_group = (req_index - jnp.arange(req_count, dtype=jnp.int32)) % req_count
    row_lengths = jnp.take(slot_lengths.reshape(req_count, local_reqs), row_group, axis=0).reshape(-1)
    places = row_lengths[:, None] + new_index[None, :]
    queries_now = jnp.dot(flat_rows, w_query, preferred_element_type=jnp.float32).reshape(
        row_count, new_count, query_cols // HD, HD
    )
    keys_now = jnp.dot(flat_rows, w_key, preferred_element_type=jnp.float32).reshape(
        row_count, new_count, key_cols // HD, HD
    )
    values_now = jnp.dot(flat_rows, w_value, preferred_element_type=jnp.float32).reshape(
        row_count, new_count, key_cols
    )
    queries_now = rotate(queries_now, places).reshape(row_count, new_count, query_cols)
    keys_now = rotate(keys_now, places).reshape(row_count, new_count, key_cols)
    projected = jnp.concatenate([queries_now, keys_now, values_now], axis=-1).astype(jnp.bfloat16)
    projected = projected.reshape(req_count, local_reqs, new_count, query_cols + 2 * key_cols)
    by_shift = jnp.stack([shift(projected[k], -k) for k in range(req_count)], axis=0)
    source_block = (jnp.arange(req_count, dtype=jnp.int32) - req_index) % req_count
    owned_rows = jnp.take(by_shift, source_block, axis=0)
    owned_rows = jnp.transpose(owned_rows, (1, 2, 0, 3))
    queries = owned_rows[..., :query_cols].reshape(local_reqs, new_count, KVH, groups, HD)
    fresh_keys = owned_rows[..., query_cols : query_cols + key_cols].reshape(
        local_reqs, new_count, KVH, HD
    )
    fresh_values = owned_rows[..., query_cols + key_cols :].reshape(local_reqs, new_count, KVH, HD)
    score_scale = 1.0 / math.sqrt(HD)
    kernel_queries = jnp.transpose(queries, (0, 2, 4, 3, 1)).reshape(
        local_reqs, KVH, HD, groups * new_count
    )
    keys_out, values_out, gathered_sum, row_peak, row_mass = arrive_and_attend(
        arrival_src,
        my_lengths,
        (seq_index * positions).reshape(1).astype(jnp.int32),
        incoming.reshape(pages_dev, 2, page_len, kv_width),
        kernel_queries,
        fresh_keys.reshape(local_reqs, new_count, kv_width),
        fresh_values.reshape(local_reqs, new_count, kv_width),
        score_scale,
    )
    gathered_sum = gathered_sum.reshape(local_reqs, KVH, groups, new_count, HD)
    row_peak = row_peak.reshape(local_reqs, KVH, groups, new_count)
    row_mass = row_mass.reshape(local_reqs, KVH, groups, new_count)
    def pack(total, peak, mass):
        stat_rows = peak.size // HD
        return jnp.concatenate(
            [total.reshape(-1, HD), peak.reshape(stat_rows, HD), mass.reshape(stat_rows, HD)], axis=0
        )

    def unpack(packed, total, peak, mass):
        stat_rows = peak.size // HD
        return (
            packed[: total.size // HD].reshape(total.shape),
            packed[total.size // HD : -stat_rows].reshape(peak.shape),
            packed[-stat_rows:].reshape(mass.shape),
        )

    def merge(step, total, peak, mass):
        pairs = [(i, i ^ step) for i in range(seq_count)]
        other = lax.ppermute(pack(total, peak, mass), "seq", pairs)
        peer_sum, peer_peak, peer_mass = unpack(other, total, peak, mass)
        upper = (seq_index & step) != 0
        peak_lo = jnp.where(upper, peer_peak, peak)
        peak_hi = jnp.where(upper, peak, peer_peak)
        mass_lo = jnp.where(upper, peer_mass, mass)
        mass_hi = jnp.where(upper, mass, peer_mass)
        sum_lo = jnp.where(upper, peer_sum, total)
        sum_hi = jnp.where(upper, total, peer_sum)
        merged_peak = jnp.maximum(peak_lo, peak_hi)
        scale_lo = jnp.exp(peak_lo - merged_peak)
        scale_hi = jnp.exp(peak_hi - merged_peak)
        return (
            sum_lo * scale_lo[..., None] + sum_hi * scale_hi[..., None],
            merged_peak,
            mass_lo * scale_lo + mass_hi * scale_hi,
        )

    gathered_sum, row_peak, row_mass = merge(1, gathered_sum, row_peak, row_mass)
    half = local_reqs // 2
    core = seq_index % 2
    mine = tuple(
        lax.dynamic_slice_in_dim(x, core * half, half, axis=0)
        for x in (gathered_sum, row_peak, row_mass)
    )
    step = 2
    while step < seq_count:
        mine = merge(step, *mine)
        step *= 2
    mine_packed = pack(*mine)
    other_packed = lax.ppermute(mine_packed, "seq", [(i, i ^ 1) for i in range(seq_count)])
    first_half = unpack(jnp.where(core == 0, mine_packed, other_packed), *mine)
    second_half = unpack(jnp.where(core == 0, other_packed, mine_packed), *mine)
    gathered_sum, row_peak, row_mass = (
        jnp.concatenate([p, q], axis=0) for p, q in zip(first_half, second_half)
    )
    own_scores = (
        jnp.einsum("rtkgd,rskd->rkgts", queries, fresh_keys, preferred_element_type=jnp.float32)
        * score_scale
    )
    causal = new_index[None, :] <= new_index[:, None]
    own_scores = jnp.where(causal, own_scores, MASKED)
    final_peak = jnp.maximum(row_peak, jnp.max(own_scores, axis=-1))
    carried = jnp.exp(row_peak - final_peak)
    own_weights = jnp.where(causal, jnp.exp(own_scores - final_peak[..., None]), 0.0)
    row_mass = row_mass * carried + jnp.sum(own_weights, axis=-1)
    gathered_sum = gathered_sum * carried[..., None] + jnp.einsum(
        "rkgts,rskd->rkgtd",
        own_weights.astype(jnp.bfloat16),
        fresh_values,
        preferred_element_type=jnp.float32,
    )
    attended = (
        jnp.transpose(gathered_sum / row_mass[..., None], (0, 3, 1, 2, 4))
        .reshape(local_reqs, new_count, KVH * groups * HD)
        .astype(jnp.bfloat16)
    )
    head_cols = attended.shape[-1] // req_count
    headed = jnp.concatenate(
        [
            shift(
                lax.dynamic_slice_in_dim(
                    attended, ((req_index + k) % req_count) * head_cols, head_cols, axis=2
                ),
                k,
            )
            for k in range(req_count)
        ],
        axis=0,
    )
    partial_out = (
        jnp.dot(headed.reshape(row_count * new_count, -1), w_out, preferred_element_type=jnp.float32)
        .reshape(req_count, local_reqs, new_count, model_width)
        .astype(jnp.bfloat16)
    )
    projected_out = shift(partial_out[0], 0).astype(jnp.float32)
    for k in range(1, req_count):
        projected_out = projected_out + shift(partial_out[k], -k).astype(jnp.float32)
    out_hidden = (tokens_wide + projected_out).astype(jnp.bfloat16)
    return (out_hidden, keys_out, values_out)


def solution(mesh):
    return jax.shard_map(
        shards,
        mesh=mesh,
        in_specs=(
            P("req", None, None),
            P(),
            P(None, "req"),
            P(None, "req"),
            P(None, "req"),
            P("req", None),
            P(("req", "seq"), None, None),
            P(("req", "seq"), None, None),
            P(),
            P(),
            P(),
        ),
        out_specs=(P("req", None, None), P("req", "seq", None), P("req", "seq", None)),
        check_vma=False,
    )
```

```python
import functools
import math

import jax
import jax.numpy as jnp
from jax import lax
from jax.experimental import pallas as pl
from jax.experimental.pallas import tpu as pltpu
from jax.sharding import PartitionSpec as P

H = 16
KVH = 8
HD = 128


NORM_EPS = 1e-05
ROPE_BASE = 1000000.0
MASKED = -1e30


def rotate(values, places):
    half_dim = values.shape[-1] // 2
    steps_up = jnp.arange(half_dim, dtype=jnp.float32) * (2.0 / values.shape[-1])
    inverse = ROPE_BASE ** (-steps_up)
    angles = places.astype(jnp.float32)[..., None] * inverse
    cosine = jnp.cos(angles)[..., None, :]
    sine_part = jnp.sin(angles)[..., None, :]
    first_half = values[..., :half_dim]
    second_half = values[..., half_dim:]
    return jnp.concatenate(
        [
            first_half * cosine - second_half * sine_part,
            second_half * cosine + first_half * sine_part,
        ],
        axis=-1,
    )


def _arrive_kernel(
    lengths_ref, base_ref, arrived_ref, q_ref, fk_ref, fv_ref,
    keys_out_ref, values_out_ref, acc_ref, peak_ref, mass_ref, *, scale
):
    r = pl.program_id(0)
    pages = arrived_ref.shape[1]
    page_len = arrived_ref.shape[3]
    positions = pages * page_len
    heads = acc_ref.shape[1]
    head_dim = acc_ref.shape[3]
    new_count = fk_ref.shape[1]
    outs = (keys_out_ref, values_out_ref)
    keys_out_ref[0] = arrived_ref[0, :, 0]
    values_out_ref[0] = arrived_ref[0, :, 1]
    length = lengths_ref[r]
    base = base_ref[0]
    spots = base + lax.broadcasted_iota(jnp.int32, (1, positions), 1)
    live = spots < length
    rows = q_ref.shape[1] // heads
    keys_all = arrived_ref[0, :, 0].reshape(positions, heads * head_dim)
    values_all = arrived_ref[0, :, 1].reshape(positions, heads * head_dim)
    scores = lax.dot_general(
        q_ref[0], keys_all, (((1,), (1,)), ((), ())), preferred_element_type=jnp.float32
    ) * scale
    scores = jnp.where(live, scores, MASKED)
    peak = jnp.max(scores, axis=1, keepdims=True)
    weights = jnp.where(live, jnp.exp(scores - peak), 0.0)
    mass = jnp.sum(weights, axis=1, keepdims=True)
    acc_all = jnp.dot(weights.astype(jnp.bfloat16), values_all, preferred_element_type=jnp.float32)
    for kh in range(heads):
        peak_ref[0, kh] = peak[kh * rows : (kh + 1) * rows]
        mass_ref[0, kh] = mass[kh * rows : (kh + 1) * rows]
        acc_ref[0, kh] = acc_all[kh * rows : (kh + 1) * rows, kh * head_dim : (kh + 1) * head_dim]
    first = length - base
    page0 = first // page_len
    row_ids = lax.broadcasted_iota(jnp.int32, (page_len, 1), 0)
    fresh = (fk_ref[0], fv_ref[0])
    for page in (page0, page0 + 1):
        @pl.when(jnp.logical_and(page >= 0, page < pages))
        def _():
            for half in range(2):
                block = outs[half][0, page]
                for t in range(new_count):
                    hit = row_ids == first + t - page * page_len
                    block = jnp.where(hit, fresh[half][t : t + 1, :], block)
                outs[half][0, page] = block


def arrive_and_attend(arrival_src, lengths, base, incoming, queries, fresh_k, fresh_v, scale):
    local_reqs, new_count, kv_width = fresh_k.shape
    _, heads, rows, head_dim = queries.shape
    eye = jnp.arange(heads)[:, None] == jnp.arange(heads)[None, :]
    block_q = jnp.where(eye[None, :, None, :, None], queries[:, :, :, None, :], jnp.zeros((), queries.dtype))
    block_q = block_q.reshape(local_reqs, heads * rows, heads * head_dim)
    page_len = incoming.shape[2]
    pages = arrival_src.shape[0] // local_reqs
    positions = pages * page_len
    arrived = incoming[arrival_src].reshape(local_reqs, pages, 2, page_len, kv_width)
    grid_spec = pltpu.PrefetchScalarGridSpec(
        num_scalar_prefetch=2,
        grid=(local_reqs,),
        in_specs=[
            pl.BlockSpec((1, pages, 2, page_len, kv_width), lambda r, *_: (r, 0, 0, 0, 0)),
            pl.BlockSpec((1, heads * rows, heads * head_dim), lambda r, *_: (r, 0, 0)),
            pl.BlockSpec((1, new_count, kv_width), lambda r, *_: (r, 0, 0)),
            pl.BlockSpec((1, new_count, kv_width), lambda r, *_: (r, 0, 0)),
        ],
        out_specs=[
            pl.BlockSpec((1, pages, page_len, kv_width), lambda r, *_: (r, 0, 0, 0)),
            pl.BlockSpec((1, pages, page_len, kv_width), lambda r, *_: (r, 0, 0, 0)),
            pl.BlockSpec((1, heads, rows, head_dim), lambda r, *_: (r, 0, 0, 0)),
            pl.BlockSpec((1, heads, rows, 1), lambda r, *_: (r, 0, 0, 0)),
            pl.BlockSpec((1, heads, rows, 1), lambda r, *_: (r, 0, 0, 0)),
        ],
    )
    cache_bytes = 2 * local_reqs * positions * kv_width * 2
    keys_out, values_out, acc, peak, mass = pl.pallas_call(
        functools.partial(_arrive_kernel, scale=scale),
        out_shape=[
            jax.ShapeDtypeStruct((local_reqs, pages, page_len, kv_width), jnp.bfloat16),
            jax.ShapeDtypeStruct((local_reqs, pages, page_len, kv_width), jnp.bfloat16),
            jax.ShapeDtypeStruct((local_reqs, heads, rows, head_dim), jnp.float32),
            jax.ShapeDtypeStruct((local_reqs, heads, rows, 1), jnp.float32),
            jax.ShapeDtypeStruct((local_reqs, heads, rows, 1), jnp.float32),
        ],
        grid_spec=grid_spec,
        compiler_params=pltpu.CompilerParams(
            dimension_semantics=("arbitrary",), vmem_limit_bytes=48 * 1024 * 1024
        ),
        cost_estimate=pl.CostEstimate(
            flops=4 * local_reqs * heads * rows * positions * head_dim,
            transcendentals=local_reqs * heads * rows * positions,
            bytes_accessed=2 * cache_bytes,
        ),
        name="arrive_and_attend",
    )(lengths, base, arrived, block_q, fresh_k, fresh_v)
    keys_out = keys_out.reshape(local_reqs, positions, kv_width)
    values_out = values_out.reshape(local_reqs, positions, kv_width)
    return keys_out, values_out, acc, peak, mass


def shards(
    new_tokens,
    norm_gain,
    w_query,
    w_key,
    w_value,
    w_out,
    pool_keys,
    pool_values,
    cache_lengths,
    owner,
    page_table,
):
    req_count = lax.axis_size("req")
    seq_count = lax.axis_size("seq")
    devices = req_count * seq_count
    req_index = lax.axis_index("req")
    seq_index = lax.axis_index("seq")
    device_index = req_index * seq_count + seq_index
    local_reqs, new_count, model_width = new_tokens.shape
    request_total = owner.shape[0]
    pages_dev, page_len, kv_width = pool_keys.shape
    pages_req = page_table.shape[1]
    pages_home = pages_req // seq_count
    positions = pages_home * page_len
    per_peer = pages_dev // devices
    groups = H // KVH
    query_cols = w_query.shape[1]
    key_cols = w_key.shape[1]
    all_requests = jnp.arange(request_total, dtype=jnp.int32)
    hits = owner[None, :] == all_requests[:, None]
    slot_request = jnp.sum(jnp.where(hits, all_requests[None, :], 0), axis=1)
    slot_lengths = jnp.sum(jnp.where(hits, cache_lengths[None, :], 0), axis=1)
    my_lengths = lax.dynamic_slice_in_dim(slot_lengths, req_index * local_reqs, local_reqs)
    slot_pages = page_table[slot_request]
    home_table = jnp.transpose(
        slot_pages.reshape(req_count, local_reqs, seq_count, pages_home), (0, 2, 1, 3)
    ).reshape(devices, local_reqs * pages_home)
    my_home = lax.dynamic_slice_in_dim(home_table, device_index, 1, axis=0).reshape(-1)
    arrival_src = my_home // pages_dev
    held_here = (home_table // pages_dev) == device_index
    send_pick = jnp.sum(jnp.where(held_here, home_table % pages_dev, 0), axis=1)
    tokens_wide = new_tokens.astype(jnp.float32)
    square_mean = jnp.mean(tokens_wide * tokens_wide, axis=-1, keepdims=True)
    normed = (tokens_wide * lax.rsqrt(square_mean + NORM_EPS) * norm_gain).astype(jnp.bfloat16)
    new_index = jnp.arange(new_count, dtype=jnp.int32)
    def shift(value, places):
        if places % req_count == 0:
            return value
        pairs = [(i, (i + places) % req_count) for i in range(req_count)]
        return lax.ppermute(value, "req", pairs)

    row_block = jnp.concatenate([shift(normed, k) for k in range(req_count)], axis=0)
    outgoing = jnp.stack([pool_keys[send_pick], pool_values[send_pick]], axis=1)
    outgoing = outgoing.reshape(devices, per_peer, 2, page_len, kv_width)
    outgoing, row_block = lax.optimization_barrier((outgoing, row_block))
    incoming = lax.all_to_all(outgoing, ("req", "seq"), split_axis=0, concat_axis=0, tiled=True)
    row_count = row_block.shape[0]
    flat_rows = row_block.reshape(row_count * new_count, model_width)
    row_group = (req_index - jnp.arange(req_count, dtype=jnp.int32)) % req_count
    row_lengths = jnp.take(slot_lengths.reshape(req_count, local_reqs), row_group, axis=0).reshape(-1)
    places = row_lengths[:, None] + new_index[None, :]
    queries_now = jnp.dot(flat_rows, w_query, preferred_element_type=jnp.float32).reshape(
        row_count, new_count, query_cols // HD, HD
    )
    keys_now = jnp.dot(flat_rows, w_key, preferred_element_type=jnp.float32).reshape(
        row_count, new_count, key_cols // HD, HD
    )
    values_now = jnp.dot(flat_rows, w_value, preferred_element_type=jnp.float32).reshape(
        row_count, new_count, key_cols
    )
    queries_now = rotate(queries_now, places).reshape(row_count, new_count, query_cols)
    keys_now = rotate(keys_now, places).reshape(row_count, new_count, key_cols)
    projected = jnp.concatenate([queries_now, keys_now, values_now], axis=-1).astype(jnp.bfloat16)
    projected = projected.reshape(req_count, local_reqs, new_count, query_cols + 2 * key_cols)
    by_shift = jnp.stack([shift(projected[k], -k) for k in range(req_count)], axis=0)
    source_block = (jnp.arange(req_count, dtype=jnp.int32) - req_index) % req_count
    owned_rows = jnp.take(by_shift, source_block, axis=0)
    owned_rows = jnp.transpose(owned_rows, (1, 2, 0, 3))
    queries = owned_rows[..., :query_cols].reshape(local_reqs, new_count, KVH, groups, HD)
    fresh_keys = owned_rows[..., query_cols : query_cols + key_cols].reshape(
        local_reqs, new_count, KVH, HD
    )
    fresh_values = owned_rows[..., query_cols + key_cols :].reshape(local_reqs, new_count, KVH, HD)
    score_scale = 1.0 / math.sqrt(HD)
    kernel_queries = jnp.transpose(queries, (0, 2, 3, 1, 4)).reshape(
        local_reqs, KVH, groups * new_count, HD
    )
    keys_out, values_out, gathered_sum, row_peak, row_mass = arrive_and_attend(
        arrival_src,
        my_lengths,
        (seq_index * positions).reshape(1).astype(jnp.int32),
        incoming.reshape(pages_dev, 2, page_len, kv_width),
        kernel_queries,
        fresh_keys.reshape(local_reqs, new_count, kv_width),
        fresh_values.reshape(local_reqs, new_count, kv_width),
        score_scale,
    )
    gathered_sum = gathered_sum.reshape(local_reqs, KVH, groups, new_count, HD)
    row_peak = row_peak.reshape(local_reqs, KVH, groups, new_count)
    row_mass = row_mass.reshape(local_reqs, KVH, groups, new_count)
    def pack(total, peak, mass):
        stat_rows = peak.size // HD
        return jnp.concatenate(
            [total.reshape(-1, HD), peak.reshape(stat_rows, HD), mass.reshape(stat_rows, HD)], axis=0
        )

    def unpack(packed, total, peak, mass):
        stat_rows = peak.size // HD
        return (
            packed[: total.size // HD].reshape(total.shape),
            packed[total.size // HD : -stat_rows].reshape(peak.shape),
            packed[-stat_rows:].reshape(mass.shape),
        )

    def merge(step, total, peak, mass):
        pairs = [(i, i ^ step) for i in range(seq_count)]
        other = lax.ppermute(pack(total, peak, mass), "seq", pairs)
        peer_sum, peer_peak, peer_mass = unpack(other, total, peak, mass)
        upper = (seq_index & step) != 0
        peak_lo = jnp.where(upper, peer_peak, peak)
        peak_hi = jnp.where(upper, peak, peer_peak)
        mass_lo = jnp.where(upper, peer_mass, mass)
        mass_hi = jnp.where(upper, mass, peer_mass)
        sum_lo = jnp.where(upper, peer_sum, total)
        sum_hi = jnp.where(upper, total, peer_sum)
        merged_peak = jnp.maximum(peak_lo, peak_hi)
        scale_lo = jnp.exp(peak_lo - merged_peak)
        scale_hi = jnp.exp(peak_hi - merged_peak)
        return (
            sum_lo * scale_lo[..., None] + sum_hi * scale_hi[..., None],
            merged_peak,
            mass_lo * scale_lo + mass_hi * scale_hi,
        )

    gathered_sum, row_peak, row_mass = merge(1, gathered_sum, row_peak, row_mass)
    half = local_reqs // 2
    core = seq_index % 2
    mine = tuple(
        lax.dynamic_slice_in_dim(x, core * half, half, axis=0)
        for x in (gathered_sum, row_peak, row_mass)
    )
    step = 2
    while step < seq_count:
        mine = merge(step, *mine)
        step *= 2
    mine_packed = pack(*mine)
    other_packed = lax.ppermute(mine_packed, "seq", [(i, i ^ 1) for i in range(seq_count)])
    first_half = unpack(jnp.where(core == 0, mine_packed, other_packed), *mine)
    second_half = unpack(jnp.where(core == 0, other_packed, mine_packed), *mine)
    gathered_sum, row_peak, row_mass = (
        jnp.concatenate([p, q], axis=0) for p, q in zip(first_half, second_half)
    )
    own_scores = (
        jnp.einsum("rtkgd,rskd->rkgts", queries, fresh_keys, preferred_element_type=jnp.float32)
        * score_scale
    )
    causal = new_index[None, :] <= new_index[:, None]
    own_scores = jnp.where(causal, own_scores, MASKED)
    final_peak = jnp.maximum(row_peak, jnp.max(own_scores, axis=-1))
    carried = jnp.exp(row_peak - final_peak)
    own_weights = jnp.where(causal, jnp.exp(own_scores - final_peak[..., None]), 0.0)
    row_mass = row_mass * carried + jnp.sum(own_weights, axis=-1)
    gathered_sum = gathered_sum * carried[..., None] + jnp.einsum(
        "rkgts,rskd->rkgtd",
        own_weights.astype(jnp.bfloat16),
        fresh_values,
        preferred_element_type=jnp.float32,
    )
    attended = (
        jnp.transpose(gathered_sum / row_mass[..., None], (0, 3, 1, 2, 4))
        .reshape(local_reqs, new_count, KVH * groups * HD)
        .astype(jnp.bfloat16)
    )
    head_cols = attended.shape[-1] // req_count
    headed = jnp.concatenate(
        [
            shift(
                lax.dynamic_slice_in_dim(
                    attended, ((req_index + k) % req_count) * head_cols, head_cols, axis=2
                ),
                k,
            )
            for k in range(req_count)
        ],
        axis=0,
    )
    partial_out = (
        jnp.dot(headed.reshape(row_count * new_count, -1), w_out, preferred_element_type=jnp.float32)
        .reshape(req_count, local_reqs, new_count, model_width)
        .astype(jnp.bfloat16)
    )
    projected_out = shift(partial_out[0], 0).astype(jnp.float32)
    for k in range(1, req_count):
        projected_out = projected_out + shift(partial_out[k], -k).astype(jnp.float32)
    out_hidden = (tokens_wide + projected_out).astype(jnp.bfloat16)
    return (out_hidden, keys_out, values_out)


def solution(mesh):
    return jax.shard_map(
        shards,
        mesh=mesh,
        in_specs=(
            P("req", None, None),
            P(),
            P(None, "req"),
            P(None, "req"),
            P(None, "req"),
            P("req", None),
            P(("req", "seq"), None, None),
            P(("req", "seq"), None, None),
            P(),
            P(),
            P(),
        ),
        out_specs=(P("req", None, None), P("req", "seq", None), P("req", "seq", None)),
        check_vma=False,
    )
```

```python
import functools
import math

import jax
import jax.numpy as jnp
from jax import lax
from jax.experimental import pallas as pl
from jax.experimental.pallas import tpu as pltpu
from jax.sharding import PartitionSpec as P

H = 16
KVH = 8
HD = 128


NORM_EPS = 1e-05
ROPE_BASE = 1000000.0
MASKED = -1e30


def rotate(values, places):
    half_dim = values.shape[-1] // 2
    steps_up = jnp.arange(half_dim, dtype=jnp.float32) * (2.0 / values.shape[-1])
    inverse = ROPE_BASE ** (-steps_up)
    angles = places.astype(jnp.float32)[..., None] * inverse
    cosine = jnp.cos(angles)[..., None, :]
    sine_part = jnp.sin(angles)[..., None, :]
    first_half = values[..., :half_dim]
    second_half = values[..., half_dim:]
    return jnp.concatenate(
        [
            first_half * cosine - second_half * sine_part,
            second_half * cosine + first_half * sine_part,
        ],
        axis=-1,
    )


def _arrive_kernel(
    lengths_ref, base_ref, arrived_ref, q_ref, fk_ref, fv_ref,
    keys_out_ref, values_out_ref, acc_ref, peak_ref, mass_ref, *, scale
):
    r = pl.program_id(0)
    pages = arrived_ref.shape[1]
    page_len = arrived_ref.shape[3]
    positions = pages * page_len
    heads = acc_ref.shape[1]
    head_dim = acc_ref.shape[3]
    new_count = fk_ref.shape[1]
    outs = (keys_out_ref, values_out_ref)
    per_step = arrived_ref.shape[0]
    for j in range(per_step):
        keys_out_ref[j] = arrived_ref[j, :, 0]
        values_out_ref[j] = arrived_ref[j, :, 1]
        length = lengths_ref[r * per_step + j]
        base = base_ref[0]
        spots = base + lax.broadcasted_iota(jnp.int32, (1, positions), 1)
        live = spots < length
        rows = q_ref.shape[1] // heads
        keys_all = arrived_ref[j, :, 0].reshape(positions, heads * head_dim)
        values_all = arrived_ref[j, :, 1].reshape(positions, heads * head_dim)
        scores = lax.dot_general(
            q_ref[j], keys_all, (((1,), (1,)), ((), ())), preferred_element_type=jnp.float32
        ) * scale
        scores = jnp.where(live, scores, MASKED)
        peak = jnp.max(scores, axis=1, keepdims=True)
        weights = jnp.where(live, jnp.exp(scores - peak), 0.0)
        mass = jnp.sum(weights, axis=1, keepdims=True)
        acc_all = jnp.dot(weights.astype(jnp.bfloat16), values_all, preferred_element_type=jnp.float32)
        for kh in range(heads):
            peak_ref[j, kh] = peak[kh * rows : (kh + 1) * rows]
            mass_ref[j, kh] = mass[kh * rows : (kh + 1) * rows]
            acc_ref[j, kh] = acc_all[kh * rows : (kh + 1) * rows, kh * head_dim : (kh + 1) * head_dim]
        first = length - base
        page0 = first // page_len
        row_ids = lax.broadcasted_iota(jnp.int32, (page_len, 1), 0)
        fresh = (fk_ref[j], fv_ref[j])
        for page in (page0, page0 + 1):
            @pl.when(jnp.logical_and(page >= 0, page < pages))
            def _():
                for half in range(2):
                    block = outs[half][j, page]
                    for t in range(new_count):
                        hit = row_ids == first + t - page * page_len
                        block = jnp.where(hit, fresh[half][t : t + 1, :], block)
                    outs[half][j, page] = block


def arrive_and_attend(arrival_src, lengths, base, incoming, queries, fresh_k, fresh_v, scale):
    local_reqs, new_count, kv_width = fresh_k.shape
    _, heads, rows, head_dim = queries.shape
    eye = jnp.arange(heads)[:, None] == jnp.arange(heads)[None, :]
    block_q = jnp.where(eye[None, :, None, :, None], queries[:, :, :, None, :], jnp.zeros((), queries.dtype))
    block_q = block_q.reshape(local_reqs, heads * rows, heads * head_dim)
    page_len = incoming.shape[2]
    pages = arrival_src.shape[0] // local_reqs
    positions = pages * page_len
    arrived = incoming[arrival_src].reshape(local_reqs, pages, 2, page_len, kv_width)
    grid_spec = pltpu.PrefetchScalarGridSpec(
        num_scalar_prefetch=2,
        grid=(local_reqs // 2,),
        in_specs=[
            pl.BlockSpec((2, pages, 2, page_len, kv_width), lambda r, *_: (r, 0, 0, 0, 0)),
            pl.BlockSpec((2, heads * rows, heads * head_dim), lambda r, *_: (r, 0, 0)),
            pl.BlockSpec((2, new_count, kv_width), lambda r, *_: (r, 0, 0)),
            pl.BlockSpec((2, new_count, kv_width), lambda r, *_: (r, 0, 0)),
        ],
        out_specs=[
            pl.BlockSpec((2, pages, page_len, kv_width), lambda r, *_: (r, 0, 0, 0)),
            pl.BlockSpec((2, pages, page_len, kv_width), lambda r, *_: (r, 0, 0, 0)),
            pl.BlockSpec((2, heads, rows, head_dim), lambda r, *_: (r, 0, 0, 0)),
            pl.BlockSpec((2, heads, rows, 1), lambda r, *_: (r, 0, 0, 0)),
            pl.BlockSpec((2, heads, rows, 1), lambda r, *_: (r, 0, 0, 0)),
        ],
    )
    cache_bytes = 2 * local_reqs * positions * kv_width * 2
    keys_out, values_out, acc, peak, mass = pl.pallas_call(
        functools.partial(_arrive_kernel, scale=scale),
        out_shape=[
            jax.ShapeDtypeStruct((local_reqs, pages, page_len, kv_width), jnp.bfloat16),
            jax.ShapeDtypeStruct((local_reqs, pages, page_len, kv_width), jnp.bfloat16),
            jax.ShapeDtypeStruct((local_reqs, heads, rows, head_dim), jnp.float32),
            jax.ShapeDtypeStruct((local_reqs, heads, rows, 1), jnp.float32),
            jax.ShapeDtypeStruct((local_reqs, heads, rows, 1), jnp.float32),
        ],
        grid_spec=grid_spec,
        compiler_params=pltpu.CompilerParams(
            dimension_semantics=("arbitrary",), vmem_limit_bytes=48 * 1024 * 1024
        ),
        cost_estimate=pl.CostEstimate(
            flops=4 * local_reqs * heads * rows * positions * head_dim,
            transcendentals=local_reqs * heads * rows * positions,
            bytes_accessed=2 * cache_bytes,
        ),
        name="arrive_and_attend",
    )(lengths, base, arrived, block_q, fresh_k, fresh_v)
    keys_out = keys_out.reshape(local_reqs, positions, kv_width)
    values_out = values_out.reshape(local_reqs, positions, kv_width)
    return keys_out, values_out, acc, peak, mass


def shards(
    new_tokens,
    norm_gain,
    w_query,
    w_key,
    w_value,
    w_out,
    pool_keys,
    pool_values,
    cache_lengths,
    owner,
    page_table,
):
    req_count = lax.axis_size("req")
    seq_count = lax.axis_size("seq")
    devices = req_count * seq_count
    req_index = lax.axis_index("req")
    seq_index = lax.axis_index("seq")
    device_index = req_index * seq_count + seq_index
    local_reqs, new_count, model_width = new_tokens.shape
    request_total = owner.shape[0]
    pages_dev, page_len, kv_width = pool_keys.shape
    pages_req = page_table.shape[1]
    pages_home = pages_req // seq_count
    positions = pages_home * page_len
    per_peer = pages_dev // devices
    groups = H // KVH
    query_cols = w_query.shape[1]
    key_cols = w_key.shape[1]
    all_requests = jnp.arange(request_total, dtype=jnp.int32)
    hits = owner[None, :] == all_requests[:, None]
    slot_request = jnp.sum(jnp.where(hits, all_requests[None, :], 0), axis=1)
    slot_lengths = jnp.sum(jnp.where(hits, cache_lengths[None, :], 0), axis=1)
    my_lengths = lax.dynamic_slice_in_dim(slot_lengths, req_index * local_reqs, local_reqs)
    slot_pages = page_table[slot_request]
    home_table = jnp.transpose(
        slot_pages.reshape(req_count, local_reqs, seq_count, pages_home), (0, 2, 1, 3)
    ).reshape(devices, local_reqs * pages_home)
    my_home = lax.dynamic_slice_in_dim(home_table, device_index, 1, axis=0).reshape(-1)
    arrival_src = my_home // pages_dev
    held_here = (home_table // pages_dev) == device_index
    send_pick = jnp.sum(jnp.where(held_here, home_table % pages_dev, 0), axis=1)
    tokens_wide = new_tokens.astype(jnp.float32)
    square_mean = jnp.mean(tokens_wide * tokens_wide, axis=-1, keepdims=True)
    normed = (tokens_wide * lax.rsqrt(square_mean + NORM_EPS) * norm_gain).astype(jnp.bfloat16)
    new_index = jnp.arange(new_count, dtype=jnp.int32)
    def shift(value, places):
        if places % req_count == 0:
            return value
        pairs = [(i, (i + places) % req_count) for i in range(req_count)]
        return lax.ppermute(value, "req", pairs)

    row_block = jnp.concatenate([shift(normed, k) for k in range(req_count)], axis=0)
    outgoing = jnp.stack([pool_keys[send_pick], pool_values[send_pick]], axis=1)
    outgoing = outgoing.reshape(devices, per_peer, 2, page_len, kv_width)
    outgoing, row_block = lax.optimization_barrier((outgoing, row_block))
    incoming = lax.all_to_all(outgoing, ("req", "seq"), split_axis=0, concat_axis=0, tiled=True)
    row_count = row_block.shape[0]
    flat_rows = row_block.reshape(row_count * new_count, model_width)
    row_group = (req_index - jnp.arange(req_count, dtype=jnp.int32)) % req_count
    row_lengths = jnp.take(slot_lengths.reshape(req_count, local_reqs), row_group, axis=0).reshape(-1)
    places = row_lengths[:, None] + new_index[None, :]
    queries_now = jnp.dot(flat_rows, w_query, preferred_element_type=jnp.float32).reshape(
        row_count, new_count, query_cols // HD, HD
    )
    keys_now = jnp.dot(flat_rows, w_key, preferred_element_type=jnp.float32).reshape(
        row_count, new_count, key_cols // HD, HD
    )
    values_now = jnp.dot(flat_rows, w_value, preferred_element_type=jnp.float32).reshape(
        row_count, new_count, key_cols
    )
    queries_now = rotate(queries_now, places).reshape(row_count, new_count, query_cols)
    keys_now = rotate(keys_now, places).reshape(row_count, new_count, key_cols)
    projected = jnp.concatenate([queries_now, keys_now, values_now], axis=-1).astype(jnp.bfloat16)
    projected = projected.reshape(req_count, local_reqs, new_count, query_cols + 2 * key_cols)
    by_shift = jnp.stack([shift(projected[k], -k) for k in range(req_count)], axis=0)
    source_block = (jnp.arange(req_count, dtype=jnp.int32) - req_index) % req_count
    owned_rows = jnp.take(by_shift, source_block, axis=0)
    owned_rows = jnp.transpose(owned_rows, (1, 2, 0, 3))
    queries = owned_rows[..., :query_cols].reshape(local_reqs, new_count, KVH, groups, HD)
    fresh_keys = owned_rows[..., query_cols : query_cols + key_cols].reshape(
        local_reqs, new_count, KVH, HD
    )
    fresh_values = owned_rows[..., query_cols + key_cols :].reshape(local_reqs, new_count, KVH, HD)
    score_scale = 1.0 / math.sqrt(HD)
    kernel_queries = jnp.transpose(queries, (0, 2, 3, 1, 4)).reshape(
        local_reqs, KVH, groups * new_count, HD
    )
    keys_out, values_out, gathered_sum, row_peak, row_mass = arrive_and_attend(
        arrival_src,
        my_lengths,
        (seq_index * positions).reshape(1).astype(jnp.int32),
        incoming.reshape(pages_dev, 2, page_len, kv_width),
        kernel_queries,
        fresh_keys.reshape(local_reqs, new_count, kv_width),
        fresh_values.reshape(local_reqs, new_count, kv_width),
        score_scale,
    )
    gathered_sum = gathered_sum.reshape(local_reqs, KVH, groups, new_count, HD)
    row_peak = row_peak.reshape(local_reqs, KVH, groups, new_count)
    row_mass = row_mass.reshape(local_reqs, KVH, groups, new_count)
    def pack(total, peak, mass):
        stat_rows = peak.size // HD
        return jnp.concatenate(
            [total.reshape(-1, HD), peak.reshape(stat_rows, HD), mass.reshape(stat_rows, HD)], axis=0
        )

    def unpack(packed, total, peak, mass):
        stat_rows = peak.size // HD
        return (
            packed[: total.size // HD].reshape(total.shape),
            packed[total.size // HD : -stat_rows].reshape(peak.shape),
            packed[-stat_rows:].reshape(mass.shape),
        )

    def merge(step, total, peak, mass):
        pairs = [(i, i ^ step) for i in range(seq_count)]
        other = lax.ppermute(pack(total, peak, mass), "seq", pairs)
        peer_sum, peer_peak, peer_mass = unpack(other, total, peak, mass)
        upper = (seq_index & step) != 0
        peak_lo = jnp.where(upper, peer_peak, peak)
        peak_hi = jnp.where(upper, peak, peer_peak)
        mass_lo = jnp.where(upper, peer_mass, mass)
        mass_hi = jnp.where(upper, mass, peer_mass)
        sum_lo = jnp.where(upper, peer_sum, total)
        sum_hi = jnp.where(upper, total, peer_sum)
        merged_peak = jnp.maximum(peak_lo, peak_hi)
        scale_lo = jnp.exp(peak_lo - merged_peak)
        scale_hi = jnp.exp(peak_hi - merged_peak)
        return (
            sum_lo * scale_lo[..., None] + sum_hi * scale_hi[..., None],
            merged_peak,
            mass_lo * scale_lo + mass_hi * scale_hi,
        )

    gathered_sum, row_peak, row_mass = merge(1, gathered_sum, row_peak, row_mass)
    half = local_reqs // 2
    core = seq_index % 2
    mine = tuple(
        lax.dynamic_slice_in_dim(x, core * half, half, axis=0)
        for x in (gathered_sum, row_peak, row_mass)
    )
    step = 2
    while step < seq_count:
        mine = merge(step, *mine)
        step *= 2
    mine_packed = pack(*mine)
    other_packed = lax.ppermute(mine_packed, "seq", [(i, i ^ 1) for i in range(seq_count)])
    first_half = unpack(jnp.where(core == 0, mine_packed, other_packed), *mine)
    second_half = unpack(jnp.where(core == 0, other_packed, mine_packed), *mine)
    gathered_sum, row_peak, row_mass = (
        jnp.concatenate([p, q], axis=0) for p, q in zip(first_half, second_half)
    )
    own_scores = (
        jnp.einsum("rtkgd,rskd->rkgts", queries, fresh_keys, preferred_element_type=jnp.float32)
        * score_scale
    )
    causal = new_index[None, :] <= new_index[:, None]
    own_scores = jnp.where(causal, own_scores, MASKED)
    final_peak = jnp.maximum(row_peak, jnp.max(own_scores, axis=-1))
    carried = jnp.exp(row_peak - final_peak)
    own_weights = jnp.where(causal, jnp.exp(own_scores - final_peak[..., None]), 0.0)
    row_mass = row_mass * carried + jnp.sum(own_weights, axis=-1)
    gathered_sum = gathered_sum * carried[..., None] + jnp.einsum(
        "rkgts,rskd->rkgtd",
        own_weights.astype(jnp.bfloat16),
        fresh_values,
        preferred_element_type=jnp.float32,
    )
    attended = (
        jnp.transpose(gathered_sum / row_mass[..., None], (0, 3, 1, 2, 4))
        .reshape(local_reqs, new_count, KVH * groups * HD)
        .astype(jnp.bfloat16)
    )
    head_cols = attended.shape[-1] // req_count
    headed = jnp.concatenate(
        [
            shift(
                lax.dynamic_slice_in_dim(
                    attended, ((req_index + k) % req_count) * head_cols, head_cols, axis=2
                ),
                k,
            )
            for k in range(req_count)
        ],
        axis=0,
    )
    partial_out = (
        jnp.dot(headed.reshape(row_count * new_count, -1), w_out, preferred_element_type=jnp.float32)
        .reshape(req_count, local_reqs, new_count, model_width)
        .astype(jnp.bfloat16)
    )
    projected_out = shift(partial_out[0], 0).astype(jnp.float32)
    for k in range(1, req_count):
        projected_out = projected_out + shift(partial_out[k], -k).astype(jnp.float32)
    out_hidden = (tokens_wide + projected_out).astype(jnp.bfloat16)
    return (out_hidden, keys_out, values_out)


def solution(mesh):
    return jax.shard_map(
        shards,
        mesh=mesh,
        in_specs=(
            P("req", None, None),
            P(),
            P(None, "req"),
            P(None, "req"),
            P(None, "req"),
            P("req", None),
            P(("req", "seq"), None, None),
            P(("req", "seq"), None, None),
            P(),
            P(),
            P(),
        ),
        out_specs=(P("req", None, None), P("req", "seq", None), P("req", "seq", None)),
        check_vma=False,
    )
```

```python
import functools
import math

import jax
import jax.numpy as jnp
from jax import lax
from jax.experimental import pallas as pl
from jax.experimental.pallas import tpu as pltpu
from jax.sharding import PartitionSpec as P

H = 16
KVH = 8
HD = 128


NORM_EPS = 1e-05
ROPE_BASE = 1000000.0
MASKED = -1e30


def rotate(values, places):
    half_dim = values.shape[-1] // 2
    steps_up = jnp.arange(half_dim, dtype=jnp.float32) * (2.0 / values.shape[-1])
    inverse = ROPE_BASE ** (-steps_up)
    angles = places.astype(jnp.float32)[..., None] * inverse
    cosine = jnp.cos(angles)[..., None, :]
    sine_part = jnp.sin(angles)[..., None, :]
    first_half = values[..., :half_dim]
    second_half = values[..., half_dim:]
    return jnp.concatenate(
        [
            first_half * cosine - second_half * sine_part,
            second_half * cosine + first_half * sine_part,
        ],
        axis=-1,
    )


def _arrive_kernel(
    lengths_ref, base_ref, arrived_ref, q_ref, fk_ref, fv_ref,
    keys_out_ref, values_out_ref, acc_ref, peak_ref, mass_ref, block_q, *, scale
):
    r = pl.program_id(0)
    pages = arrived_ref.shape[1]
    page_len = arrived_ref.shape[3]
    positions = pages * page_len
    heads = acc_ref.shape[1]
    head_dim = acc_ref.shape[3]
    new_count = fk_ref.shape[1]
    outs = (keys_out_ref, values_out_ref)
    per_step = arrived_ref.shape[0]
    rows = q_ref.shape[2]

    @pl.when(r == 0)
    def _():
        block_q[...] = jnp.zeros_like(block_q)

    for j in range(per_step):
        for kh in range(heads):
            block_q[kh * rows : (kh + 1) * rows, kh * head_dim : (kh + 1) * head_dim] = q_ref[j, kh]
        keys_out_ref[j] = arrived_ref[j, :, 0]
        values_out_ref[j] = arrived_ref[j, :, 1]
        length = lengths_ref[r * per_step + j]
        base = base_ref[0]
        spots = base + lax.broadcasted_iota(jnp.int32, (1, positions), 1)
        live = spots < length
        keys_all = arrived_ref[j, :, 0].reshape(positions, heads * head_dim)
        values_all = arrived_ref[j, :, 1].reshape(positions, heads * head_dim)
        scores = lax.dot_general(
            block_q[...], keys_all, (((1,), (1,)), ((), ())), preferred_element_type=jnp.float32
        ) * scale
        scores = jnp.where(live, scores, MASKED)
        peak = jnp.max(scores, axis=1, keepdims=True)
        weights = jnp.where(live, jnp.exp(scores - peak), 0.0)
        mass = jnp.sum(weights, axis=1, keepdims=True)
        acc_all = jnp.dot(weights.astype(jnp.bfloat16), values_all, preferred_element_type=jnp.float32)
        for kh in range(heads):
            peak_ref[j, kh] = peak[kh * rows : (kh + 1) * rows]
            mass_ref[j, kh] = mass[kh * rows : (kh + 1) * rows]
            acc_ref[j, kh] = acc_all[kh * rows : (kh + 1) * rows, kh * head_dim : (kh + 1) * head_dim]
        first = length - base
        page0 = first // page_len
        row_ids = lax.broadcasted_iota(jnp.int32, (page_len, 1), 0)
        fresh = (fk_ref[j], fv_ref[j])
        for page in (page0, page0 + 1):
            @pl.when(jnp.logical_and(page >= 0, page < pages))
            def _():
                for half in range(2):
                    block = outs[half][j, page]
                    for t in range(new_count):
                        hit = row_ids == first + t - page * page_len
                        block = jnp.where(hit, fresh[half][t : t + 1, :], block)
                    outs[half][j, page] = block


def arrive_and_attend(arrival_src, lengths, base, incoming, queries, fresh_k, fresh_v, scale):
    local_reqs, new_count, kv_width = fresh_k.shape
    _, heads, rows, head_dim = queries.shape
    page_len = incoming.shape[2]
    pages = arrival_src.shape[0] // local_reqs
    positions = pages * page_len
    arrived = incoming[arrival_src].reshape(local_reqs, pages, 2, page_len, kv_width)
    grid_spec = pltpu.PrefetchScalarGridSpec(
        num_scalar_prefetch=2,
        grid=(local_reqs // 2,),
        in_specs=[
            pl.BlockSpec((2, pages, 2, page_len, kv_width), lambda r, *_: (r, 0, 0, 0, 0)),
            pl.BlockSpec((2, heads, rows, head_dim), lambda r, *_: (r, 0, 0, 0)),
            pl.BlockSpec((2, new_count, kv_width), lambda r, *_: (r, 0, 0)),
            pl.BlockSpec((2, new_count, kv_width), lambda r, *_: (r, 0, 0)),
        ],
        out_specs=[
            pl.BlockSpec((2, pages, page_len, kv_width), lambda r, *_: (r, 0, 0, 0)),
            pl.BlockSpec((2, pages, page_len, kv_width), lambda r, *_: (r, 0, 0, 0)),
            pl.BlockSpec((2, heads, rows, head_dim), lambda r, *_: (r, 0, 0, 0)),
            pl.BlockSpec((2, heads, rows, 1), lambda r, *_: (r, 0, 0, 0)),
            pl.BlockSpec((2, heads, rows, 1), lambda r, *_: (r, 0, 0, 0)),
        ],
        scratch_shapes=[pltpu.VMEM((heads * rows, heads * head_dim), jnp.bfloat16)],
    )
    cache_bytes = 2 * local_reqs * positions * kv_width * 2
    keys_out, values_out, acc, peak, mass = pl.pallas_call(
        functools.partial(_arrive_kernel, scale=scale),
        out_shape=[
            jax.ShapeDtypeStruct((local_reqs, pages, page_len, kv_width), jnp.bfloat16),
            jax.ShapeDtypeStruct((local_reqs, pages, page_len, kv_width), jnp.bfloat16),
            jax.ShapeDtypeStruct((local_reqs, heads, rows, head_dim), jnp.float32),
            jax.ShapeDtypeStruct((local_reqs, heads, rows, 1), jnp.float32),
            jax.ShapeDtypeStruct((local_reqs, heads, rows, 1), jnp.float32),
        ],
        grid_spec=grid_spec,
        compiler_params=pltpu.CompilerParams(
            dimension_semantics=("arbitrary",), vmem_limit_bytes=48 * 1024 * 1024
        ),
        cost_estimate=pl.CostEstimate(
            flops=4 * local_reqs * heads * rows * positions * head_dim,
            transcendentals=local_reqs * heads * rows * positions,
            bytes_accessed=2 * cache_bytes,
        ),
        name="arrive_and_attend",
    )(lengths, base, arrived, queries, fresh_k, fresh_v)
    keys_out = keys_out.reshape(local_reqs, positions, kv_width)
    values_out = values_out.reshape(local_reqs, positions, kv_width)
    return keys_out, values_out, acc, peak, mass


def shards(
    new_tokens,
    norm_gain,
    w_query,
    w_key,
    w_value,
    w_out,
    pool_keys,
    pool_values,
    cache_lengths,
    owner,
    page_table,
):
    req_count = lax.axis_size("req")
    seq_count = lax.axis_size("seq")
    devices = req_count * seq_count
    req_index = lax.axis_index("req")
    seq_index = lax.axis_index("seq")
    device_index = req_index * seq_count + seq_index
    local_reqs, new_count, model_width = new_tokens.shape
    request_total = owner.shape[0]
    pages_dev, page_len, kv_width = pool_keys.shape
    pages_req = page_table.shape[1]
    pages_home = pages_req // seq_count
    positions = pages_home * page_len
    per_peer = pages_dev // devices
    groups = H // KVH
    query_cols = w_query.shape[1]
    key_cols = w_key.shape[1]
    all_requests = jnp.arange(request_total, dtype=jnp.int32)
    hits = owner[None, :] == all_requests[:, None]
    slot_request = jnp.sum(jnp.where(hits, all_requests[None, :], 0), axis=1)
    slot_lengths = jnp.sum(jnp.where(hits, cache_lengths[None, :], 0), axis=1)
    my_lengths = lax.dynamic_slice_in_dim(slot_lengths, req_index * local_reqs, local_reqs)
    slot_pages = page_table[slot_request]
    home_table = jnp.transpose(
        slot_pages.reshape(req_count, local_reqs, seq_count, pages_home), (0, 2, 1, 3)
    ).reshape(devices, local_reqs * pages_home)
    my_home = lax.dynamic_slice_in_dim(home_table, device_index, 1, axis=0).reshape(-1)
    arrival_src = my_home // pages_dev
    held_here = (home_table // pages_dev) == device_index
    send_pick = jnp.sum(jnp.where(held_here, home_table % pages_dev, 0), axis=1)
    tokens_wide = new_tokens.astype(jnp.float32)
    square_mean = jnp.mean(tokens_wide * tokens_wide, axis=-1, keepdims=True)
    normed = (tokens_wide * lax.rsqrt(square_mean + NORM_EPS) * norm_gain).astype(jnp.bfloat16)
    new_index = jnp.arange(new_count, dtype=jnp.int32)
    def shift(value, places):
        if places % req_count == 0:
            return value
        pairs = [(i, (i + places) % req_count) for i in range(req_count)]
        return lax.ppermute(value, "req", pairs)

    row_block = jnp.concatenate([shift(normed, k) for k in range(req_count)], axis=0)
    outgoing = jnp.stack([pool_keys[send_pick], pool_values[send_pick]], axis=1)
    outgoing = outgoing.reshape(devices, per_peer, 2, page_len, kv_width)
    outgoing, row_block = lax.optimization_barrier((outgoing, row_block))
    incoming = lax.all_to_all(outgoing, ("req", "seq"), split_axis=0, concat_axis=0, tiled=True)
    row_count = row_block.shape[0]
    flat_rows = row_block.reshape(row_count * new_count, model_width)
    row_group = (req_index - jnp.arange(req_count, dtype=jnp.int32)) % req_count
    row_lengths = jnp.take(slot_lengths.reshape(req_count, local_reqs), row_group, axis=0).reshape(-1)
    places = row_lengths[:, None] + new_index[None, :]
    queries_now = jnp.dot(flat_rows, w_query, preferred_element_type=jnp.float32).reshape(
        row_count, new_count, query_cols // HD, HD
    )
    keys_now = jnp.dot(flat_rows, w_key, preferred_element_type=jnp.float32).reshape(
        row_count, new_count, key_cols // HD, HD
    )
    values_now = jnp.dot(flat_rows, w_value, preferred_element_type=jnp.float32).reshape(
        row_count, new_count, key_cols
    )
    queries_now = rotate(queries_now, places).reshape(row_count, new_count, query_cols)
    keys_now = rotate(keys_now, places).reshape(row_count, new_count, key_cols)
    projected = jnp.concatenate([queries_now, keys_now, values_now], axis=-1).astype(jnp.bfloat16)
    projected = projected.reshape(req_count, local_reqs, new_count, query_cols + 2 * key_cols)
    by_shift = jnp.stack([shift(projected[k], -k) for k in range(req_count)], axis=0)
    source_block = (jnp.arange(req_count, dtype=jnp.int32) - req_index) % req_count
    owned_rows = jnp.take(by_shift, source_block, axis=0)
    owned_rows = jnp.transpose(owned_rows, (1, 2, 0, 3))
    queries = owned_rows[..., :query_cols].reshape(local_reqs, new_count, KVH, groups, HD)
    fresh_keys = owned_rows[..., query_cols : query_cols + key_cols].reshape(
        local_reqs, new_count, KVH, HD
    )
    fresh_values = owned_rows[..., query_cols + key_cols :].reshape(local_reqs, new_count, KVH, HD)
    score_scale = 1.0 / math.sqrt(HD)
    kernel_queries = jnp.transpose(queries, (0, 2, 3, 1, 4)).reshape(
        local_reqs, KVH, groups * new_count, HD
    )
    keys_out, values_out, gathered_sum, row_peak, row_mass = arrive_and_attend(
        arrival_src,
        my_lengths,
        (seq_index * positions).reshape(1).astype(jnp.int32),
        incoming.reshape(pages_dev, 2, page_len, kv_width),
        kernel_queries,
        fresh_keys.reshape(local_reqs, new_count, kv_width),
        fresh_values.reshape(local_reqs, new_count, kv_width),
        score_scale,
    )
    gathered_sum = gathered_sum.reshape(local_reqs, KVH, groups, new_count, HD)
    row_peak = row_peak.reshape(local_reqs, KVH, groups, new_count)
    row_mass = row_mass.reshape(local_reqs, KVH, groups, new_count)
    def pack(total, peak, mass):
        stat_rows = peak.size // HD
        return jnp.concatenate(
            [total.reshape(-1, HD), peak.reshape(stat_rows, HD), mass.reshape(stat_rows, HD)], axis=0
        )

    def unpack(packed, total, peak, mass):
        stat_rows = peak.size // HD
        return (
            packed[: total.size // HD].reshape(total.shape),
            packed[total.size // HD : -stat_rows].reshape(peak.shape),
            packed[-stat_rows:].reshape(mass.shape),
        )

    def merge(step, total, peak, mass):
        pairs = [(i, i ^ step) for i in range(seq_count)]
        other = lax.ppermute(pack(total, peak, mass), "seq", pairs)
        peer_sum, peer_peak, peer_mass = unpack(other, total, peak, mass)
        upper = (seq_index & step) != 0
        peak_lo = jnp.where(upper, peer_peak, peak)
        peak_hi = jnp.where(upper, peak, peer_peak)
        mass_lo = jnp.where(upper, peer_mass, mass)
        mass_hi = jnp.where(upper, mass, peer_mass)
        sum_lo = jnp.where(upper, peer_sum, total)
        sum_hi = jnp.where(upper, total, peer_sum)
        merged_peak = jnp.maximum(peak_lo, peak_hi)
        scale_lo = jnp.exp(peak_lo - merged_peak)
        scale_hi = jnp.exp(peak_hi - merged_peak)
        return (
            sum_lo * scale_lo[..., None] + sum_hi * scale_hi[..., None],
            merged_peak,
            mass_lo * scale_lo + mass_hi * scale_hi,
        )

    gathered_sum, row_peak, row_mass = merge(1, gathered_sum, row_peak, row_mass)
    half = local_reqs // 2
    core = seq_index % 2
    mine = tuple(
        lax.dynamic_slice_in_dim(x, core * half, half, axis=0)
        for x in (gathered_sum, row_peak, row_mass)
    )
    step = 2
    while step < seq_count:
        mine = merge(step, *mine)
        step *= 2
    mine_packed = pack(*mine)
    other_packed = lax.ppermute(mine_packed, "seq", [(i, i ^ 1) for i in range(seq_count)])
    first_half = unpack(jnp.where(core == 0, mine_packed, other_packed), *mine)
    second_half = unpack(jnp.where(core == 0, other_packed, mine_packed), *mine)
    gathered_sum, row_peak, row_mass = (
        jnp.concatenate([p, q], axis=0) for p, q in zip(first_half, second_half)
    )
    own_scores = (
        jnp.einsum("rtkgd,rskd->rkgts", queries, fresh_keys, preferred_element_type=jnp.float32)
        * score_scale
    )
    causal = new_index[None, :] <= new_index[:, None]
    own_scores = jnp.where(causal, own_scores, MASKED)
    final_peak = jnp.maximum(row_peak, jnp.max(own_scores, axis=-1))
    carried = jnp.exp(row_peak - final_peak)
    own_weights = jnp.where(causal, jnp.exp(own_scores - final_peak[..., None]), 0.0)
    row_mass = row_mass * carried + jnp.sum(own_weights, axis=-1)
    gathered_sum = gathered_sum * carried[..., None] + jnp.einsum(
        "rkgts,rskd->rkgtd",
        own_weights.astype(jnp.bfloat16),
        fresh_values,
        preferred_element_type=jnp.float32,
    )
    attended = (
        jnp.transpose(gathered_sum / row_mass[..., None], (0, 3, 1, 2, 4))
        .reshape(local_reqs, new_count, KVH * groups * HD)
        .astype(jnp.bfloat16)
    )
    head_cols = attended.shape[-1] // req_count
    headed = jnp.concatenate(
        [
            shift(
                lax.dynamic_slice_in_dim(
                    attended, ((req_index + k) % req_count) * head_cols, head_cols, axis=2
                ),
                k,
            )
            for k in range(req_count)
        ],
        axis=0,
    )
    partial_out = (
        jnp.dot(headed.reshape(row_count * new_count, -1), w_out, preferred_element_type=jnp.float32)
        .reshape(req_count, local_reqs, new_count, model_width)
        .astype(jnp.bfloat16)
    )
    projected_out = shift(partial_out[0], 0).astype(jnp.float32)
    for k in range(1, req_count):
        projected_out = projected_out + shift(partial_out[k], -k).astype(jnp.float32)
    out_hidden = (tokens_wide + projected_out).astype(jnp.bfloat16)
    return (out_hidden, keys_out, values_out)


def solution(mesh):
    return jax.shard_map(
        shards,
        mesh=mesh,
        in_specs=(
            P("req", None, None),
            P(),
            P(None, "req"),
            P(None, "req"),
            P(None, "req"),
            P("req", None),
            P(("req", "seq"), None, None),
            P(("req", "seq"), None, None),
            P(),
            P(),
            P(),
        ),
        out_specs=(P("req", None, None), P("req", "seq", None), P("req", "seq", None)),
        check_vma=False,
    )
```
